128 devices in a mesh: lat: 16 (over y, z), lon: 8 (over x, core).
Axes of the slice: x: 4, y: 4, z: 4, core: 2. Of those that a mesh axis runs over, the one named last changes fastest.
Arguments:
- inputs: bfloat16 [640, 1440, 256], P('lat', 'lon'), may hold values from -6 to 6
- w_enc: bfloat16 [3, 3, 256, 256], replicated, may hold values from -0.125 to 0.125
- w_proj: bfloat16 [256, 128], replicated, may hold values from -0.375 to 0.375
- film_scale: float32 [720, 128], replicated, may hold values from -3 to 3
- film_shift: float32 [720, 128], replicated, may hold values from -3 to 3
- lead_ids: int32 [16], replicated, may hold values from 0 to 719
- w_head: bfloat16 [3, 3, 128, 128], replicated, may hold values from -0.1875 to 0.1875
- zonal_mix: bfloat16 [720, 720], replicated, may hold values from -0.21875 to 0.21875
Outputs:
- forecast: bfloat16 [16, 320, 720, 128], P('lon', 'lat')
The draws below stay inside these ranges and needn't reach their ends.
Inputs may be any that keep to these rules, and one draw needn't show every extreme that they name: `lead_ids`: rows of the tables; repeats may occur.
All inputs are finite; a program needn't handle non-finite values.
Results may differ from the reference program's by a relative error of at most 0.015.
Values may be sent and summed in bfloat16 or wider, within the bound.
A program may use at most 128 MiB of HBM per device.

```python
import jax
import jax.numpy as jnp
from jax import lax

C = 256
H = 128
LEAD_TABLE = 720
LEADS = 16
LAT = 640
LON = 1440
LONP = 720


def with_ends(values, key, least, top_value):
    spot = [jax.random.randint(jax.random.fold_in(key, axis), (), 0, length) for axis, length in enumerate(values.shape)]
    widest = values.shape.index(max(values.shape))
    beside = spot[:widest] + [(spot[widest] + 1) % values.shape[widest]] + spot[widest + 1:]
    return values.at[tuple(spot)].set(least).at[tuple(beside)].set(top_value)


def levels(key, dims, pieces, least, high):
    loudness = 1.0
    for axis_at, parts in pieces:
        steps = jax.random.uniform(jax.random.fold_in(jax.random.fold_in(key, 6), axis_at), (parts,), jnp.float32, least / len(pieces), high / len(pieces))
        loudness = loudness * jnp.repeat(jnp.exp(steps), dims[axis_at] // parts).reshape((-1,) + (1,) * (len(dims) - 1 - axis_at))
    return loudness


def bell_draw(own_key, shape, deviation, bound, split=(), held_as=jnp.bfloat16):
    entries = deviation * jax.random.normal(own_key, shape, jnp.float32)
    if split:
        entries = entries * levels(own_key, shape, split, -0.22, 0.18)
    return jnp.clip(entries, -bound, bound).astype(held_as)


def setup_inputs(seed: int = 0) -> dict:
    streams_of = jax.random.split(jax.random.key(seed), 9)
    inputs = bell_draw(streams_of[0], (LAT, LON, C), 1.0, 6.0, ((0, 16), (1, 8)))
    w_enc = bell_draw(streams_of[1], (3, 3, C, C), (9 * C) ** -0.5, 0.125)
    w_proj = bell_draw(streams_of[2], (C, H), C ** -0.5, 0.375)
    film_scale = bell_draw(streams_of[3], (LEAD_TABLE, H), 0.5, 3.0, (), jnp.float32)
    film_shift = bell_draw(streams_of[4], (LEAD_TABLE, H), 0.5, 3.0, (), jnp.float32)
    lead_ids = with_ends(jax.random.randint(streams_of[5], (LEADS,), 0, LEAD_TABLE), jax.random.fold_in(streams_of[5], 1), 0, LEAD_TABLE - 1).astype(jnp.int32)
    w_head = bell_draw(streams_of[6], (3, 3, H, H), (9 * H) ** -0.5, 0.1875)
    zonal_mix = bell_draw(streams_of[7], (LONP, LONP), LONP ** -0.5, 0.21875)
    return dict(inputs=inputs, w_enc=w_enc, w_proj=w_proj, film_scale=film_scale, film_shift=film_shift, lead_ids=lead_ids, w_head=w_head, zonal_mix=zonal_mix)


def conv_three(padded, weight):
    batched = padded if padded.ndim == 4 else padded[None]
    result = lax.conv_general_dilated(batched, weight, (1, 1), "VALID", dimension_numbers=("NHWC", "HWIO", "NHWC"), preferred_element_type=jnp.float32)
    return result if padded.ndim == 4 else result[0]


def pool_pairs(field):
    summed = lax.reduce_window(field, jnp.array(0, field.dtype), lax.add, (2, 2, 1), (2, 2, 1), "VALID")
    return summed * 0.25


def wrap_columns(field):
    return jnp.concatenate([field[..., -1:, :], field, field[..., :1, :]], axis=-2)


def reference(inputs, w_enc, w_proj, film_scale, film_shift, lead_ids, w_head, zonal_mix):
    lat_rows, lon_cols, channels = inputs.shape
    padded = wrap_columns(jnp.pad(inputs, ((1, 1), (0, 0), (0, 0))))
    encoded = jax.nn.gelu(conv_three(padded, w_enc))
    pooled = pool_pairs(encoded).astype(jnp.bfloat16)
    head_width = w_proj.shape[1]
    projected = jnp.dot(pooled.reshape(-1, channels), w_proj, preferred_element_type=jnp.float32).astype(jnp.bfloat16)
    projected = projected.reshape(lat_rows // 2, lon_cols // 2, head_width)
    scales = film_scale[lead_ids]
    shifts = film_shift[lead_ids]

    def one_head(pair):
        scale_row, shift_row = pair
        modulated = (projected.astype(jnp.float32) * (1.0 + scale_row) + shift_row).astype(jnp.bfloat16)
        padded_head = wrap_columns(jnp.pad(modulated, ((1, 1), (0, 0), (0, 0))))
        hidden = jax.nn.gelu(conv_three(padded_head, w_head)).astype(jnp.bfloat16)
        mixed = jnp.einsum("ij,ajc->aic", zonal_mix.astype(jnp.float32), hidden.astype(jnp.float32))
        return (modulated.astype(jnp.float32) + mixed).astype(jnp.bfloat16)

    return lax.map(one_head, (scales, shifts))
```

```python
import functools

import jax
import jax.numpy as jnp
from jax import lax
from jax.experimental import pallas as pl
from jax.experimental.pallas import tpu as pltpu
from jax.sharding import PartitionSpec as P

LEAD_DEV = 2
HEAD_ROWS = 4


def extended(x, sides, width, wrap):
    for axis, dim in sides:
        devices, length = (lax.axis_size(axis), x.shape[dim])
        up = [(i, (i + 1) % devices) for i in range(devices if wrap else devices - 1)]
        down = [(j, i) for i, j in up]
        last = lax.slice_in_dim(x, length - width, length, axis=dim)
        initial = lax.slice_in_dim(x, 0, width, axis=dim)
        before = lax.ppermute(last, axis, up)
        after = lax.ppermute(initial, axis, down)
        x = jnp.concatenate([before, x, after], axis=dim)
    return x


def conv_three(padded, weight):
    batched = padded if padded.ndim == 4 else padded[None]
    result = lax.conv_general_dilated(
        batched,
        weight,
        (1, 1),
        "VALID",
        dimension_numbers=("NHWC", "HWIO", "NHWC"),
        preferred_element_type=jnp.float32,
    )
    return result if padded.ndim == 4 else result[0]


def pool_pairs(field):
    summed = lax.reduce_window(
        field, jnp.array(0, field.dtype), lax.add, (2, 2, 1), (2, 2, 1), "VALID"
    )
    return summed * 0.25


def head_kernel(valid_ref, band_ref, scale_ref, shift_ref, w_ref, mix_ref, out_ref):
    block = pl.program_id(1)
    cols = band_ref.shape[1]
    width = band_ref.shape[2]
    gain = 1.0 + scale_ref[0]
    shift = shift_ref[0]

    def modulated(row):
        value = (band_ref[row].astype(jnp.float32) * gain + shift).astype(jnp.bfloat16)
        return jnp.where(valid_ref[row] > 0, value, jnp.zeros_like(value))

    def one_row(j, carry):
        row = block * HEAD_ROWS + j
        rows = [modulated(row + k) for k in range(3)]
        stacked = jnp.concatenate(rows, axis=-1)
        taps = jnp.dot(stacked, w_ref[...], preferred_element_type=jnp.float32)
        conv = (
            pltpu.roll(taps[:, :width], 1, 0)
            + taps[:, width : 2 * width]
            + pltpu.roll(taps[:, 2 * width :], cols - 1, 0)
        )
        hidden = jax.nn.gelu(conv).astype(jnp.bfloat16)
        mixed = jnp.dot(mix_ref[...], hidden, preferred_element_type=jnp.float32)
        out_ref[0, j] = (rows[1].astype(jnp.float32) + mixed).astype(out_ref.dtype)
        return carry

    lax.fori_loop(0, HEAD_ROWS, one_row, 0)


def head(valid, band, scales, shifts, w_all, zonal_mix):
    halo_rows, cols, width = band.shape
    rows = halo_rows - 2
    leads = scales.shape[0]
    return pl.pallas_call(
        head_kernel,
        out_shape=jax.ShapeDtypeStruct((leads, rows, cols, width), jnp.bfloat16),
        grid=(leads, rows // HEAD_ROWS),
        in_specs=[
            pl.BlockSpec(memory_space=pltpu.SMEM),
            pl.BlockSpec((halo_rows, cols, width), lambda l, b: (0, 0, 0)),
            pl.BlockSpec((1, 1, width), lambda l, b: (l, 0, 0)),
            pl.BlockSpec((1, 1, width), lambda l, b: (l, 0, 0)),
            pl.BlockSpec((3 * width, 3 * width), lambda l, b: (0, 0)),
            pl.BlockSpec((cols, cols), lambda l, b: (0, 0)),
        ],
        out_specs=pl.BlockSpec((1, HEAD_ROWS, cols, width), lambda l, b: (l, b, 0, 0)),
        compiler_params=pltpu.CompilerParams(vmem_limit_bytes=48 * 1024 * 1024),
    )(valid, band, scales[:, None, :], shifts[:, None, :], w_all, zonal_mix)


def shards(inputs, w_enc, w_proj, film_scale, film_shift, lead_ids, w_head, zonal_mix):
    lat_rows, lon_cols, channels = inputs.shape
    with_rows = extended(inputs, (("lat", 0),), 1, False)
    padded = extended(with_rows, (("lon", 1),), 1, True)
    encoded = jax.nn.gelu(conv_three(padded, w_enc))
    pooled = pool_pairs(encoded).astype(jnp.bfloat16)
    head_width = w_proj.shape[1]
    lon_group = lax.axis_index("lon")
    my_rows = lax.dynamic_slice_in_dim(lead_ids, lon_group * LEAD_DEV, LEAD_DEV)
    flat = jnp.dot(pooled.reshape(-1, channels), w_proj, preferred_element_type=jnp.float32)
    tile = flat.astype(jnp.bfloat16).reshape(pooled.shape[0], pooled.shape[1], head_width)
    tile = extended(tile, (("lat", 0),), 1, False)
    band = lax.all_gather(tile, "lon", axis=1, tiled=True)
    scales = jnp.take(film_scale, my_rows, axis=0)
    shifts = jnp.take(film_shift, my_rows, axis=0)
    lat = lax.axis_index("lat")
    halo_rows = band.shape[0]
    index = jnp.arange(halo_rows, dtype=jnp.int32)
    valid = ((index > 0) | (lat > 0)) & ((index < halo_rows - 1) | (lat < lax.axis_size("lat") - 1))
    w_all = jnp.transpose(w_head, (0, 2, 1, 3)).reshape(3 * head_width, 3 * head_width)
    return head(valid.astype(jnp.int32), band, scales, shifts, w_all, zonal_mix)


def solution(mesh):
    in_specs = (P("lat", "lon", None), P(), P(), P(), P(), P(), P(), P())
    out_specs = P("lon", "lat", None, None)
    return jax.shard_map(shards, mesh=mesh, in_specs=in_specs, out_specs=out_specs, check_vma=False)
```

```python
import functools

import jax
import jax.numpy as jnp
from jax import lax
from jax.experimental import pallas as pl
from jax.experimental.pallas import tpu as pltpu
from jax.sharding import PartitionSpec as P

LEAD_DEV = 2
HEAD_ROWS = 4


def extended(x, sides, width, wrap):
    for axis, dim in sides:
        devices, length = (lax.axis_size(axis), x.shape[dim])
        up = [(i, (i + 1) % devices) for i in range(devices if wrap else devices - 1)]
        down = [(j, i) for i, j in up]
        last = lax.slice_in_dim(x, length - width, length, axis=dim)
        initial = lax.slice_in_dim(x, 0, width, axis=dim)
        before = lax.ppermute(last, axis, up)
        after = lax.ppermute(initial, axis, down)
        x = jnp.concatenate([before, x, after], axis=dim)
    return x


def conv_three(padded, weight):
    batched = padded if padded.ndim == 4 else padded[None]
    result = lax.conv_general_dilated(
        batched,
        weight,
        (1, 1),
        "VALID",
        dimension_numbers=("NHWC", "HWIO", "NHWC"),
        preferred_element_type=jnp.float32,
    )
    return result if padded.ndim == 4 else result[0]


def pool_pairs(field):
    summed = lax.reduce_window(
        field, jnp.array(0, field.dtype), lax.add, (2, 2, 1), (2, 2, 1), "VALID"
    )
    return summed * 0.25


def encoder_kernel(x_ref, w_ref, proj_ref, out_ref, pair_ref):
    cols = x_ref.shape[1]
    width = x_ref.shape[2]
    pooled_cols = out_ref.shape[1]

    def encoded(row):
        stacked = jnp.concatenate([x_ref[row + k] for k in range(3)], axis=-1)
        taps = jnp.dot(stacked, w_ref[...], preferred_element_type=jnp.float32)
        conv = (
            taps[:, :width]
            + pltpu.roll(taps[:, width : 2 * width], cols - 1, 0)
            + pltpu.roll(taps[:, 2 * width :], cols - 2, 0)
        )
        return jax.nn.gelu(conv)

    def one_row(p, carry):
        pair = encoded(2 * p) + encoded(2 * p + 1)
        lanes = pair_ref.shape[2]
        chunks = []
        for c in range(width // lanes):
            pair_ref[c, pl.ds(0, cols)] = pair[:, c * lanes : (c + 1) * lanes]
            pair_ref[c, pl.ds(cols, 8)] = jnp.zeros((8, lanes), jnp.float32)
            half = pair_ref.shape[1] // 2
            chunks.append(
                pair_ref[c, pl.ds(0, half, stride=2)] + pair_ref[c, pl.ds(1, half, stride=2)]
            )
        summed = jnp.concatenate(chunks, axis=-1)
        pooled = (summed * 0.25).astype(jnp.bfloat16)
        projected = jnp.dot(pooled, proj_ref[...], preferred_element_type=jnp.float32)
        out_ref[p] = projected[:pooled_cols].astype(out_ref.dtype)
        return carry

    lax.fori_loop(0, out_ref.shape[0], one_row, 0)


def encoder(padded, w_enc, w_proj):
    rows, cols, width = padded.shape
    pooled_rows, pooled_cols = (rows - 2) // 2, (cols - 4) // 2
    w_all = jnp.transpose(w_enc, (0, 2, 1, 3)).reshape(3 * width, 3 * width)
    vmem = pl.BlockSpec(memory_space=pltpu.VMEM)
    return pl.pallas_call(
        encoder_kernel,
        out_shape=jax.ShapeDtypeStruct((pooled_rows, pooled_cols, w_proj.shape[1]), jnp.bfloat16),
        in_specs=[vmem, vmem, vmem],
        out_specs=vmem,
        scratch_shapes=[pltpu.VMEM((width // 128, cols + 8, 128), jnp.float32)],
        compiler_params=pltpu.CompilerParams(vmem_limit_bytes=48 * 1024 * 1024),
    )(padded, w_all, w_proj)


def head_kernel(valid_ref, band_ref, scale_ref, shift_ref, w_ref, mix_ref, out_ref):
    block = pl.program_id(1)
    cols = band_ref.shape[1]
    width = band_ref.shape[2]
    gain = 1.0 + scale_ref[0]
    shift = shift_ref[0]

    def modulated(row):
        value = (band_ref[row].astype(jnp.float32) * gain + shift).astype(jnp.bfloat16)
        return jnp.where(valid_ref[row] > 0, value, jnp.zeros_like(value))

    def one_row(j, carry):
        row = block * HEAD_ROWS + j
        rows = [modulated(row + k) for k in range(3)]
        stacked = jnp.concatenate(rows, axis=-1)
        taps = jnp.dot(stacked, w_ref[...], preferred_element_type=jnp.float32)
        conv = (
            pltpu.roll(taps[:, :width], 1, 0)
            + taps[:, width : 2 * width]
            + pltpu.roll(taps[:, 2 * width :], cols - 1, 0)
        )
        hidden = jax.nn.gelu(conv).astype(jnp.bfloat16)
        mixed = jnp.dot(mix_ref[...], hidden, preferred_element_type=jnp.float32)
        out_ref[0, j] = (rows[1].astype(jnp.float32) + mixed).astype(out_ref.dtype)
        return carry

    lax.fori_loop(0, HEAD_ROWS, one_row, 0)


def head(valid, band, scales, shifts, w_all, zonal_mix):
    halo_rows, cols, width = band.shape
    rows = halo_rows - 2
    leads = scales.shape[0]
    return pl.pallas_call(
        head_kernel,
        out_shape=jax.ShapeDtypeStruct((leads, rows, cols, width), jnp.bfloat16),
        grid=(leads, rows // HEAD_ROWS),
        in_specs=[
            pl.BlockSpec(memory_space=pltpu.SMEM),
            pl.BlockSpec((halo_rows, cols, width), lambda l, b: (0, 0, 0)),
            pl.BlockSpec((1, 1, width), lambda l, b: (l, 0, 0)),
            pl.BlockSpec((1, 1, width), lambda l, b: (l, 0, 0)),
            pl.BlockSpec((3 * width, 3 * width), lambda l, b: (0, 0)),
            pl.BlockSpec((cols, cols), lambda l, b: (0, 0)),
        ],
        out_specs=pl.BlockSpec((1, HEAD_ROWS, cols, width), lambda l, b: (l, b, 0, 0)),
        compiler_params=pltpu.CompilerParams(vmem_limit_bytes=48 * 1024 * 1024),
    )(valid, band, scales[:, None, :], shifts[:, None, :], w_all, zonal_mix)


def shards(inputs, w_enc, w_proj, film_scale, film_shift, lead_ids, w_head, zonal_mix):
    lat_rows, lon_cols, channels = inputs.shape
    with_rows = extended(inputs, (("lat", 0),), 1, False)
    padded = extended(with_rows, (("lon", 1),), 1, True)
    padded = jnp.pad(padded, ((0, 0), (0, 2), (0, 0)))
    tile = encoder(padded, w_enc, w_proj)
    head_width = w_proj.shape[1]
    lon_group = lax.axis_index("lon")
    my_rows = lax.dynamic_slice_in_dim(lead_ids, lon_group * LEAD_DEV, LEAD_DEV)
    tile = extended(tile, (("lat", 0),), 1, False)
    band = lax.all_gather(tile, "lon", axis=1, tiled=True)
    scales = jnp.take(film_scale, my_rows, axis=0)
    shifts = jnp.take(film_shift, my_rows, axis=0)
    lat = lax.axis_index("lat")
    halo_rows = band.shape[0]
    index = jnp.arange(halo_rows, dtype=jnp.int32)
    valid = ((index > 0) | (lat > 0)) & ((index < halo_rows - 1) | (lat < lax.axis_size("lat") - 1))
    w_all = jnp.transpose(w_head, (0, 2, 1, 3)).reshape(3 * head_width, 3 * head_width)
    return head(valid.astype(jnp.int32), band, scales, shifts, w_all, zonal_mix)


def solution(mesh):
    in_specs = (P("lat", "lon", None), P(), P(), P(), P(), P(), P(), P())
    out_specs = P("lon", "lat", None, None)
    return jax.shard_map(shards, mesh=mesh, in_specs=in_specs, out_specs=out_specs, check_vma=False)
```

```python
import functools

import jax
import jax.numpy as jnp
from jax import lax
from jax.experimental import pallas as pl
from jax.experimental.pallas import tpu as pltpu
from jax.sharding import PartitionSpec as P

LEAD_DEV = 2
HEAD_ROWS = 5


def extended(x, sides, width, wrap):
    for axis, dim in sides:
        devices, length = (lax.axis_size(axis), x.shape[dim])
        up = [(i, (i + 1) % devices) for i in range(devices if wrap else devices - 1)]
        down = [(j, i) for i, j in up]
        last = lax.slice_in_dim(x, length - width, length, axis=dim)
        initial = lax.slice_in_dim(x, 0, width, axis=dim)
        before = lax.ppermute(last, axis, up)
        after = lax.ppermute(initial, axis, down)
        x = jnp.concatenate([before, x, after], axis=dim)
    return x


def conv_three(padded, weight):
    batched = padded if padded.ndim == 4 else padded[None]
    result = lax.conv_general_dilated(
        batched,
        weight,
        (1, 1),
        "VALID",
        dimension_numbers=("NHWC", "HWIO", "NHWC"),
        preferred_element_type=jnp.float32,
    )
    return result if padded.ndim == 4 else result[0]


def pool_pairs(field):
    summed = lax.reduce_window(
        field, jnp.array(0, field.dtype), lax.add, (2, 2, 1), (2, 2, 1), "VALID"
    )
    return summed * 0.25


def encoder_kernel(x_ref, w_ref, proj_ref, out_ref, pair_ref):
    cols = x_ref.shape[1]
    width = x_ref.shape[2]
    pooled_cols = out_ref.shape[1]

    def encoded(row):
        stacked = jnp.concatenate([x_ref[row + k] for k in range(3)], axis=-1)
        taps = jnp.dot(stacked, w_ref[...], preferred_element_type=jnp.float32)
        conv = (
            taps[:, :width]
            + pltpu.roll(taps[:, width : 2 * width], cols - 1, 0)
            + pltpu.roll(taps[:, 2 * width :], cols - 2, 0)
        )
        return jax.nn.gelu(conv)

    def one_row(p, carry):
        pair = encoded(2 * p) + encoded(2 * p + 1)
        lanes = pair_ref.shape[2]
        chunks = []
        for c in range(width // lanes):
            pair_ref[c, pl.ds(0, cols)] = pair[:, c * lanes : (c + 1) * lanes]
            pair_ref[c, pl.ds(cols, 8)] = jnp.zeros((8, lanes), jnp.float32)
            half = pair_ref.shape[1] // 2
            chunks.append(
                pair_ref[c, pl.ds(0, half, stride=2)] + pair_ref[c, pl.ds(1, half, stride=2)]
            )
        summed = jnp.concatenate(chunks, axis=-1)
        pooled = (summed * 0.25).astype(jnp.bfloat16)
        projected = jnp.dot(pooled, proj_ref[...], preferred_element_type=jnp.float32)
        out_ref[p] = projected[:pooled_cols].astype(out_ref.dtype)
        return carry

    lax.fori_loop(0, out_ref.shape[0], one_row, 0)


def encoder(padded, w_enc, w_proj):
    rows, cols, width = padded.shape
    pooled_rows, pooled_cols = (rows - 2) // 2, (cols - 4) // 2
    w_all = jnp.transpose(w_enc, (0, 2, 1, 3)).reshape(3 * width, 3 * width)
    vmem = pl.BlockSpec(memory_space=pltpu.VMEM)
    return pl.pallas_call(
        encoder_kernel,
        out_shape=jax.ShapeDtypeStruct((pooled_rows, pooled_cols, w_proj.shape[1]), jnp.bfloat16),
        in_specs=[vmem, vmem, vmem],
        out_specs=vmem,
        scratch_shapes=[pltpu.VMEM((width // 128, cols + 8, 128), jnp.float32)],
        compiler_params=pltpu.CompilerParams(vmem_limit_bytes=48 * 1024 * 1024),
    )(padded, w_all, w_proj)


def head_kernel(chunk, valid_ref, main_ref, next_ref, scale_ref, shift_ref, w_ref, mix_ref, *rest):
    out_ref, mod_ref, hidden_ref = rest[-3:]
    rows = main_ref.shape[0]
    cols = main_ref.shape[1]
    width = main_ref.shape[2]
    gain = 1.0 + scale_ref[0]
    shift = shift_ref[0]
    for j in range(rows + 2):
        source = main_ref[j] if j < rows else next_ref[j - rows]
        value = (source.astype(jnp.float32) * gain + shift).astype(jnp.bfloat16)
        keep = valid_ref[chunk * rows + j] > 0
        mod_ref[j] = jnp.where(keep, value, jnp.zeros_like(value))
    for j in range(rows):
        stacked = jnp.concatenate([mod_ref[j + k] for k in range(3)], axis=-1)
        taps = jnp.dot(stacked, w_ref[...], preferred_element_type=jnp.float32)
        conv = (
            pltpu.roll(taps[:, :width], 1, 0)
            + taps[:, width : 2 * width]
            + pltpu.roll(taps[:, 2 * width :], cols - 1, 0)
        )
        hidden_ref[:, j * width : (j + 1) * width] = jax.nn.gelu(conv).astype(jnp.bfloat16)
    mixed = jnp.dot(mix_ref[...], hidden_ref[...], preferred_element_type=jnp.float32)
    for j in range(rows):
        own = mod_ref[j + 1].astype(jnp.float32)
        out_ref[0, j] = (own + mixed[:, j * width : (j + 1) * width]).astype(out_ref.dtype)


def head(chunk, total_rows, previous, valid, main, following, scales, shifts, w_all, zonal_mix):
    rows, cols, width = main.shape
    leads = scales.shape[0]
    in_specs = [
        pl.BlockSpec(memory_space=pltpu.SMEM),
        pl.BlockSpec((rows, cols, width), lambda l: (0, 0, 0)),
        pl.BlockSpec((2, cols, width), lambda l: (0, 0, 0)),
        pl.BlockSpec((1, 1, width), lambda l: (l, 0, 0)),
        pl.BlockSpec((1, 1, width), lambda l: (l, 0, 0)),
        pl.BlockSpec((3 * width, 3 * width), lambda l: (0, 0)),
        pl.BlockSpec((cols, cols), lambda l: (0, 0)),
    ]
    operands = [valid, main, following, scales[:, None, :], shifts[:, None, :], w_all, zonal_mix]
    aliases = {}
    if previous is not None:
        in_specs.append(pl.BlockSpec(memory_space=pl.ANY))
        operands.append(previous)
        aliases = {len(operands) - 1: 0}
    return pl.pallas_call(
        functools.partial(head_kernel, chunk),
        out_shape=jax.ShapeDtypeStruct((leads, total_rows, cols, width), jnp.bfloat16),
        grid=(leads,),
        in_specs=in_specs,
        out_specs=pl.BlockSpec((1, rows, cols, width), lambda l: (l, chunk, 0, 0)),
        scratch_shapes=[
            pltpu.VMEM((rows + 2, cols, width), jnp.bfloat16),
            pltpu.VMEM((cols, rows * width), jnp.bfloat16),
        ],
        input_output_aliases=aliases,
        compiler_params=pltpu.CompilerParams(vmem_limit_bytes=48 * 1024 * 1024),
    )(*operands)


def shards(inputs, w_enc, w_proj, film_scale, film_shift, lead_ids, w_head, zonal_mix):
    lat_rows, lon_cols, channels = inputs.shape
    with_rows = extended(inputs, (("lat", 0),), 1, False)
    padded = extended(with_rows, (("lon", 1),), 1, True)
    padded = jnp.pad(padded, ((0, 0), (0, 2), (0, 0)))
    tile = encoder(padded, w_enc, w_proj)
    head_width = w_proj.shape[1]
    lon_group = lax.axis_index("lon")
    my_rows = lax.dynamic_slice_in_dim(lead_ids, lon_group * LEAD_DEV, LEAD_DEV)
    tile = extended(tile, (("lat", 0),), 1, False)
    scales = jnp.take(film_scale, my_rows, axis=0)
    shifts = jnp.take(film_shift, my_rows, axis=0)
    lat = lax.axis_index("lat")
    halo_rows = tile.shape[0]
    rows = halo_rows - 2
    index = jnp.arange(halo_rows, dtype=jnp.int32)
    valid = ((index > 0) | (lat > 0)) & ((index < halo_rows - 1) | (lat < lax.axis_size("lat") - 1))
    valid = valid.astype(jnp.int32)
    w_all = jnp.transpose(w_head, (0, 2, 1, 3)).reshape(3 * head_width, 3 * head_width)
    chunks = rows // HEAD_ROWS
    bands = [
        lax.all_gather(tile[k * HEAD_ROWS : (k + 1) * HEAD_ROWS], "lon", axis=1, tiled=True)
        for k in range(chunks)
    ]
    bands.append(lax.all_gather(tile[rows:], "lon", axis=1, tiled=True))
    out = None
    for k in range(chunks):
        out = head(k, rows, out, valid, bands[k], bands[k + 1], scales, shifts, w_all, zonal_mix)
    return out


def solution(mesh):
    in_specs = (P("lat", "lon", None), P(), P(), P(), P(), P(), P(), P())
    out_specs = P("lon", "lat", None, None)
    return jax.shard_map(shards, mesh=mesh, in_specs=in_specs, out_specs=out_specs, check_vma=False)
```

```python
import functools

import jax
import jax.numpy as jnp
from jax import lax
from jax.experimental import pallas as pl
from jax.experimental.pallas import tpu as pltpu
from jax.sharding import PartitionSpec as P

LEAD_DEV = 2
HEAD_ROWS = 2
MESH = pl.DeviceIdType.MESH


def extended(x, sides, width, wrap):
    for axis, dim in sides:
        devices, length = (lax.axis_size(axis), x.shape[dim])
        up = [(i, (i + 1) % devices) for i in range(devices if wrap else devices - 1)]
        down = [(j, i) for i, j in up]
        last = lax.slice_in_dim(x, length - width, length, axis=dim)
        initial = lax.slice_in_dim(x, 0, width, axis=dim)
        before = lax.ppermute(last, axis, up)
        after = lax.ppermute(initial, axis, down)
        x = jnp.concatenate([before, x, after], axis=dim)
    return x


def conv_three(padded, weight):
    batched = padded if padded.ndim == 4 else padded[None]
    result = lax.conv_general_dilated(
        batched,
        weight,
        (1, 1),
        "VALID",
        dimension_numbers=("NHWC", "HWIO", "NHWC"),
        preferred_element_type=jnp.float32,
    )
    return result if padded.ndim == 4 else result[0]


def pool_pairs(field):
    summed = lax.reduce_window(
        field, jnp.array(0, field.dtype), lax.add, (2, 2, 1), (2, 2, 1), "VALID"
    )
    return summed * 0.25


def encoder_kernel(x_ref, w_ref, proj_ref, out_ref, pair_ref):
    cols = x_ref.shape[1]
    width = x_ref.shape[2]
    pooled_cols = out_ref.shape[1]

    def encoded(row):
        stacked = jnp.concatenate([x_ref[row + k] for k in range(3)], axis=-1)
        taps = jnp.dot(stacked, w_ref[...], preferred_element_type=jnp.float32)
        conv = (
            taps[:, :width]
            + pltpu.roll(taps[:, width : 2 * width], cols - 1, 0)
            + pltpu.roll(taps[:, 2 * width :], cols - 2, 0)
        )
        return jax.nn.gelu(conv)

    def one_row(p, carry):
        pair = encoded(2 * p) + encoded(2 * p + 1)
        lanes = pair_ref.shape[2]
        chunks = []
        for c in range(width // lanes):
            pair_ref[c, pl.ds(0, cols)] = pair[:, c * lanes : (c + 1) * lanes]
            pair_ref[c, pl.ds(cols, 8)] = jnp.zeros((8, lanes), jnp.float32)
            half = pair_ref.shape[1] // 2
            chunks.append(
                pair_ref[c, pl.ds(0, half, stride=2)] + pair_ref[c, pl.ds(1, half, stride=2)]
            )
        summed = jnp.concatenate(chunks, axis=-1)
        pooled = (summed * 0.25).astype(jnp.bfloat16)
        projected = jnp.dot(pooled, proj_ref[...], preferred_element_type=jnp.float32)
        out_ref[p] = projected[:pooled_cols].astype(out_ref.dtype)
        return carry

    lax.fori_loop(0, out_ref.shape[0], one_row, 0)


def encoder(padded, w_enc, w_proj):
    rows, cols, width = padded.shape
    pooled_rows, pooled_cols = (rows - 2) // 2, (cols - 4) // 2
    w_all = jnp.transpose(w_enc, (0, 2, 1, 3)).reshape(3 * width, 3 * width)
    vmem = pl.BlockSpec(memory_space=pltpu.VMEM)
    return pl.pallas_call(
        encoder_kernel,
        out_shape=jax.ShapeDtypeStruct((pooled_rows, pooled_cols, w_proj.shape[1]), jnp.bfloat16),
        in_specs=[vmem, vmem, vmem],
        out_specs=vmem,
        scratch_shapes=[pltpu.VMEM((width // 128, cols + 8, 128), jnp.float32)],
        compiler_params=pltpu.CompilerParams(vmem_limit_bytes=48 * 1024 * 1024),
    )(padded, w_all, w_proj)


def head_kernel(tile_ref, scale_ref, shift_ref, w_ref, mix_ref, out_ref, band_ref, mod_ref,
                hidden_ref, send_sem, recv_sem, local_sem):
    me = lax.axis_index("lon")
    n = lax.axis_size("lon")
    lat = lax.axis_index("lat")
    last_lat = lax.axis_size("lat") - 1
    halo_rows, tile_cols, width = tile_ref.shape
    cols = band_ref.shape[1]
    leads = out_ref.shape[0]
    step = HEAD_ROWS
    pieces = halo_rows // step

    barrier = pltpu.get_barrier_semaphore()
    for s in range(1, n):
        peer = lax.rem(me + s, n)
        pl.semaphore_signal(barrier, inc=1, device_id=(lat, peer), device_id_type=MESH)
    pl.semaphore_wait(barrier, n - 1)

    def slot(piece, source):
        start = pl.multiple_of(piece * step, step)
        return band_ref.at[pl.ds(start, step), pl.ds(source * tile_cols, tile_cols)]

    def source_rows(piece):
        return tile_ref.at[pl.ds(pl.multiple_of(piece * step, step), step)]

    def local_copy(piece):
        return pltpu.make_async_copy(source_rows(piece), slot(piece, me), local_sem.at[piece])

    def remote_copy(piece, s, target, source):
        return pltpu.make_async_remote_copy(
            src_ref=source_rows(piece),
            dst_ref=slot(piece, source),
            send_sem=send_sem.at[piece * n + s],
            recv_sem=recv_sem.at[piece * n + s],
            device_id=(lat, target),
            device_id_type=MESH,
        )

    for piece in range(pieces):
        local_copy(piece).start()
        for s in range(1, n):
            remote_copy(piece, s, lax.rem(me + s, n), me).start()

    def arrived(piece):
        local_copy(piece).wait()
        for s in range(1, n):
            remote_copy(piece, s, me, lax.rem(me + n - s, n)).wait_recv()

    arrived(0)

    def one_chunk(k, carry):
        arrived(k + 1)
        base = k * step
        for l in range(leads):
            gain = 1.0 + scale_ref[l]
            shift = shift_ref[l]
            for j in range(step + 2):
                row = base + j
                keep = ((row > 0) | (lat > 0)) & ((row < halo_rows - 1) | (lat < last_lat))
                value = band_ref[row].astype(jnp.float32) * gain + shift
                value = jnp.where(keep, value, 0.0)
                mod_ref[l, j] = value.astype(jnp.bfloat16)
            for j in range(step):
                stacked = jnp.concatenate([mod_ref[l, j + t] for t in range(3)], axis=-1)
                taps = jnp.dot(stacked, w_ref[...], preferred_element_type=jnp.float32)
                conv = (
                    pltpu.roll(taps[:, :width], 1, 0)
                    + taps[:, width : 2 * width]
                    + pltpu.roll(taps[:, 2 * width :], cols - 1, 0)
                )
                at = (l * step + j) * width
                hidden_ref[:, at : at + width] = jax.nn.gelu(conv).astype(jnp.bfloat16)
        mixed = jnp.dot(mix_ref[...], hidden_ref[...], preferred_element_type=jnp.float32)
        for l in range(leads):
            for j in range(step):
                at = (l * step + j) * width
                own = mod_ref[l, j + 1].astype(jnp.float32)
                out_ref[l, base + j] = (own + mixed[:, at : at + width]).astype(out_ref.dtype)
        return carry

    lax.fori_loop(0, pieces - 1, one_chunk, 0)

    for piece in range(pieces):
        for s in range(1, n):
            remote_copy(piece, s, lax.rem(me + s, n), me).wait_send()


def head(tile, scales, shifts, w_all, zonal_mix, lon_devices):
    halo_rows, tile_cols, width = tile.shape
    rows = halo_rows - 2
    cols = tile_cols * lon_devices
    leads = scales.shape[0]
    pieces = halo_rows // HEAD_ROWS
    vmem = pl.BlockSpec(memory_space=pltpu.VMEM)
    return pl.pallas_call(
        head_kernel,
        out_shape=jax.ShapeDtypeStruct((leads, rows, cols, width), jnp.bfloat16),
        in_specs=[pl.BlockSpec(memory_space=pl.ANY), vmem, vmem, vmem, vmem],
        out_specs=vmem,
        scratch_shapes=[
            pltpu.VMEM((halo_rows, cols, width), jnp.bfloat16),
            pltpu.VMEM((leads, HEAD_ROWS + 2, cols, width), jnp.bfloat16),
            pltpu.VMEM((cols, leads * HEAD_ROWS * width), jnp.bfloat16),
            pltpu.SemaphoreType.DMA((pieces * lon_devices,)),
            pltpu.SemaphoreType.DMA((pieces * lon_devices,)),
            pltpu.SemaphoreType.DMA((pieces,)),
        ],
        compiler_params=pltpu.CompilerParams(
            collective_id=0, has_side_effects=True, vmem_limit_bytes=56 * 1024 * 1024
        ),
    )(tile, scales[:, None, :], shifts[:, None, :], w_all, zonal_mix)


def shards(inputs, w_enc, w_proj, film_scale, film_shift, lead_ids, w_head, zonal_mix):
    lat_rows, lon_cols, channels = inputs.shape
    with_rows = extended(inputs, (("lat", 0),), 1, False)
    padded = extended(with_rows, (("lon", 1),), 1, True)
    padded = jnp.pad(padded, ((0, 0), (0, 2), (0, 0)))
    tile = encoder(padded, w_enc, w_proj)
    head_width = w_proj.shape[1]
    lon_group = lax.axis_index("lon")
    my_rows = lax.dynamic_slice_in_dim(lead_ids, lon_group * LEAD_DEV, LEAD_DEV)
    tile = extended(tile, (("lat", 0),), 1, False)
    scales = jnp.take(film_scale, my_rows, axis=0)
    shifts = jnp.take(film_shift, my_rows, axis=0)
    w_all = jnp.transpose(w_head, (0, 2, 1, 3)).reshape(3 * head_width, 3 * head_width)
    return head(tile, scales, shifts, w_all, zonal_mix, lax.axis_size("lon"))

def solution(mesh):
    in_specs = (P("lat", "lon", None), P(), P(), P(), P(), P(), P(), P())
    out_specs = P("lon", "lat", None, None)
    return jax.shard_map(shards, mesh=mesh, in_specs=in_specs, out_specs=out_specs, check_vma=False)
```

```python
import functools

import jax
import jax.numpy as jnp
from jax import lax
from jax.experimental import pallas as pl
from jax.experimental.pallas import tpu as pltpu
from jax.sharding import PartitionSpec as P

LEAD_DEV = 2
HEAD_ROWS = 2
MESH = pl.DeviceIdType.MESH


def extended(x, sides, width, wrap):
    for axis, dim in sides:
        devices, length = (lax.axis_size(axis), x.shape[dim])
        up = [(i, (i + 1) % devices) for i in range(devices if wrap else devices - 1)]
        down = [(j, i) for i, j in up]
        last = lax.slice_in_dim(x, length - width, length, axis=dim)
        initial = lax.slice_in_dim(x, 0, width, axis=dim)
        before = lax.ppermute(last, axis, up)
        after = lax.ppermute(initial, axis, down)
        x = jnp.concatenate([before, x, after], axis=dim)
    return x


def conv_three(padded, weight):
    batched = padded if padded.ndim == 4 else padded[None]
    result = lax.conv_general_dilated(
        batched,
        weight,
        (1, 1),
        "VALID",
        dimension_numbers=("NHWC", "HWIO", "NHWC"),
        preferred_element_type=jnp.float32,
    )
    return result if padded.ndim == 4 else result[0]


def pool_pairs(field):
    summed = lax.reduce_window(
        field, jnp.array(0, field.dtype), lax.add, (2, 2, 1), (2, 2, 1), "VALID"
    )
    return summed * 0.25


def encoder_kernel(x_ref, w_ref, proj_ref, out_ref, pair_ref):
    cols = x_ref.shape[1]
    width = x_ref.shape[2]
    pooled_cols = out_ref.shape[1]

    def encoded(row):
        stacked = jnp.concatenate([x_ref[row + k] for k in range(3)], axis=-1)
        taps = jnp.dot(stacked, w_ref[...], preferred_element_type=jnp.float32)
        conv = (
            taps[:, :width]
            + pltpu.roll(taps[:, width : 2 * width], cols - 1, 0)
            + pltpu.roll(taps[:, 2 * width :], cols - 2, 0)
        )
        return jax.nn.gelu(conv)

    def one_row(p, carry):
        pair = encoded(2 * p) + encoded(2 * p + 1)
        lanes = pair_ref.shape[2]
        chunks = []
        for c in range(width // lanes):
            pair_ref[c, pl.ds(0, cols)] = pair[:, c * lanes : (c + 1) * lanes]
            pair_ref[c, pl.ds(cols, 8)] = jnp.zeros((8, lanes), jnp.float32)
            half = pair_ref.shape[1] // 2
            chunks.append(
                pair_ref[c, pl.ds(0, half, stride=2)] + pair_ref[c, pl.ds(1, half, stride=2)]
            )
        summed = jnp.concatenate(chunks, axis=-1)
        pooled = (summed * 0.25).astype(jnp.bfloat16)
        projected = jnp.dot(pooled, proj_ref[...], preferred_element_type=jnp.float32)
        out_ref[p] = projected[:pooled_cols].astype(out_ref.dtype)
        return carry

    lax.fori_loop(0, out_ref.shape[0], one_row, 0)


def encoder(padded, w_enc, w_proj):
    rows, cols, width = padded.shape
    pooled_rows, pooled_cols = (rows - 2) // 2, (cols - 4) // 2
    w_all = jnp.transpose(w_enc, (0, 2, 1, 3)).reshape(3 * width, 3 * width)
    vmem = pl.BlockSpec(memory_space=pltpu.VMEM)
    return pl.pallas_call(
        encoder_kernel,
        out_shape=jax.ShapeDtypeStruct((pooled_rows, pooled_cols, w_proj.shape[1]), jnp.bfloat16),
        in_specs=[vmem, vmem, vmem],
        out_specs=vmem,
        scratch_shapes=[pltpu.VMEM((width // 128, cols + 8, 128), jnp.float32)],
        compiler_params=pltpu.CompilerParams(vmem_limit_bytes=48 * 1024 * 1024),
    )(padded, w_all, w_proj)


def head_kernel(tile_ref, scale_ref, shift_ref, w_ref, mix_ref, out_ref, band_ref, mod_ref,
                hidden_ref, send_sem, recv_sem, local_sem):
    me = lax.axis_index("lon")
    n = lax.axis_size("lon")
    lat = lax.axis_index("lat")
    last_lat = lax.axis_size("lat") - 1
    halo_rows, tile_cols, width = tile_ref.shape
    cols = band_ref.shape[1]
    leads = out_ref.shape[0]
    step = HEAD_ROWS
    pieces = halo_rows // step

    chips = n // 2
    chip = me // 2
    core = me % 2
    sense = 1 - 2 * core
    kinds = 7

    def device(at_chip, at_core):
        return 2 * lax.rem(at_chip + 2 * chips, chips) + at_core

    sibling = device(chip, 1 - core)
    east = device(chip + 1, core)
    west = device(chip - 1, core)
    far = device(chip + 2, core)
    behind = device(chip - sense, core)
    ahead = device(chip + sense, core)

    barrier = pltpu.get_barrier_semaphore()
    for peer in (sibling, east, west):
        pl.semaphore_signal(barrier, inc=1, device_id=(lat, peer), device_id_type=MESH)
    pl.semaphore_wait(barrier, 3)

    def slot(piece, source):
        start = pl.multiple_of(piece * step, step)
        return band_ref.at[pl.ds(start, step), pl.ds(source * tile_cols, tile_cols)]

    def source_rows(piece):
        return tile_ref.at[pl.ds(pl.multiple_of(piece * step, step), step)]

    def local_copy(piece):
        return pltpu.make_async_copy(source_rows(piece), slot(piece, me), local_sem.at[piece])

    def transfer(piece, kind, origin, target, own=False):
        return pltpu.make_async_remote_copy(
            src_ref=source_rows(piece) if own else slot(piece, origin),
            dst_ref=slot(piece, origin),
            send_sem=send_sem.at[piece * kinds + kind],
            recv_sem=recv_sem.at[piece * kinds + kind],
            device_id=(lat, target),
            device_id_type=MESH,
        )

    def sends(piece):
        return [
            transfer(piece, 0, me, sibling, own=True),
            transfer(piece, 1, me, east, own=True),
            transfer(piece, 2, me, west, own=True),
            transfer(piece, 3, behind, ahead),
            transfer(piece, 4, west, sibling),
            transfer(piece, 5, east, sibling),
            transfer(piece, 6, far, sibling),
        ]

    def receive(piece, kind, origin):
        transfer(piece, kind, origin, me).wait_recv()

    for piece in range(pieces):
        local_copy(piece).start()
        for copy in sends(piece)[:3]:
            copy.start()

    def forward_x(piece):
        receive(piece, 1 + core, behind)
        sends(piece)[3].start()

    def forward_sibling(piece):
        receive(piece, 2 - core, ahead)
        receive(piece, 3, far)
        for copy in sends(piece)[4:]:
            copy.start()

    def arrived(piece):
        local_copy(piece).wait()
        receive(piece, 0, sibling)
        receive(piece, 4, device(chip - 1, 1 - core))
        receive(piece, 5, device(chip + 1, 1 - core))
        receive(piece, 6, device(chip + 2, 1 - core))

    for piece in range(min(3, pieces)):
        forward_x(piece)
    for piece in range(min(2, pieces)):
        forward_sibling(piece)
    arrived(0)

    def one_chunk(k, carry):
        @pl.when(k + 3 < pieces)
        def _():
            forward_x(k + 3)

        @pl.when(k + 2 < pieces)
        def _():
            forward_sibling(k + 2)

        arrived(k + 1)
        base = k * step
        for l in range(leads):
            gain = 1.0 + scale_ref[l]
            shift = shift_ref[l]
            for j in range(step + 2):
                row = base + j
                keep = ((row > 0) | (lat > 0)) & ((row < halo_rows - 1) | (lat < last_lat))
                value = band_ref[row].astype(jnp.float32) * gain + shift
                value = jnp.where(keep, value, 0.0)
                mod_ref[l, j] = value.astype(jnp.bfloat16)
            for j in range(step):
                stacked = jnp.concatenate([mod_ref[l, j + t] for t in range(3)], axis=-1)
                taps = jnp.dot(stacked, w_ref[...], preferred_element_type=jnp.float32)
                conv = (
                    pltpu.roll(taps[:, :width], 1, 0)
                    + taps[:, width : 2 * width]
                    + pltpu.roll(taps[:, 2 * width :], cols - 1, 0)
                )
                at = (l * step + j) * width
                hidden_ref[:, at : at + width] = jax.nn.gelu(conv).astype(jnp.bfloat16)
        mixed = jnp.dot(mix_ref[...], hidden_ref[...], preferred_element_type=jnp.float32)
        for l in range(leads):
            for j in range(step):
                at = (l * step + j) * width
                own = mod_ref[l, j + 1].astype(jnp.float32)
                out_ref[l, base + j] = (own + mixed[:, at : at + width]).astype(out_ref.dtype)
        return carry

    lax.fori_loop(0, pieces - 1, one_chunk, 0)

    for piece in range(pieces):
        for copy in sends(piece):
            copy.wait_send()


def head(tile, scales, shifts, w_all, zonal_mix, lon_devices):
    halo_rows, tile_cols, width = tile.shape
    rows = halo_rows - 2
    cols = tile_cols * lon_devices
    leads = scales.shape[0]
    pieces = halo_rows // HEAD_ROWS
    vmem = pl.BlockSpec(memory_space=pltpu.VMEM)
    return pl.pallas_call(
        head_kernel,
        out_shape=jax.ShapeDtypeStruct((leads, rows, cols, width), jnp.bfloat16),
        in_specs=[pl.BlockSpec(memory_space=pl.ANY), vmem, vmem, vmem, vmem],
        out_specs=vmem,
        scratch_shapes=[
            pltpu.VMEM((halo_rows, cols, width), jnp.bfloat16),
            pltpu.VMEM((leads, HEAD_ROWS + 2, cols, width), jnp.bfloat16),
            pltpu.VMEM((cols, leads * HEAD_ROWS * width), jnp.bfloat16),
            pltpu.SemaphoreType.DMA((pieces * 7,)),
            pltpu.SemaphoreType.DMA((pieces * 7,)),
            pltpu.SemaphoreType.DMA((pieces,)),
        ],
        compiler_params=pltpu.CompilerParams(
            collective_id=0, has_side_effects=True, vmem_limit_bytes=56 * 1024 * 1024
        ),
    )(tile, scales[:, None, :], shifts[:, None, :], w_all, zonal_mix)


def shards(inputs, w_enc, w_proj, film_scale, film_shift, lead_ids, w_head, zonal_mix):
    lat_rows, lon_cols, channels = inputs.shape
    with_rows = extended(inputs, (("lat", 0),), 1, False)
    padded = extended(with_rows, (("lon", 1),), 1, True)
    padded = jnp.pad(padded, ((0, 0), (0, 2), (0, 0)))
    tile = encoder(padded, w_enc, w_proj)
    head_width = w_proj.shape[1]
    lon_group = lax.axis_index("lon")
    my_rows = lax.dynamic_slice_in_dim(lead_ids, lon_group * LEAD_DEV, LEAD_DEV)
    tile = extended(tile, (("lat", 0),), 1, False)
    scales = jnp.take(film_scale, my_rows, axis=0)
    shifts = jnp.take(film_shift, my_rows, axis=0)
    w_all = jnp.transpose(w_head, (0, 2, 1, 3)).reshape(3 * head_width, 3 * head_width)
    return head(tile, scales, shifts, w_all, zonal_mix, lax.axis_size("lon"))

def solution(mesh):
    in_specs = (P("lat", "lon", None), P(), P(), P(), P(), P(), P(), P())
    out_specs = P("lon", "lat", None, None)
    return jax.shard_map(shards, mesh=mesh, in_specs=in_specs, out_specs=out_specs, check_vma=False)
```

```python
import functools

import jax
import jax.numpy as jnp
from jax import lax
from jax.experimental import pallas as pl
from jax.experimental.pallas import tpu as pltpu
from jax.sharding import PartitionSpec as P

LEAD_DEV = 2
HEAD_ROWS = 2
AHEAD = 1
MESH = pl.DeviceIdType.MESH


def extended(x, sides, width, wrap):
    for axis, dim in sides:
        devices, length = (lax.axis_size(axis), x.shape[dim])
        up = [(i, (i + 1) % devices) for i in range(devices if wrap else devices - 1)]
        down = [(j, i) for i, j in up]
        last = lax.slice_in_dim(x, length - width, length, axis=dim)
        initial = lax.slice_in_dim(x, 0, width, axis=dim)
        before = lax.ppermute(last, axis, up)
        after = lax.ppermute(initial, axis, down)
        x = jnp.concatenate([before, x, after], axis=dim)
    return x


def conv_three(padded, weight):
    batched = padded if padded.ndim == 4 else padded[None]
    result = lax.conv_general_dilated(
        batched,
        weight,
        (1, 1),
        "VALID",
        dimension_numbers=("NHWC", "HWIO", "NHWC"),
        preferred_element_type=jnp.float32,
    )
    return result if padded.ndim == 4 else result[0]


def pool_pairs(field):
    summed = lax.reduce_window(
        field, jnp.array(0, field.dtype), lax.add, (2, 2, 1), (2, 2, 1), "VALID"
    )
    return summed * 0.25


def encoder_kernel(x_ref, w_ref, proj_ref, out_ref, pair_ref):
    cols = x_ref.shape[1]
    width = x_ref.shape[2]
    pooled_cols = out_ref.shape[1]

    def encoded(row):
        stacked = jnp.concatenate([x_ref[row + k] for k in range(3)], axis=-1)
        taps = jnp.dot(stacked, w_ref[...], preferred_element_type=jnp.float32)
        conv = (
            taps[:, :width]
            + pltpu.roll(taps[:, width : 2 * width], cols - 1, 0)
            + pltpu.roll(taps[:, 2 * width :], cols - 2, 0)
        )
        return jax.nn.gelu(conv)

    def one_row(p, carry):
        pair = encoded(2 * p) + encoded(2 * p + 1)
        lanes = pair_ref.shape[2]
        chunks = []
        for c in range(width // lanes):
            pair_ref[c, pl.ds(0, cols)] = pair[:, c * lanes : (c + 1) * lanes]
            pair_ref[c, pl.ds(cols, 8)] = jnp.zeros((8, lanes), jnp.float32)
            half = pair_ref.shape[1] // 2
            chunks.append(
                pair_ref[c, pl.ds(0, half, stride=2)] + pair_ref[c, pl.ds(1, half, stride=2)]
            )
        summed = jnp.concatenate(chunks, axis=-1)
        pooled = (summed * 0.25).astype(jnp.bfloat16)
        projected = jnp.dot(pooled, proj_ref[...], preferred_element_type=jnp.float32)
        out_ref[p] = projected[:pooled_cols].astype(out_ref.dtype)
        return carry

    lax.fori_loop(0, out_ref.shape[0], one_row, 0)


def encoder(padded, w_enc, w_proj):
    rows, cols, width = padded.shape
    pooled_rows, pooled_cols = (rows - 2) // 2, (cols - 4) // 2
    w_all = jnp.transpose(w_enc, (0, 2, 1, 3)).reshape(3 * width, 3 * width)
    vmem = pl.BlockSpec(memory_space=pltpu.VMEM)
    return pl.pallas_call(
        encoder_kernel,
        out_shape=jax.ShapeDtypeStruct((pooled_rows, pooled_cols, w_proj.shape[1]), jnp.bfloat16),
        in_specs=[vmem, vmem, vmem],
        out_specs=vmem,
        scratch_shapes=[pltpu.VMEM((width // 128, cols + 8, 128), jnp.float32)],
        compiler_params=pltpu.CompilerParams(vmem_limit_bytes=48 * 1024 * 1024),
    )(padded, w_all, w_proj)


def head_kernel(tile_ref, scale_ref, shift_ref, w_ref, mix_ref, out_ref, band_ref, mod_ref,
                hidden_ref, send_sem, recv_sem, local_sem):
    me = lax.axis_index("lon")
    n = lax.axis_size("lon")
    lat = lax.axis_index("lat")
    last_lat = lax.axis_size("lat") - 1
    halo_rows, tile_cols, width = tile_ref.shape
    cols = band_ref.shape[1]
    leads = out_ref.shape[0]
    step = HEAD_ROWS
    pieces = halo_rows // step

    chips = n // 2
    chip = me // 2
    core = me % 2
    sense = 1 - 2 * core
    kinds = 7

    def device(at_chip, at_core):
        return 2 * lax.rem(at_chip + 2 * chips, chips) + at_core

    sibling = device(chip, 1 - core)
    east = device(chip + 1, core)
    west = device(chip - 1, core)
    far = device(chip + 2, core)
    behind = device(chip - sense, core)
    ahead = device(chip + sense, core)

    barrier = pltpu.get_barrier_semaphore()
    for peer in (sibling, east, west):
        pl.semaphore_signal(barrier, inc=1, device_id=(lat, peer), device_id_type=MESH)
    pl.semaphore_wait(barrier, 3)

    def slot(piece, source):
        start = pl.multiple_of(piece * step, step)
        return band_ref.at[pl.ds(start, step), pl.ds(source * tile_cols, tile_cols)]

    def source_rows(piece):
        return tile_ref.at[pl.ds(pl.multiple_of(piece * step, step), step)]

    def local_copy(piece):
        return pltpu.make_async_copy(source_rows(piece), slot(piece, me), local_sem.at[piece])

    def transfer(piece, kind, origin, target, own=False):
        return pltpu.make_async_remote_copy(
            src_ref=source_rows(piece) if own else slot(piece, origin),
            dst_ref=slot(piece, origin),
            send_sem=send_sem.at[piece * kinds + kind],
            recv_sem=recv_sem.at[piece * kinds + kind],
            device_id=(lat, target),
            device_id_type=MESH,
        )

    def sends(piece):
        return [
            transfer(piece, 0, me, sibling, own=True),
            transfer(piece, 1, me, east, own=True),
            transfer(piece, 2, me, west, own=True),
            transfer(piece, 3, behind, ahead),
            transfer(piece, 4, west, sibling),
            transfer(piece, 5, east, sibling),
            transfer(piece, 6, far, sibling),
        ]

    def receive(piece, kind, origin):
        transfer(piece, kind, origin, me).wait_recv()

    def direct(piece):
        local_copy(piece).start()
        for copy in sends(piece)[:3]:
            copy.start()

    def forward_x(piece):
        receive(piece, 1 + core, behind)
        sends(piece)[3].start()

    def forward_sibling(piece):
        receive(piece, 2 - core, ahead)
        receive(piece, 3, far)
        for copy in sends(piece)[4:]:
            copy.start()

    def arrived(piece):
        local_copy(piece).wait()
        receive(piece, 0, sibling)
        receive(piece, 4, device(chip - 1, 1 - core))
        receive(piece, 5, device(chip + 1, 1 - core))
        receive(piece, 6, device(chip + 2, 1 - core))

    for piece in range(min(AHEAD + 3, pieces)):
        direct(piece)
    for piece in range(min(3, pieces)):
        forward_x(piece)
    for piece in range(min(2, pieces)):
        forward_sibling(piece)
    arrived(0)

    def one_chunk(k, carry):
        @pl.when(k + AHEAD + 3 < pieces)
        def _():
            direct(k + AHEAD + 3)

        @pl.when(k + 3 < pieces)
        def _():
            forward_x(k + 3)

        @pl.when(k + 2 < pieces)
        def _():
            forward_sibling(k + 2)

        arrived(k + 1)
        base = k * step
        for l in range(leads):
            gain = 1.0 + scale_ref[l]
            shift = shift_ref[l]
            for j in range(step + 2):
                row = base + j
                keep = ((row > 0) | (lat > 0)) & ((row < halo_rows - 1) | (lat < last_lat))
                value = band_ref[row].astype(jnp.float32) * gain + shift
                value = jnp.where(keep, value, 0.0)
                mod_ref[l, j] = value.astype(jnp.bfloat16)
            for j in range(step):
                stacked = jnp.concatenate([mod_ref[l, j + t] for t in range(3)], axis=-1)
                taps = jnp.dot(stacked, w_ref[...], preferred_element_type=jnp.float32)
                conv = (
                    pltpu.roll(taps[:, :width], 1, 0)
                    + taps[:, width : 2 * width]
                    + pltpu.roll(taps[:, 2 * width :], cols - 1, 0)
                )
                at = (l * step + j) * width
                hidden_ref[:, at : at + width] = jax.nn.gelu(conv).astype(jnp.bfloat16)
        mixed = jnp.dot(mix_ref[...], hidden_ref[...], preferred_element_type=jnp.float32)
        for l in range(leads):
            for j in range(step):
                at = (l * step + j) * width
                own = mod_ref[l, j + 1].astype(jnp.float32)
                out_ref[l, base + j] = (own + mixed[:, at : at + width]).astype(out_ref.dtype)
        return carry

    lax.fori_loop(0, pieces - 1, one_chunk, 0)

    for piece in range(pieces):
        for copy in sends(piece):
            copy.wait_send()


def head(tile, scales, shifts, w_all, zonal_mix, lon_devices):
    halo_rows, tile_cols, width = tile.shape
    rows = halo_rows - 2
    cols = tile_cols * lon_devices
    leads = scales.shape[0]
    pieces = halo_rows // HEAD_ROWS
    vmem = pl.BlockSpec(memory_space=pltpu.VMEM)
    return pl.pallas_call(
        head_kernel,
        out_shape=jax.ShapeDtypeStruct((leads, rows, cols, width), jnp.bfloat16),
        in_specs=[pl.BlockSpec(memory_space=pl.ANY), vmem, vmem, vmem, vmem],
        out_specs=vmem,
        scratch_shapes=[
            pltpu.VMEM((halo_rows, cols, width), jnp.bfloat16),
            pltpu.VMEM((leads, HEAD_ROWS + 2, cols, width), jnp.bfloat16),
            pltpu.VMEM((cols, leads * HEAD_ROWS * width), jnp.bfloat16),
            pltpu.SemaphoreType.DMA((pieces * 7,)),
            pltpu.SemaphoreType.DMA((pieces * 7,)),
            pltpu.SemaphoreType.DMA((pieces,)),
        ],
        compiler_params=pltpu.CompilerParams(
            collective_id=0, has_side_effects=True, vmem_limit_bytes=56 * 1024 * 1024
        ),
    )(tile, scales[:, None, :], shifts[:, None, :], w_all, zonal_mix)


def shards(inputs, w_enc, w_proj, film_scale, film_shift, lead_ids, w_head, zonal_mix):
    lat_rows, lon_cols, channels = inputs.shape
    with_rows = extended(inputs, (("lat", 0),), 1, False)
    padded = extended(with_rows, (("lon", 1),), 1, True)
    padded = jnp.pad(padded, ((0, 0), (0, 2), (0, 0)))
    tile = encoder(padded, w_enc, w_proj)
    head_width = w_proj.shape[1]
    lon_group = lax.axis_index("lon")
    my_rows = lax.dynamic_slice_in_dim(lead_ids, lon_group * LEAD_DEV, LEAD_DEV)
    tile = extended(tile, (("lat", 0),), 1, False)
    scales = jnp.take(film_scale, my_rows, axis=0)
    shifts = jnp.take(film_shift, my_rows, axis=0)
    w_all = jnp.transpose(w_head, (0, 2, 1, 3)).reshape(3 * head_width, 3 * head_width)
    return head(tile, scales, shifts, w_all, zonal_mix, lax.axis_size("lon"))

def solution(mesh):
    in_specs = (P("lat", "lon", None), P(), P(), P(), P(), P(), P(), P())
    out_specs = P("lon", "lat", None, None)
    return jax.shard_map(shards, mesh=mesh, in_specs=in_specs, out_specs=out_specs, check_vma=False)
```

```python
import functools

import jax
import jax.numpy as jnp
from jax import lax
from jax.experimental import pallas as pl
from jax.experimental.pallas import tpu as pltpu
from jax.sharding import PartitionSpec as P

LEAD_DEV = 2
HEAD_ROWS = 2
AHEAD = 1
MESH = pl.DeviceIdType.MESH


def extended(x, sides, width, wrap):
    for axis, dim in sides:
        devices, length = (lax.axis_size(axis), x.shape[dim])
        up = [(i, (i + 1) % devices) for i in range(devices if wrap else devices - 1)]
        down = [(j, i) for i, j in up]
        last = lax.slice_in_dim(x, length - width, length, axis=dim)
        initial = lax.slice_in_dim(x, 0, width, axis=dim)
        before = lax.ppermute(last, axis, up)
        after = lax.ppermute(initial, axis, down)
        x = jnp.concatenate([before, x, after], axis=dim)
    return x


def conv_three(padded, weight):
    batched = padded if padded.ndim == 4 else padded[None]
    result = lax.conv_general_dilated(
        batched,
        weight,
        (1, 1),
        "VALID",
        dimension_numbers=("NHWC", "HWIO", "NHWC"),
        preferred_element_type=jnp.float32,
    )
    return result if padded.ndim == 4 else result[0]


def pool_pairs(field):
    summed = lax.reduce_window(
        field, jnp.array(0, field.dtype), lax.add, (2, 2, 1), (2, 2, 1), "VALID"
    )
    return summed * 0.25


def encoder_kernel(x_hbm, w_ref, proj_ref, out_ref, xpad, pair_ref, local_sem, send_sem, recv_sem):
    lat = lax.axis_index("lat")
    lon = lax.axis_index("lon")
    lats = lax.axis_size("lat")
    lons = lax.axis_size("lon")
    has_up = lat > 0
    has_down = lat < lats - 1
    up, down = lat - 1, lat + 1
    left, right = lax.rem(lon + lons - 1, lons), lax.rem(lon + 1, lons)
    rows, tile_cols, width = x_hbm.shape
    cols = xpad.shape[2]
    pooled_rows, pooled_cols = rows // 2, tile_cols // 2

    barrier = pltpu.get_barrier_semaphore()

    @pl.when(has_up)
    def _():
        pl.semaphore_signal(barrier, inc=1, device_id=(up, lon), device_id_type=MESH)

    @pl.when(has_down)
    def _():
        pl.semaphore_signal(barrier, inc=1, device_id=(down, lon), device_id_type=MESH)

    for peer in (left, right):
        pl.semaphore_signal(barrier, inc=1, device_id=(lat, peer), device_id_type=MESH)
    pl.semaphore_wait(barrier, 2 + has_up.astype(jnp.int32) + has_down.astype(jnp.int32))

    def remote(kind, src, dst, target):
        return pltpu.make_async_remote_copy(
            src_ref=src, dst_ref=dst, send_sem=send_sem.at[kind], recv_sem=recv_sem.at[kind],
            device_id=target, device_id_type=MESH,
        )

    halves = xpad.shape[1]
    lanes = xpad.shape[3]
    inner = pl.ds(0, tile_cols)
    locals_ = []
    to_up, to_down = [], []
    for h in range(halves):
        part = pl.ds(h * lanes, lanes)
        locals_.append(
            pltpu.make_async_copy(x_hbm.at[:, :, part], xpad.at[pl.ds(1, rows), h, inner], local_sem.at[h])
        )
        to_up.append(remote(h, x_hbm.at[0, :, part], xpad.at[rows + 1, h, inner], (up, lon)))
        to_down.append(remote(2 + h, x_hbm.at[rows - 1, :, part], xpad.at[0, h, inner], (down, lon)))
    for h in range(halves):
        locals_[h].start()
        pl.when(has_up)(to_up[h].start)
        pl.when(has_down)(to_down[h].start)

    def zero_edges(first, count):
        span = pl.ds(first, count)

        @pl.when(lat == 0)
        def _():
            xpad[0, :, span] = jnp.zeros((halves, count, lanes), xpad.dtype)

        @pl.when(lat == lats - 1)
        def _():
            xpad[rows + 1, :, span] = jnp.zeros((halves, count, lanes), xpad.dtype)

    for h in range(halves):
        locals_[h].wait()
        pl.when(has_down)(to_up[h].wait_recv)
        pl.when(has_up)(to_down[h].wait_recv)
    zero_edges(0, tile_cols)
    to_left, to_right = [], []
    for h in range(halves):
        pair_cols = pl.ds(0, 2)
        to_left.append(
            remote(4 + h, xpad.at[:, h, pair_cols], xpad.at[:, h, pl.ds(tile_cols, 2)], (lat, left))
        )
        to_right.append(
            remote(
                6 + h,
                xpad.at[:, h, pl.ds(tile_cols - 2, 2)],
                xpad.at[:, h, pl.ds(cols - 2, 2)],
                (lat, right),
            )
        )
    for h in range(halves):
        to_left[h].start()
        to_right[h].start()
    for h in range(halves):
        to_left[h].wait_recv()
        to_right[h].wait_recv()
    zero_edges(tile_cols, cols - tile_cols)

    def encoded(row):
        stacked = jnp.concatenate(
            [xpad[row + k, h] for k in range(3) for h in range(halves)], axis=-1
        )
        taps = jnp.dot(stacked, w_ref[...], preferred_element_type=jnp.float32)
        conv = (
            pltpu.roll(taps[:, :width], 1, 0)
            + taps[:, width : 2 * width]
            + pltpu.roll(taps[:, 2 * width :], cols - 1, 0)
        )
        return jax.nn.gelu(conv)

    def pooled_row(p):
        pair = encoded(2 * p) + encoded(2 * p + 1)
        lanes = pair_ref.shape[2]
        chunks = []
        for c in range(width // lanes):
            pair_ref[c, pl.ds(0, cols)] = pair[:, c * lanes : (c + 1) * lanes]
            pair_ref[c, pl.ds(cols, 8)] = jnp.zeros((8, lanes), jnp.float32)
            half = pair_ref.shape[1] // 2
            chunks.append(
                pair_ref[c, pl.ds(0, half, stride=2)] + pair_ref[c, pl.ds(1, half, stride=2)]
            )
        summed = jnp.concatenate(chunks, axis=-1)
        pooled = (summed * 0.25).astype(jnp.bfloat16)
        projected = jnp.dot(pooled, proj_ref[...], preferred_element_type=jnp.float32)
        out_ref[p + 1] = projected[:pooled_cols].astype(out_ref.dtype)

    pooled_row(0)
    edge_up = remote(8, out_ref.at[1], out_ref.at[pooled_rows + 1], (up, lon))
    pl.when(has_up)(edge_up.start)
    pooled_row(pooled_rows - 1)
    edge_down = remote(9, out_ref.at[pooled_rows], out_ref.at[0], (down, lon))
    pl.when(has_down)(edge_down.start)

    def one_row(p, carry):
        pooled_row(p)
        return carry

    lax.fori_loop(1, pooled_rows - 1, one_row, 0)
    pl.when(has_down)(edge_up.wait_recv)
    pl.when(has_up)(edge_down.wait_recv)

    @pl.when(lat == 0)
    def _():
        out_ref[0] = jnp.zeros(out_ref.shape[1:], out_ref.dtype)

    @pl.when(lat == lats - 1)
    def _():
        out_ref[pooled_rows + 1] = jnp.zeros(out_ref.shape[1:], out_ref.dtype)

    for h in range(halves):
        pl.when(has_up)(to_up[h].wait_send)
        pl.when(has_down)(to_down[h].wait_send)
        to_left[h].wait_send()
        to_right[h].wait_send()
    pl.when(has_up)(edge_up.wait_send)
    pl.when(has_down)(edge_down.wait_send)


def encoder(tile, w_enc, w_proj):
    rows, tile_cols, width = tile.shape
    cols = tile_cols + 4
    w_all = jnp.transpose(w_enc, (0, 2, 1, 3)).reshape(3 * width, 3 * width)
    vmem = pl.BlockSpec(memory_space=pltpu.VMEM)
    return pl.pallas_call(
        encoder_kernel,
        out_shape=jax.ShapeDtypeStruct((rows // 2 + 2, tile_cols // 2, w_proj.shape[1]), jnp.bfloat16),
        in_specs=[pl.BlockSpec(memory_space=pl.ANY), vmem, vmem],
        out_specs=vmem,
        scratch_shapes=[
            pltpu.VMEM((rows + 2, width // 128, cols, 128), jnp.bfloat16),
            pltpu.VMEM((width // 128, cols + 8, 128), jnp.float32),
            pltpu.SemaphoreType.DMA((width // 128,)),
            pltpu.SemaphoreType.DMA((10,)),
            pltpu.SemaphoreType.DMA((10,)),
        ],
        compiler_params=pltpu.CompilerParams(
            collective_id=1, has_side_effects=True, vmem_limit_bytes=48 * 1024 * 1024
        ),
    )(tile, w_all, w_proj)


def head_kernel(tile_ref, scale_ref, shift_ref, w_ref, mix_ref, out_ref, band_ref, mod_ref,
                hidden_ref, send_sem, recv_sem, local_sem):
    me = lax.axis_index("lon")
    n = lax.axis_size("lon")
    lat = lax.axis_index("lat")
    last_lat = lax.axis_size("lat") - 1
    halo_rows, tile_cols, width = tile_ref.shape
    cols = band_ref.shape[1]
    leads = out_ref.shape[0]
    step = HEAD_ROWS
    pieces = halo_rows // step

    chips = n // 2
    chip = me // 2
    core = me % 2
    sense = 1 - 2 * core
    kinds = 7

    def device(at_chip, at_core):
        return 2 * lax.rem(at_chip + 2 * chips, chips) + at_core

    sibling = device(chip, 1 - core)
    east = device(chip + 1, core)
    west = device(chip - 1, core)
    far = device(chip + 2, core)
    behind = device(chip - sense, core)
    ahead = device(chip + sense, core)

    barrier = pltpu.get_barrier_semaphore()
    for peer in (sibling, east, west):
        pl.semaphore_signal(barrier, inc=1, device_id=(lat, peer), device_id_type=MESH)
    pl.semaphore_wait(barrier, 3)

    def slot(piece, source):
        start = pl.multiple_of(piece * step, step)
        return band_ref.at[pl.ds(start, step), pl.ds(source * tile_cols, tile_cols)]

    def source_rows(piece):
        return tile_ref.at[pl.ds(pl.multiple_of(piece * step, step), step)]

    def local_copy(piece):
        return pltpu.make_async_copy(source_rows(piece), slot(piece, me), local_sem.at[piece])

    def transfer(piece, kind, origin, target, own=False):
        return pltpu.make_async_remote_copy(
            src_ref=source_rows(piece) if own else slot(piece, origin),
            dst_ref=slot(piece, origin),
            send_sem=send_sem.at[piece * kinds + kind],
            recv_sem=recv_sem.at[piece * kinds + kind],
            device_id=(lat, target),
            device_id_type=MESH,
        )

    def sends(piece):
        return [
            transfer(piece, 0, me, sibling, own=True),
            transfer(piece, 1, me, east, own=True),
            transfer(piece, 2, me, west, own=True),
            transfer(piece, 3, behind, ahead),
            transfer(piece, 4, west, sibling),
            transfer(piece, 5, east, sibling),
            transfer(piece, 6, far, sibling),
        ]

    def receive(piece, kind, origin):
        transfer(piece, kind, origin, me).wait_recv()

    def direct(piece):
        local_copy(piece).start()
        for copy in sends(piece)[:3]:
            copy.start()

    def forward_x(piece):
        receive(piece, 1 + core, behind)
        sends(piece)[3].start()

    def forward_sibling(piece):
        receive(piece, 2 - core, ahead)
        receive(piece, 3, far)
        for copy in sends(piece)[4:]:
            copy.start()

    def arrived(piece):
        local_copy(piece).wait()
        receive(piece, 0, sibling)
        receive(piece, 4, device(chip - 1, 1 - core))
        receive(piece, 5, device(chip + 1, 1 - core))
        receive(piece, 6, device(chip + 2, 1 - core))

    for piece in range(min(AHEAD + 3, pieces)):
        direct(piece)
    for piece in range(min(3, pieces)):
        forward_x(piece)
    for piece in range(min(2, pieces)):
        forward_sibling(piece)
    arrived(0)

    def one_chunk(k, carry):
        @pl.when(k + AHEAD + 3 < pieces)
        def _():
            direct(k + AHEAD + 3)

        @pl.when(k + 3 < pieces)
        def _():
            forward_x(k + 3)

        @pl.when(k + 2 < pieces)
        def _():
            forward_sibling(k + 2)

        arrived(k + 1)
        base = k * step
        for l in range(leads):
            gain = 1.0 + scale_ref[l]
            shift = shift_ref[l]
            for j in range(step + 2):
                row = base + j
                keep = ((row > 0) | (lat > 0)) & ((row < halo_rows - 1) | (lat < last_lat))
                value = band_ref[row].astype(jnp.float32) * gain + shift
                value = jnp.where(keep, value, 0.0)
                mod_ref[l, j] = value.astype(jnp.bfloat16)
            for j in range(step):
                stacked = jnp.concatenate([mod_ref[l, j + t] for t in range(3)], axis=-1)
                taps = jnp.dot(stacked, w_ref[...], preferred_element_type=jnp.float32)
                conv = (
                    pltpu.roll(taps[:, :width], 1, 0)
                    + taps[:, width : 2 * width]
                    + pltpu.roll(taps[:, 2 * width :], cols - 1, 0)
                )
                at = (l * step + j) * width
                hidden_ref[:, at : at + width] = jax.nn.gelu(conv).astype(jnp.bfloat16)
        mixed = jnp.dot(mix_ref[...], hidden_ref[...], preferred_element_type=jnp.float32)
        for l in range(leads):
            for j in range(step):
                at = (l * step + j) * width
                own = mod_ref[l, j + 1].astype(jnp.float32)
                out_ref[l, base + j] = (own + mixed[:, at : at + width]).astype(out_ref.dtype)
        return carry

    lax.fori_loop(0, pieces - 1, one_chunk, 0)

    for piece in range(pieces):
        for copy in sends(piece):
            copy.wait_send()


def head(tile, scales, shifts, w_all, zonal_mix, lon_devices):
    halo_rows, tile_cols, width = tile.shape
    rows = halo_rows - 2
    cols = tile_cols * lon_devices
    leads = scales.shape[0]
    pieces = halo_rows // HEAD_ROWS
    vmem = pl.BlockSpec(memory_space=pltpu.VMEM)
    return pl.pallas_call(
        head_kernel,
        out_shape=jax.ShapeDtypeStruct((leads, rows, cols, width), jnp.bfloat16),
        in_specs=[pl.BlockSpec(memory_space=pl.ANY), vmem, vmem, vmem, vmem],
        out_specs=vmem,
        scratch_shapes=[
            pltpu.VMEM((halo_rows, cols, width), jnp.bfloat16),
            pltpu.VMEM((leads, HEAD_ROWS + 2, cols, width), jnp.bfloat16),
            pltpu.VMEM((cols, leads * HEAD_ROWS * width), jnp.bfloat16),
            pltpu.SemaphoreType.DMA((pieces * 7,)),
            pltpu.SemaphoreType.DMA((pieces * 7,)),
            pltpu.SemaphoreType.DMA((pieces,)),
        ],
        compiler_params=pltpu.CompilerParams(
            collective_id=0, has_side_effects=True, vmem_limit_bytes=56 * 1024 * 1024
        ),
    )(tile, scales[:, None, :], shifts[:, None, :], w_all, zonal_mix)


def shards(inputs, w_enc, w_proj, film_scale, film_shift, lead_ids, w_head, zonal_mix):
    lat_rows, lon_cols, channels = inputs.shape
    tile = encoder(inputs, w_enc, w_proj)
    head_width = w_proj.shape[1]
    lon_group = lax.axis_index("lon")
    my_rows = lax.dynamic_slice_in_dim(lead_ids, lon_group * LEAD_DEV, LEAD_DEV)
    scales = jnp.take(film_scale, my_rows, axis=0)
    shifts = jnp.take(film_shift, my_rows, axis=0)
    w_all = jnp.transpose(w_head, (0, 2, 1, 3)).reshape(3 * head_width, 3 * head_width)
    return head(tile, scales, shifts, w_all, zonal_mix, lax.axis_size("lon"))

def solution(mesh):
    in_specs = (P("lat", "lon", None), P(), P(), P(), P(), P(), P(), P())
    out_specs = P("lon", "lat", None, None)
    return jax.shard_map(shards, mesh=mesh, in_specs=in_specs, out_specs=out_specs, check_vma=False)
```

```python
import functools

import jax
import jax.numpy as jnp
from jax import lax
from jax.experimental import pallas as pl
from jax.experimental.pallas import tpu as pltpu
from jax.sharding import PartitionSpec as P

LEAD_DEV = 2
HEAD_ROWS = 2
AHEAD = 1
MESH = pl.DeviceIdType.MESH


def extended(x, sides, width, wrap):
    for axis, dim in sides:
        devices, length = (lax.axis_size(axis), x.shape[dim])
        up = [(i, (i + 1) % devices) for i in range(devices if wrap else devices - 1)]
        down = [(j, i) for i, j in up]
        last = lax.slice_in_dim(x, length - width, length, axis=dim)
        initial = lax.slice_in_dim(x, 0, width, axis=dim)
        before = lax.ppermute(last, axis, up)
        after = lax.ppermute(initial, axis, down)
        x = jnp.concatenate([before, x, after], axis=dim)
    return x


def conv_three(padded, weight):
    batched = padded if padded.ndim == 4 else padded[None]
    result = lax.conv_general_dilated(
        batched,
        weight,
        (1, 1),
        "VALID",
        dimension_numbers=("NHWC", "HWIO", "NHWC"),
        preferred_element_type=jnp.float32,
    )
    return result if padded.ndim == 4 else result[0]


def pool_pairs(field):
    summed = lax.reduce_window(
        field, jnp.array(0, field.dtype), lax.add, (2, 2, 1), (2, 2, 1), "VALID"
    )
    return summed * 0.25


def encoder_kernel(x_hbm, w_in, proj_ref, out_ref, xpad, pair_ref, w_ref, local_sem, send_sem, recv_sem):
    lat = lax.axis_index("lat")
    lon = lax.axis_index("lon")
    lats = lax.axis_size("lat")
    lons = lax.axis_size("lon")
    has_up = lat > 0
    has_down = lat < lats - 1
    up, down = lat - 1, lat + 1
    left, right = lax.rem(lon + lons - 1, lons), lax.rem(lon + 1, lons)
    rows, tile_cols, width = x_hbm.shape
    cols = xpad.shape[2]
    pooled_rows, pooled_cols = rows // 2, tile_cols // 2

    barrier = pltpu.get_barrier_semaphore()

    @pl.when(has_up)
    def _():
        pl.semaphore_signal(barrier, inc=1, device_id=(up, lon), device_id_type=MESH)

    @pl.when(has_down)
    def _():
        pl.semaphore_signal(barrier, inc=1, device_id=(down, lon), device_id_type=MESH)

    for peer in (left, right):
        pl.semaphore_signal(barrier, inc=1, device_id=(lat, peer), device_id_type=MESH)
    pl.semaphore_wait(barrier, 2 + has_up.astype(jnp.int32) + has_down.astype(jnp.int32))

    def remote(kind, src, dst, target):
        return pltpu.make_async_remote_copy(
            src_ref=src, dst_ref=dst, send_sem=send_sem.at[kind], recv_sem=recv_sem.at[kind],
            device_id=target, device_id_type=MESH,
        )

    halves = xpad.shape[1]
    lanes = xpad.shape[3]
    inner = pl.ds(0, tile_cols)
    locals_ = []
    to_up, to_down = [], []
    for h in range(halves):
        part = pl.ds(h * lanes, lanes)
        locals_.append(
            pltpu.make_async_copy(x_hbm.at[:, :, part], xpad.at[pl.ds(1, rows), h, inner], local_sem.at[h])
        )
        to_up.append(remote(h, x_hbm.at[0, :, part], xpad.at[rows + 1, h, inner], (up, lon)))
        to_down.append(remote(2 + h, x_hbm.at[rows - 1, :, part], xpad.at[0, h, inner], (down, lon)))
    for h in range(halves):
        locals_[h].start()
        pl.when(has_up)(to_up[h].start)
        pl.when(has_down)(to_down[h].start)

    def zero_edges(first, count):
        span = pl.ds(first, count)

        @pl.when(lat == 0)
        def _():
            xpad[0, :, span] = jnp.zeros((halves, count, lanes), xpad.dtype)

        @pl.when(lat == lats - 1)
        def _():
            xpad[rows + 1, :, span] = jnp.zeros((halves, count, lanes), xpad.dtype)

    taps_n = w_in.shape[0]
    for di in range(taps_n):
        for dj in range(taps_n):
            w_ref[di * width : (di + 1) * width, dj * width : (dj + 1) * width] = w_in[di, dj]
    for h in range(halves):
        locals_[h].wait()
        pl.when(has_down)(to_up[h].wait_recv)
        pl.when(has_up)(to_down[h].wait_recv)
    zero_edges(0, tile_cols)
    to_left, to_right = [], []
    for h in range(halves):
        pair_cols = pl.ds(0, 2)
        to_left.append(
            remote(4 + h, xpad.at[:, h, pair_cols], xpad.at[:, h, pl.ds(tile_cols, 2)], (lat, left))
        )
        to_right.append(
            remote(
                6 + h,
                xpad.at[:, h, pl.ds(tile_cols - 2, 2)],
                xpad.at[:, h, pl.ds(cols - 2, 2)],
                (lat, right),
            )
        )
    for h in range(halves):
        to_left[h].start()
        to_right[h].start()
    for h in range(halves):
        to_left[h].wait_recv()
        to_right[h].wait_recv()
    zero_edges(tile_cols, cols - tile_cols)

    def encoded(row):
        stacked = jnp.concatenate(
            [xpad[row + k, h] for k in range(3) for h in range(halves)], axis=-1
        )
        taps = jnp.dot(stacked, w_ref[...], preferred_element_type=jnp.float32)
        conv = (
            pltpu.roll(taps[:, :width], 1, 0)
            + taps[:, width : 2 * width]
            + pltpu.roll(taps[:, 2 * width :], cols - 1, 0)
        )
        return jax.nn.gelu(conv)

    def pooled_row(p):
        pair = encoded(2 * p) + encoded(2 * p + 1)
        lanes = pair_ref.shape[2]
        chunks = []
        for c in range(width // lanes):
            pair_ref[c, pl.ds(0, cols)] = pair[:, c * lanes : (c + 1) * lanes]
            pair_ref[c, pl.ds(cols, 8)] = jnp.zeros((8, lanes), jnp.float32)
            half = pair_ref.shape[1] // 2
            chunks.append(
                pair_ref[c, pl.ds(0, half, stride=2)] + pair_ref[c, pl.ds(1, half, stride=2)]
            )
        summed = jnp.concatenate(chunks, axis=-1)
        pooled = (summed * 0.25).astype(jnp.bfloat16)
        projected = jnp.dot(pooled, proj_ref[...], preferred_element_type=jnp.float32)
        out_ref[p + 1] = projected[:pooled_cols].astype(out_ref.dtype)

    pooled_row(0)
    edge_up = remote(8, out_ref.at[1], out_ref.at[pooled_rows + 1], (up, lon))
    pl.when(has_up)(edge_up.start)
    pooled_row(pooled_rows - 1)
    edge_down = remote(9, out_ref.at[pooled_rows], out_ref.at[0], (down, lon))
    pl.when(has_down)(edge_down.start)

    def one_row(p, carry):
        pooled_row(p)
        return carry

    lax.fori_loop(1, pooled_rows - 1, one_row, 0)
    pl.when(has_down)(edge_up.wait_recv)
    pl.when(has_up)(edge_down.wait_recv)

    @pl.when(lat == 0)
    def _():
        out_ref[0] = jnp.zeros(out_ref.shape[1:], out_ref.dtype)

    @pl.when(lat == lats - 1)
    def _():
        out_ref[pooled_rows + 1] = jnp.zeros(out_ref.shape[1:], out_ref.dtype)

    for h in range(halves):
        pl.when(has_up)(to_up[h].wait_send)
        pl.when(has_down)(to_down[h].wait_send)
        to_left[h].wait_send()
        to_right[h].wait_send()
    pl.when(has_up)(edge_up.wait_send)
    pl.when(has_down)(edge_down.wait_send)


def encoder(tile, w_enc, w_proj):
    rows, tile_cols, width = tile.shape
    cols = tile_cols + 4
    vmem = pl.BlockSpec(memory_space=pltpu.VMEM)
    return pl.pallas_call(
        encoder_kernel,
        out_shape=jax.ShapeDtypeStruct((rows // 2 + 2, tile_cols // 2, w_proj.shape[1]), jnp.bfloat16),
        in_specs=[pl.BlockSpec(memory_space=pl.ANY), vmem, vmem],
        out_specs=vmem,
        scratch_shapes=[
            pltpu.VMEM((rows + 2, width // 128, cols, 128), jnp.bfloat16),
            pltpu.VMEM((width // 128, cols + 8, 128), jnp.float32),
            pltpu.VMEM((3 * width, 3 * width), jnp.bfloat16),
            pltpu.SemaphoreType.DMA((width // 128,)),
            pltpu.SemaphoreType.DMA((10,)),
            pltpu.SemaphoreType.DMA((10,)),
        ],
        compiler_params=pltpu.CompilerParams(
            collective_id=1, has_side_effects=True, vmem_limit_bytes=48 * 1024 * 1024
        ),
    )(tile, w_enc, w_proj)


def head_kernel(ids_ref, tile_ref, scale_ref, shift_ref, w_in, mix_ref, out_ref, band_ref, mod_ref,
                hidden_ref, w_ref, send_sem, recv_sem, local_sem):
    me = lax.axis_index("lon")
    n = lax.axis_size("lon")
    lat = lax.axis_index("lat")
    last_lat = lax.axis_size("lat") - 1
    halo_rows, tile_cols, width = tile_ref.shape
    cols = band_ref.shape[1]
    leads = out_ref.shape[0]
    step = HEAD_ROWS
    pieces = halo_rows // step

    chips = n // 2
    chip = me // 2
    core = me % 2
    sense = 1 - 2 * core
    kinds = 7

    def device(at_chip, at_core):
        return 2 * lax.rem(at_chip + 2 * chips, chips) + at_core

    sibling = device(chip, 1 - core)
    east = device(chip + 1, core)
    west = device(chip - 1, core)
    far = device(chip + 2, core)
    behind = device(chip - sense, core)
    ahead = device(chip + sense, core)

    barrier = pltpu.get_barrier_semaphore()
    for peer in (sibling, east, west):
        pl.semaphore_signal(barrier, inc=1, device_id=(lat, peer), device_id_type=MESH)
    pl.semaphore_wait(barrier, 3)

    def slot(piece, source):
        start = pl.multiple_of(piece * step, step)
        return band_ref.at[pl.ds(start, step), pl.ds(source * tile_cols, tile_cols)]

    def source_rows(piece):
        return tile_ref.at[pl.ds(pl.multiple_of(piece * step, step), step)]

    def local_copy(piece):
        return pltpu.make_async_copy(source_rows(piece), slot(piece, me), local_sem.at[piece])

    def transfer(piece, kind, origin, target, own=False):
        return pltpu.make_async_remote_copy(
            src_ref=source_rows(piece) if own else slot(piece, origin),
            dst_ref=slot(piece, origin),
            send_sem=send_sem.at[piece * kinds + kind],
            recv_sem=recv_sem.at[piece * kinds + kind],
            device_id=(lat, target),
            device_id_type=MESH,
        )

    def sends(piece):
        return [
            transfer(piece, 0, me, sibling, own=True),
            transfer(piece, 1, me, east, own=True),
            transfer(piece, 2, me, west, own=True),
            transfer(piece, 3, behind, ahead),
            transfer(piece, 4, west, sibling),
            transfer(piece, 5, east, sibling),
            transfer(piece, 6, far, sibling),
        ]

    def receive(piece, kind, origin):
        transfer(piece, kind, origin, me).wait_recv()

    def direct(piece):
        local_copy(piece).start()
        for copy in sends(piece)[:3]:
            copy.start()

    def forward_x(piece):
        receive(piece, 1 + core, behind)
        sends(piece)[3].start()

    def forward_sibling(piece):
        receive(piece, 2 - core, ahead)
        receive(piece, 3, far)
        for copy in sends(piece)[4:]:
            copy.start()

    def arrived(piece):
        local_copy(piece).wait()
        receive(piece, 0, sibling)
        receive(piece, 4, device(chip - 1, 1 - core))
        receive(piece, 5, device(chip + 1, 1 - core))
        receive(piece, 6, device(chip + 2, 1 - core))

    for piece in range(min(AHEAD + 3, pieces)):
        direct(piece)
    taps_n = w_in.shape[0]
    for di in range(taps_n):
        for dj in range(taps_n):
            w_ref[di * width : (di + 1) * width, dj * width : (dj + 1) * width] = w_in[di, dj]
    gains, shifts = [], []
    for l in range(leads):
        row = ids_ref[leads * me + l]
        gains.append(1.0 + scale_ref[pl.ds(row, 1), :])
        shifts.append(shift_ref[pl.ds(row, 1), :])
    for piece in range(min(3, pieces)):
        forward_x(piece)
    for piece in range(min(2, pieces)):
        forward_sibling(piece)
    arrived(0)

    def one_chunk(k, carry):
        @pl.when(k + AHEAD + 3 < pieces)
        def _():
            direct(k + AHEAD + 3)

        @pl.when(k + 3 < pieces)
        def _():
            forward_x(k + 3)

        @pl.when(k + 2 < pieces)
        def _():
            forward_sibling(k + 2)

        arrived(k + 1)
        base = k * step
        for l in range(leads):
            gain = gains[l]
            shift = shifts[l]
            for j in range(step + 2):
                row = base + j
                keep = ((row > 0) | (lat > 0)) & ((row < halo_rows - 1) | (lat < last_lat))
                value = band_ref[row].astype(jnp.float32) * gain + shift
                value = jnp.where(keep, value, 0.0)
                mod_ref[l, j] = value.astype(jnp.bfloat16)
            for j in range(step):
                stacked = jnp.concatenate([mod_ref[l, j + t] for t in range(3)], axis=-1)
                taps = jnp.dot(stacked, w_ref[...], preferred_element_type=jnp.float32)
                conv = (
                    pltpu.roll(taps[:, :width], 1, 0)
                    + taps[:, width : 2 * width]
                    + pltpu.roll(taps[:, 2 * width :], cols - 1, 0)
                )
                at = (l * step + j) * width
                hidden_ref[:, at : at + width] = jax.nn.gelu(conv).astype(jnp.bfloat16)
        mixed = jnp.dot(mix_ref[...], hidden_ref[...], preferred_element_type=jnp.float32)
        for l in range(leads):
            for j in range(step):
                at = (l * step + j) * width
                own = mod_ref[l, j + 1].astype(jnp.float32)
                out_ref[l, base + j] = (own + mixed[:, at : at + width]).astype(out_ref.dtype)
        return carry

    lax.fori_loop(0, pieces - 1, one_chunk, 0)

    for piece in range(pieces):
        for copy in sends(piece):
            copy.wait_send()


def head(lead_ids, tile, film_scale, film_shift, w_head, zonal_mix, lon_devices):
    halo_rows, tile_cols, width = tile.shape
    rows = halo_rows - 2
    cols = tile_cols * lon_devices
    leads = LEAD_DEV
    pieces = halo_rows // HEAD_ROWS
    vmem = pl.BlockSpec(memory_space=pltpu.VMEM)
    return pl.pallas_call(
        head_kernel,
        out_shape=jax.ShapeDtypeStruct((leads, rows, cols, width), jnp.bfloat16),
        in_specs=[pl.BlockSpec(memory_space=pltpu.SMEM), pl.BlockSpec(memory_space=pl.ANY), vmem, vmem, vmem, vmem],
        out_specs=vmem,
        scratch_shapes=[
            pltpu.VMEM((halo_rows, cols, width), jnp.bfloat16),
            pltpu.VMEM((leads, HEAD_ROWS + 2, cols, width), jnp.bfloat16),
            pltpu.VMEM((cols, leads * HEAD_ROWS * width), jnp.bfloat16),
            pltpu.VMEM((3 * width, 3 * width), jnp.bfloat16),
            pltpu.SemaphoreType.DMA((pieces * 7,)),
            pltpu.SemaphoreType.DMA((pieces * 7,)),
            pltpu.SemaphoreType.DMA((pieces,)),
        ],
        compiler_params=pltpu.CompilerParams(
            collective_id=0, has_side_effects=True, vmem_limit_bytes=56 * 1024 * 1024
        ),
    )(lead_ids, tile, film_scale, film_shift, w_head, zonal_mix)


def shards(inputs, w_enc, w_proj, film_scale, film_shift, lead_ids, w_head, zonal_mix):
    lat_rows, lon_cols, channels = inputs.shape
    tile = encoder(inputs, w_enc, w_proj)
    return head(lead_ids, tile, film_scale, film_shift, w_head, zonal_mix, lax.axis_size("lon"))

def solution(mesh):
    in_specs = (P("lat", "lon", None), P(), P(), P(), P(), P(), P(), P())
    out_specs = P("lon", "lat", None, None)
    return jax.shard_map(shards, mesh=mesh, in_specs=in_specs, out_specs=out_specs, check_vma=False)
```

```python
import functools

import jax
import jax.numpy as jnp
from jax import lax
from jax.experimental import pallas as pl
from jax.experimental.pallas import tpu as pltpu
from jax.sharding import PartitionSpec as P

LEAD_DEV = 2
HEAD_ROWS = 2
AHEAD = 1
VMEM_ALL = 67043328
MESH = pl.DeviceIdType.MESH


def extended(x, sides, width, wrap):
    for axis, dim in sides:
        devices, length = (lax.axis_size(axis), x.shape[dim])
        up = [(i, (i + 1) % devices) for i in range(devices if wrap else devices - 1)]
        down = [(j, i) for i, j in up]
        last = lax.slice_in_dim(x, length - width, length, axis=dim)
        initial = lax.slice_in_dim(x, 0, width, axis=dim)
        before = lax.ppermute(last, axis, up)
        after = lax.ppermute(initial, axis, down)
        x = jnp.concatenate([before, x, after], axis=dim)
    return x


def conv_three(padded, weight):
    batched = padded if padded.ndim == 4 else padded[None]
    result = lax.conv_general_dilated(
        batched,
        weight,
        (1, 1),
        "VALID",
        dimension_numbers=("NHWC", "HWIO", "NHWC"),
        preferred_element_type=jnp.float32,
    )
    return result if padded.ndim == 4 else result[0]


def pool_pairs(field):
    summed = lax.reduce_window(
        field, jnp.array(0, field.dtype), lax.add, (2, 2, 1), (2, 2, 1), "VALID"
    )
    return summed * 0.25


def encoder_kernel(x_hbm, w_in, proj_ref, out_ref, xpad, pair_ref, w_ref, local_sem, send_sem, recv_sem):
    lat = lax.axis_index("lat")
    lon = lax.axis_index("lon")
    lats = lax.axis_size("lat")
    lons = lax.axis_size("lon")
    has_up = lat > 0
    has_down = lat < lats - 1
    up, down = lat - 1, lat + 1
    left, right = lax.rem(lon + lons - 1, lons), lax.rem(lon + 1, lons)
    rows, tile_cols, width = x_hbm.shape
    cols = xpad.shape[2]
    pooled_rows, pooled_cols = rows // 2, tile_cols // 2

    barrier = pltpu.get_barrier_semaphore()

    @pl.when(has_up)
    def _():
        pl.semaphore_signal(barrier, inc=1, device_id=(up, lon), device_id_type=MESH)

    @pl.when(has_down)
    def _():
        pl.semaphore_signal(barrier, inc=1, device_id=(down, lon), device_id_type=MESH)

    for peer in (left, right):
        pl.semaphore_signal(barrier, inc=1, device_id=(lat, peer), device_id_type=MESH)
    pl.semaphore_wait(barrier, 2 + has_up.astype(jnp.int32) + has_down.astype(jnp.int32))

    def remote(kind, src, dst, target):
        return pltpu.make_async_remote_copy(
            src_ref=src, dst_ref=dst, send_sem=send_sem.at[kind], recv_sem=recv_sem.at[kind],
            device_id=target, device_id_type=MESH,
        )

    halves = xpad.shape[1]
    lanes = xpad.shape[3]
    inner = pl.ds(0, tile_cols)
    locals_ = []
    to_up, to_down = [], []
    for h in range(halves):
        part = pl.ds(h * lanes, lanes)
        locals_.append(
            pltpu.make_async_copy(x_hbm.at[:, :, part], xpad.at[pl.ds(1, rows), h, inner], local_sem.at[h])
        )
        to_up.append(remote(h, x_hbm.at[0, :, part], xpad.at[rows + 1, h, inner], (up, lon)))
        to_down.append(remote(2 + h, x_hbm.at[rows - 1, :, part], xpad.at[0, h, inner], (down, lon)))
    for h in range(halves):
        locals_[h].start()
        pl.when(has_up)(to_up[h].start)
        pl.when(has_down)(to_down[h].start)

    def zero_edges(first, count):
        span = pl.ds(first, count)

        @pl.when(lat == 0)
        def _():
            xpad[0, :, span] = jnp.zeros((halves, count, lanes), xpad.dtype)

        @pl.when(lat == lats - 1)
        def _():
            xpad[rows + 1, :, span] = jnp.zeros((halves, count, lanes), xpad.dtype)

    taps_n = w_in.shape[0]
    for di in range(taps_n):
        for dj in range(taps_n):
            w_ref[di * width : (di + 1) * width, dj * width : (dj + 1) * width] = w_in[di, dj]
    for h in range(halves):
        locals_[h].wait()
        pl.when(has_down)(to_up[h].wait_recv)
        pl.when(has_up)(to_down[h].wait_recv)
    zero_edges(0, tile_cols)
    to_left, to_right = [], []
    for h in range(halves):
        pair_cols = pl.ds(0, 2)
        to_left.append(
            remote(4 + h, xpad.at[:, h, pair_cols], xpad.at[:, h, pl.ds(tile_cols, 2)], (lat, left))
        )
        to_right.append(
            remote(
                6 + h,
                xpad.at[:, h, pl.ds(tile_cols - 2, 2)],
                xpad.at[:, h, pl.ds(cols - 2, 2)],
                (lat, right),
            )
        )
    for h in range(halves):
        to_left[h].start()
        to_right[h].start()
    for h in range(halves):
        to_left[h].wait_recv()
        to_right[h].wait_recv()
    zero_edges(tile_cols, cols - tile_cols)

    def encoded(row):
        stacked = jnp.concatenate(
            [xpad[row + k, h] for k in range(3) for h in range(halves)], axis=-1
        )
        taps = jnp.dot(stacked, w_ref[...], preferred_element_type=jnp.float32)
        conv = (
            pltpu.roll(taps[:, :width], 1, 0)
            + taps[:, width : 2 * width]
            + pltpu.roll(taps[:, 2 * width :], cols - 1, 0)
        )
        return jax.nn.gelu(conv)

    def pooled_row(p):
        pair = encoded(2 * p) + encoded(2 * p + 1)
        lanes = pair_ref.shape[2]
        chunks = []
        for c in range(width // lanes):
            pair_ref[c, pl.ds(0, cols)] = pair[:, c * lanes : (c + 1) * lanes]
            pair_ref[c, pl.ds(cols, 8)] = jnp.zeros((8, lanes), jnp.float32)
            half = pair_ref.shape[1] // 2
            chunks.append(
                pair_ref[c, pl.ds(0, half, stride=2)] + pair_ref[c, pl.ds(1, half, stride=2)]
            )
        summed = jnp.concatenate(chunks, axis=-1)
        pooled = (summed * 0.25).astype(jnp.bfloat16)
        projected = jnp.dot(pooled, proj_ref[...], preferred_element_type=jnp.float32)
        out_ref[p + 1] = projected[:pooled_cols].astype(out_ref.dtype)

    pooled_row(0)
    edge_up = remote(8, out_ref.at[1], out_ref.at[pooled_rows + 1], (up, lon))
    pl.when(has_up)(edge_up.start)
    pooled_row(pooled_rows - 1)
    edge_down = remote(9, out_ref.at[pooled_rows], out_ref.at[0], (down, lon))
    pl.when(has_down)(edge_down.start)

    def one_row(p, carry):
        pooled_row(p)
        return carry

    lax.fori_loop(1, pooled_rows - 1, one_row, 0)
    pl.when(has_down)(edge_up.wait_recv)
    pl.when(has_up)(edge_down.wait_recv)

    @pl.when(lat == 0)
    def _():
        out_ref[0] = jnp.zeros(out_ref.shape[1:], out_ref.dtype)

    @pl.when(lat == lats - 1)
    def _():
        out_ref[pooled_rows + 1] = jnp.zeros(out_ref.shape[1:], out_ref.dtype)

    for h in range(halves):
        pl.when(has_up)(to_up[h].wait_send)
        pl.when(has_down)(to_down[h].wait_send)
        to_left[h].wait_send()
        to_right[h].wait_send()
    pl.when(has_up)(edge_up.wait_send)
    pl.when(has_down)(edge_down.wait_send)


def encoder(tile, w_enc, w_proj):
    rows, tile_cols, width = tile.shape
    cols = tile_cols + 4
    vmem = pl.BlockSpec(memory_space=pltpu.VMEM)
    return pl.pallas_call(
        encoder_kernel,
        out_shape=jax.ShapeDtypeStruct((rows // 2 + 2, tile_cols // 2, w_proj.shape[1]), jnp.bfloat16),
        in_specs=[pl.BlockSpec(memory_space=pl.ANY), vmem, vmem],
        out_specs=vmem,
        scratch_shapes=[
            pltpu.VMEM((rows + 2, width // 128, cols, 128), jnp.bfloat16),
            pltpu.VMEM((width // 128, cols + 8, 128), jnp.float32),
            pltpu.VMEM((3 * width, 3 * width), jnp.bfloat16),
            pltpu.SemaphoreType.DMA((width // 128,)),
            pltpu.SemaphoreType.DMA((10,)),
            pltpu.SemaphoreType.DMA((10,)),
        ],
        compiler_params=pltpu.CompilerParams(
            collective_id=1, has_side_effects=True, vmem_limit_bytes=VMEM_ALL
        ),
    )(tile, w_enc, w_proj)


def head_kernel(ids_ref, tile_ref, scale_ref, shift_ref, w_in, mix_ref, out_ref, band_ref, mod_ref,
                hidden_ref, w_ref, send_sem, recv_sem, local_sem):
    me = lax.axis_index("lon")
    n = lax.axis_size("lon")
    lat = lax.axis_index("lat")
    last_lat = lax.axis_size("lat") - 1
    halo_rows, tile_cols, width = tile_ref.shape
    cols = band_ref.shape[1]
    leads = out_ref.shape[0]
    step = HEAD_ROWS
    pieces = halo_rows // step

    chips = n // 2
    chip = me // 2
    core = me % 2
    sense = 1 - 2 * core
    kinds = 7

    def device(at_chip, at_core):
        return 2 * lax.rem(at_chip + 2 * chips, chips) + at_core

    sibling = device(chip, 1 - core)
    east = device(chip + 1, core)
    west = device(chip - 1, core)
    far = device(chip + 2, core)
    behind = device(chip - sense, core)
    ahead = device(chip + sense, core)

    barrier = pltpu.get_barrier_semaphore()
    for peer in (sibling, east, west):
        pl.semaphore_signal(barrier, inc=1, device_id=(lat, peer), device_id_type=MESH)
    pl.semaphore_wait(barrier, 3)

    def slot(piece, source):
        start = pl.multiple_of(piece * step, step)
        return band_ref.at[pl.ds(start, step), pl.ds(source * tile_cols, tile_cols)]

    def source_rows(piece):
        return tile_ref.at[pl.ds(pl.multiple_of(piece * step, step), step)]

    def local_copy(piece):
        return pltpu.make_async_copy(source_rows(piece), slot(piece, me), local_sem.at[piece])

    def transfer(piece, kind, origin, target, own=False):
        return pltpu.make_async_remote_copy(
            src_ref=source_rows(piece) if own else slot(piece, origin),
            dst_ref=slot(piece, origin),
            send_sem=send_sem.at[piece * kinds + kind],
            recv_sem=recv_sem.at[piece * kinds + kind],
            device_id=(lat, target),
            device_id_type=MESH,
        )

    def sends(piece):
        return [
            transfer(piece, 0, me, sibling, own=True),
            transfer(piece, 1, me, east, own=True),
            transfer(piece, 2, me, west, own=True),
            transfer(piece, 3, behind, ahead),
            transfer(piece, 4, west, sibling),
            transfer(piece, 5, east, sibling),
            transfer(piece, 6, far, sibling),
        ]

    def receive(piece, kind, origin):
        transfer(piece, kind, origin, me).wait_recv()

    def direct(piece):
        local_copy(piece).start()
        for copy in sends(piece)[:3]:
            copy.start()

    def forward_x(piece):
        receive(piece, 1 + core, behind)
        sends(piece)[3].start()

    def forward_sibling(piece):
        receive(piece, 2 - core, ahead)
        receive(piece, 3, far)
        for copy in sends(piece)[4:]:
            copy.start()

    def arrived(piece):
        local_copy(piece).wait()
        receive(piece, 0, sibling)
        receive(piece, 4, device(chip - 1, 1 - core))
        receive(piece, 5, device(chip + 1, 1 - core))
        receive(piece, 6, device(chip + 2, 1 - core))

    for piece in range(min(AHEAD + 3, pieces)):
        direct(piece)
    taps_n = w_in.shape[0]
    for di in range(taps_n):
        for dj in range(taps_n):
            w_ref[di * width : (di + 1) * width, dj * width : (dj + 1) * width] = w_in[di, dj]
    gains, shifts = [], []
    for l in range(leads):
        row = ids_ref[leads * me + l]
        gains.append(1.0 + scale_ref[pl.ds(row, 1), :])
        shifts.append(shift_ref[pl.ds(row, 1), :])
    for piece in range(min(3, pieces)):
        forward_x(piece)
    for piece in range(min(2, pieces)):
        forward_sibling(piece)
    arrived(0)

    def modulate(piece):
        for j in range(step):
            row = piece * step + j
            keep = ((row > 0) | (lat > 0)) & ((row < halo_rows - 1) | (lat < last_lat))
            source = band_ref[row].astype(jnp.float32)
            for l in range(leads):
                value = jnp.where(keep, source * gains[l] + shifts[l], 0.0)
                mod_ref[l, row] = value.astype(jnp.bfloat16)

    modulate(0)

    def one_chunk(k, carry):
        @pl.when(k + AHEAD + 3 < pieces)
        def _():
            direct(k + AHEAD + 3)

        @pl.when(k + 3 < pieces)
        def _():
            forward_x(k + 3)

        @pl.when(k + 2 < pieces)
        def _():
            forward_sibling(k + 2)

        arrived(k + 1)
        modulate(k + 1)
        base = k * step
        for l in range(leads):
            for j in range(step):
                stacked = jnp.concatenate([mod_ref[l, base + j + t] for t in range(3)], axis=-1)
                taps = jnp.dot(stacked, w_ref[...], preferred_element_type=jnp.float32)
                conv = (
                    pltpu.roll(taps[:, :width], 1, 0)
                    + taps[:, width : 2 * width]
                    + pltpu.roll(taps[:, 2 * width :], cols - 1, 0)
                )
                at = (l * step + j) * width
                hidden_ref[:, at : at + width] = jax.nn.gelu(conv).astype(jnp.bfloat16)
        mixed = jnp.dot(mix_ref[...], hidden_ref[...], preferred_element_type=jnp.float32)
        for l in range(leads):
            for j in range(step):
                at = (l * step + j) * width
                own = mod_ref[l, base + j + 1].astype(jnp.float32)
                out_ref[l, base + j] = (own + mixed[:, at : at + width]).astype(out_ref.dtype)
        return carry

    lax.fori_loop(0, pieces - 1, one_chunk, 0)

    for piece in range(pieces):
        for copy in sends(piece):
            copy.wait_send()


def head(lead_ids, tile, film_scale, film_shift, w_head, zonal_mix, lon_devices):
    halo_rows, tile_cols, width = tile.shape
    rows = halo_rows - 2
    cols = tile_cols * lon_devices
    leads = LEAD_DEV
    pieces = halo_rows // HEAD_ROWS
    vmem = pl.BlockSpec(memory_space=pltpu.VMEM)
    return pl.pallas_call(
        head_kernel,
        out_shape=jax.ShapeDtypeStruct((leads, rows, cols, width), jnp.bfloat16),
        in_specs=[pl.BlockSpec(memory_space=pltpu.SMEM), pl.BlockSpec(memory_space=pl.ANY), vmem, vmem, vmem, vmem],
        out_specs=vmem,
        scratch_shapes=[
            pltpu.VMEM((halo_rows, cols, width), jnp.bfloat16),
            pltpu.VMEM((leads, halo_rows, cols, width), jnp.bfloat16),
            pltpu.VMEM((cols, leads * HEAD_ROWS * width), jnp.bfloat16),
            pltpu.VMEM((3 * width, 3 * width), jnp.bfloat16),
            pltpu.SemaphoreType.DMA((pieces * 7,)),
            pltpu.SemaphoreType.DMA((pieces * 7,)),
            pltpu.SemaphoreType.DMA((pieces,)),
        ],
        compiler_params=pltpu.CompilerParams(
            collective_id=0, has_side_effects=True, vmem_limit_bytes=VMEM_ALL
        ),
    )(lead_ids, tile, film_scale, film_shift, w_head, zonal_mix)


def shards(inputs, w_enc, w_proj, film_scale, film_shift, lead_ids, w_head, zonal_mix):
    lat_rows, lon_cols, channels = inputs.shape
    tile = encoder(inputs, w_enc, w_proj)
    return head(lead_ids, tile, film_scale, film_shift, w_head, zonal_mix, lax.axis_size("lon"))

def solution(mesh):
    in_specs = (P("lat", "lon", None), P(), P(), P(), P(), P(), P(), P())
    out_specs = P("lon", "lat", None, None)
    return jax.shard_map(shards, mesh=mesh, in_specs=in_specs, out_specs=out_specs, check_vma=False)
```

```python
import functools

import jax
import jax.numpy as jnp
from jax import lax
from jax.experimental import pallas as pl
from jax.experimental.pallas import tpu as pltpu
from jax.sharding import PartitionSpec as P

LEAD_DEV = 2
HEAD_ROWS = 2
AHEAD = 2
FORWARD = 4
VMEM_ALL = 67043328
MESH = pl.DeviceIdType.MESH


def extended(x, sides, width, wrap):
    for axis, dim in sides:
        devices, length = (lax.axis_size(axis), x.shape[dim])
        up = [(i, (i + 1) % devices) for i in range(devices if wrap else devices - 1)]
        down = [(j, i) for i, j in up]
        last = lax.slice_in_dim(x, length - width, length, axis=dim)
        initial = lax.slice_in_dim(x, 0, width, axis=dim)
        before = lax.ppermute(last, axis, up)
        after = lax.ppermute(initial, axis, down)
        x = jnp.concatenate([before, x, after], axis=dim)
    return x


def conv_three(padded, weight):
    batched = padded if padded.ndim == 4 else padded[None]
    result = lax.conv_general_dilated(
        batched,
        weight,
        (1, 1),
        "VALID",
        dimension_numbers=("NHWC", "HWIO", "NHWC"),
        preferred_element_type=jnp.float32,
    )
    return result if padded.ndim == 4 else result[0]


def pool_pairs(field):
    summed = lax.reduce_window(
        field, jnp.array(0, field.dtype), lax.add, (2, 2, 1), (2, 2, 1), "VALID"
    )
    return summed * 0.25


def encoder_kernel(x_hbm, w_in, proj_ref, out_ref, xpad, pair_ref, w_ref, local_sem, send_sem, recv_sem):
    lat = lax.axis_index("lat")
    lon = lax.axis_index("lon")
    lats = lax.axis_size("lat")
    lons = lax.axis_size("lon")
    has_up = lat > 0
    has_down = lat < lats - 1
    up, down = lat - 1, lat + 1
    left, right = lax.rem(lon + lons - 1, lons), lax.rem(lon + 1, lons)
    rows, tile_cols, width = x_hbm.shape
    cols = xpad.shape[2]
    pooled_rows, pooled_cols = rows // 2, tile_cols // 2

    barrier = pltpu.get_barrier_semaphore()

    @pl.when(has_up)
    def _():
        pl.semaphore_signal(barrier, inc=1, device_id=(up, lon), device_id_type=MESH)

    @pl.when(has_down)
    def _():
        pl.semaphore_signal(barrier, inc=1, device_id=(down, lon), device_id_type=MESH)

    for peer in (left, right):
        pl.semaphore_signal(barrier, inc=1, device_id=(lat, peer), device_id_type=MESH)
    pl.semaphore_wait(barrier, 2 + has_up.astype(jnp.int32) + has_down.astype(jnp.int32))

    def remote(kind, src, dst, target):
        return pltpu.make_async_remote_copy(
            src_ref=src, dst_ref=dst, send_sem=send_sem.at[kind], recv_sem=recv_sem.at[kind],
            device_id=target, device_id_type=MESH,
        )

    halves = xpad.shape[1]
    lanes = xpad.shape[3]
    inner = pl.ds(0, tile_cols)
    right_halo = pl.ds(tile_cols, 2)
    left_halo = pl.ds(cols - 2, 2)
    halo = pl.ds(tile_cols, cols - tile_cols)

    @pl.when(lat == 0)
    def _():
        xpad[0] = jnp.zeros(xpad.shape[1:], xpad.dtype)

    @pl.when(lat == lats - 1)
    def _():
        xpad[rows + 1] = jnp.zeros(xpad.shape[1:], xpad.dtype)

    to_up, to_down, to_left, to_right, corner_up, corner_down = [], [], [], [], [], []
    body = pl.ds(1, rows)
    for h in range(halves):
        part = pl.ds(h * lanes, lanes)
        to_up.append(remote(h, x_hbm.at[0, :, part], xpad.at[rows + 1, h, inner], (up, lon)))
        to_down.append(remote(2 + h, x_hbm.at[rows - 1, :, part], xpad.at[0, h, inner], (down, lon)))
        to_left.append(
            remote(4 + h, x_hbm.at[:, pl.ds(0, 2), part], xpad.at[body, h, right_halo], (lat, left))
        )
        to_right.append(
            remote(6 + h, x_hbm.at[:, pl.ds(tile_cols - 2, 2), part], xpad.at[body, h, left_halo], (lat, right))
        )
        corner_up.append(remote(8 + h, xpad.at[1, h, halo], xpad.at[rows + 1, h, halo], (up, lon)))
        corner_down.append(remote(10 + h, xpad.at[rows, h, halo], xpad.at[0, h, halo], (down, lon)))
    for h in range(halves):
        to_left[h].start()
        to_right[h].start()
        pl.when(has_up)(to_up[h].start)
        pl.when(has_down)(to_down[h].start)
    for h in range(halves):
        xpad[body, h, inner] = x_hbm[:, :, h * lanes : (h + 1) * lanes]
    taps_n = w_in.shape[0]
    for di in range(taps_n):
        for dj in range(taps_n):
            w_ref[di * width : (di + 1) * width, dj * width : (dj + 1) * width] = w_in[di, dj]
    for h in range(halves):
        to_left[h].wait_recv()
        to_right[h].wait_recv()
    for h in range(halves):
        pl.when(has_up)(corner_up[h].start)
        pl.when(has_down)(corner_down[h].start)

    def encoded(row):
        stacked = jnp.concatenate(
            [xpad[row + k, h] for k in range(3) for h in range(halves)], axis=-1
        )
        taps = jnp.dot(stacked, w_ref[...], preferred_element_type=jnp.float32)
        conv = (
            pltpu.roll(taps[:, :width], 1, 0)
            + taps[:, width : 2 * width]
            + pltpu.roll(taps[:, 2 * width :], cols - 1, 0)
        )
        return jax.nn.gelu(conv)

    def pooled_row(p):
        pair = encoded(2 * p) + encoded(2 * p + 1)
        lanes = pair_ref.shape[2]
        chunks = []
        for c in range(width // lanes):
            pair_ref[c, pl.ds(0, cols)] = pair[:, c * lanes : (c + 1) * lanes]
            pair_ref[c, pl.ds(cols, 8)] = jnp.zeros((8, lanes), jnp.float32)
            half = pair_ref.shape[1] // 2
            chunks.append(
                pair_ref[c, pl.ds(0, half, stride=2)] + pair_ref[c, pl.ds(1, half, stride=2)]
            )
        summed = jnp.concatenate(chunks, axis=-1)
        pooled = (summed * 0.25).astype(jnp.bfloat16)
        projected = jnp.dot(pooled, proj_ref[...], preferred_element_type=jnp.float32)
        out_ref[p + 1] = projected[:pooled_cols].astype(out_ref.dtype)

    def one_row(p, carry):
        pooled_row(p)
        return carry

    lax.fori_loop(1, pooled_rows - 1, one_row, 0)
    for h in range(halves):
        pl.when(has_down)(to_up[h].wait_recv)
        pl.when(has_up)(to_down[h].wait_recv)
        pl.when(has_down)(corner_up[h].wait_recv)
        pl.when(has_up)(corner_down[h].wait_recv)
    pooled_row(0)
    edge_up = remote(12, out_ref.at[1], out_ref.at[pooled_rows + 1], (up, lon))
    pl.when(has_up)(edge_up.start)
    pooled_row(pooled_rows - 1)
    edge_down = remote(13, out_ref.at[pooled_rows], out_ref.at[0], (down, lon))
    pl.when(has_down)(edge_down.start)
    pl.when(has_down)(edge_up.wait_recv)
    pl.when(has_up)(edge_down.wait_recv)

    @pl.when(lat == 0)
    def _():
        out_ref[0] = jnp.zeros(out_ref.shape[1:], out_ref.dtype)

    @pl.when(lat == lats - 1)
    def _():
        out_ref[pooled_rows + 1] = jnp.zeros(out_ref.shape[1:], out_ref.dtype)

    for h in range(halves):
        pl.when(has_up)(to_up[h].wait_send)
        pl.when(has_down)(to_down[h].wait_send)
        to_left[h].wait_send()
        to_right[h].wait_send()
        pl.when(has_up)(corner_up[h].wait_send)
        pl.when(has_down)(corner_down[h].wait_send)
    pl.when(has_up)(edge_up.wait_send)
    pl.when(has_down)(edge_down.wait_send)


def encoder(tile, w_enc, w_proj):
    rows, tile_cols, width = tile.shape
    cols = tile_cols + 4
    vmem = pl.BlockSpec(memory_space=pltpu.VMEM)
    return pl.pallas_call(
        encoder_kernel,
        out_shape=jax.ShapeDtypeStruct((rows // 2 + 2, tile_cols // 2, w_proj.shape[1]), jnp.bfloat16),
        in_specs=[vmem, vmem, vmem],
        out_specs=vmem,
        scratch_shapes=[
            pltpu.VMEM((rows + 2, width // 128, cols, 128), jnp.bfloat16),
            pltpu.VMEM((width // 128, cols + 8, 128), jnp.float32),
            pltpu.VMEM((3 * width, 3 * width), jnp.bfloat16),
            pltpu.SemaphoreType.DMA((width // 128,)),
            pltpu.SemaphoreType.DMA((14,)),
            pltpu.SemaphoreType.DMA((14,)),
        ],
        compiler_params=pltpu.CompilerParams(
            collective_id=1, has_side_effects=True, vmem_limit_bytes=48 * 1024 * 1024
        ),
    )(tile, w_enc, w_proj)


def head_kernel(ids_ref, tile_ref, scale_ref, shift_ref, w_in, mix_ref, out_ref, band_ref, mod_ref,
                hidden_ref, w_ref, send_sem, recv_sem, local_sem):
    me = lax.axis_index("lon")
    n = lax.axis_size("lon")
    lat = lax.axis_index("lat")
    last_lat = lax.axis_size("lat") - 1
    halo_rows, tile_cols, width = tile_ref.shape
    cols = band_ref.shape[1]
    leads = out_ref.shape[0]
    step = HEAD_ROWS
    pieces = halo_rows // step

    chips = n // 2
    chip = me // 2
    core = me % 2
    sense = 1 - 2 * core
    kinds = 7

    def device(at_chip, at_core):
        return 2 * lax.rem(at_chip + 2 * chips, chips) + at_core

    sibling = device(chip, 1 - core)
    east = device(chip + 1, core)
    west = device(chip - 1, core)
    far = device(chip + 2, core)
    behind = device(chip - sense, core)
    ahead = device(chip + sense, core)

    barrier = pltpu.get_barrier_semaphore()
    for peer in (sibling, east, west):
        pl.semaphore_signal(barrier, inc=1, device_id=(lat, peer), device_id_type=MESH)
    pl.semaphore_wait(barrier, 3)

    def slot(piece, source):
        start = pl.multiple_of(piece * step, step)
        return band_ref.at[pl.ds(start, step), pl.ds(source * tile_cols, tile_cols)]

    def source_rows(piece):
        return tile_ref.at[pl.ds(pl.multiple_of(piece * step, step), step)]

    def local_copy(piece):
        return pltpu.make_async_copy(source_rows(piece), slot(piece, me), local_sem.at[piece])

    def transfer(piece, kind, origin, target, own=False):
        return pltpu.make_async_remote_copy(
            src_ref=source_rows(piece) if own else slot(piece, origin),
            dst_ref=slot(piece, origin),
            send_sem=send_sem.at[piece * kinds + kind],
            recv_sem=recv_sem.at[piece * kinds + kind],
            device_id=(lat, target),
            device_id_type=MESH,
        )

    def sends(piece):
        return [
            transfer(piece, 0, me, sibling, own=True),
            transfer(piece, 1, me, east, own=True),
            transfer(piece, 2, me, west, own=True),
            transfer(piece, 3, behind, ahead),
            transfer(piece, 4, west, sibling),
            transfer(piece, 5, east, sibling),
            transfer(piece, 6, far, sibling),
        ]

    def receive(piece, kind, origin):
        transfer(piece, kind, origin, me).wait_recv()

    def direct(piece):
        local_copy(piece).start()
        for copy in sends(piece)[:3]:
            copy.start()

    def forward_x(piece):
        receive(piece, 1 + core, behind)
        sends(piece)[3].start()

    def forward_sibling(piece):
        receive(piece, 2 - core, ahead)
        receive(piece, 3, far)
        for copy in sends(piece)[4:]:
            copy.start()

    def arrived(piece):
        local_copy(piece).wait()
        receive(piece, 0, sibling)
        receive(piece, 4, device(chip - 1, 1 - core))
        receive(piece, 5, device(chip + 1, 1 - core))
        receive(piece, 6, device(chip + 2, 1 - core))

    for piece in range(min(AHEAD + FORWARD, pieces)):
        direct(piece)
    taps_n = w_in.shape[0]
    for di in range(taps_n):
        for dj in range(taps_n):
            w_ref[di * width : (di + 1) * width, dj * width : (dj + 1) * width] = w_in[di, dj]
    gains, shifts = [], []
    for l in range(leads):
        row = ids_ref[leads * me + l]
        gains.append(1.0 + scale_ref[pl.ds(row, 1), :])
        shifts.append(shift_ref[pl.ds(row, 1), :])
    for piece in range(min(FORWARD, pieces)):
        forward_x(piece)
        if 1 <= piece <= 2:
            forward_sibling(piece - 1)
    arrived(0)

    def modulate(piece):
        for j in range(step):
            row = piece * step + j
            keep = ((row > 0) | (lat > 0)) & ((row < halo_rows - 1) | (lat < last_lat))
            source = band_ref[row].astype(jnp.float32)
            for l in range(leads):
                value = jnp.where(keep, source * gains[l] + shifts[l], 0.0)
                mod_ref[l, row] = value.astype(jnp.bfloat16)

    modulate(0)

    def one_chunk(k, carry):
        @pl.when(k + AHEAD + FORWARD < pieces)
        def _():
            direct(k + AHEAD + FORWARD)

        @pl.when(k + 2 < pieces)
        def _():
            forward_sibling(k + 2)

        arrived(k + 1)
        modulate(k + 1)
        base = k * step
        for l in range(leads):
            for j in range(step):
                stacked = jnp.concatenate([mod_ref[l, base + j + t] for t in range(3)], axis=-1)
                taps = jnp.dot(stacked, w_ref[...], preferred_element_type=jnp.float32)
                conv = (
                    pltpu.roll(taps[:, :width], 1, 0)
                    + taps[:, width : 2 * width]
                    + pltpu.roll(taps[:, 2 * width :], cols - 1, 0)
                )
                at = (l * step + j) * width
                hidden_ref[:, at : at + width] = jax.nn.gelu(conv).astype(jnp.bfloat16)
        mixed = jnp.dot(mix_ref[...], hidden_ref[...], preferred_element_type=jnp.float32)
        for l in range(leads):
            for j in range(step):
                at = (l * step + j) * width
                own = mod_ref[l, base + j + 1].astype(jnp.float32)
                out_ref[l, base + j] = (own + mixed[:, at : at + width]).astype(out_ref.dtype)

        @pl.when(k + FORWARD < pieces)
        def _():
            forward_x(k + FORWARD)

        return carry

    lax.fori_loop(0, pieces - 1, one_chunk, 0)

    for piece in range(pieces):
        for copy in sends(piece):
            copy.wait_send()


def head(lead_ids, tile, film_scale, film_shift, w_head, zonal_mix, lon_devices):
    halo_rows, tile_cols, width = tile.shape
    rows = halo_rows - 2
    cols = tile_cols * lon_devices
    leads = LEAD_DEV
    pieces = halo_rows // HEAD_ROWS
    vmem = pl.BlockSpec(memory_space=pltpu.VMEM)
    return pl.pallas_call(
        head_kernel,
        out_shape=jax.ShapeDtypeStruct((leads, rows, cols, width), jnp.bfloat16),
        in_specs=[pl.BlockSpec(memory_space=pltpu.SMEM), pl.BlockSpec(memory_space=pl.ANY), vmem, vmem, vmem, vmem],
        out_specs=vmem,
        scratch_shapes=[
            pltpu.VMEM((halo_rows, cols, width), jnp.bfloat16),
            pltpu.VMEM((leads, halo_rows, cols, width), jnp.bfloat16),
            pltpu.VMEM((cols, leads * HEAD_ROWS * width), jnp.bfloat16),
            pltpu.VMEM((3 * width, 3 * width), jnp.bfloat16),
            pltpu.SemaphoreType.DMA((pieces * 7,)),
            pltpu.SemaphoreType.DMA((pieces * 7,)),
            pltpu.SemaphoreType.DMA((pieces,)),
        ],
        compiler_params=pltpu.CompilerParams(
            collective_id=0, has_side_effects=True, vmem_limit_bytes=VMEM_ALL
        ),
    )(lead_ids, tile, film_scale, film_shift, w_head, zonal_mix)


def shards(inputs, w_enc, w_proj, film_scale, film_shift, lead_ids, w_head, zonal_mix):
    lat_rows, lon_cols, channels = inputs.shape
    tile = encoder(inputs, w_enc, w_proj)
    return head(lead_ids, tile, film_scale, film_shift, w_head, zonal_mix, lax.axis_size("lon"))

def solution(mesh):
    in_specs = (P("lat", "lon", None), P(), P(), P(), P(), P(), P(), P())
    out_specs = P("lon", "lat", None, None)
    return jax.shard_map(shards, mesh=mesh, in_specs=in_specs, out_specs=out_specs, check_vma=False)
```

```python
import functools

import jax
import jax.numpy as jnp
from jax import lax
from jax.experimental import pallas as pl
from jax.experimental.pallas import tpu as pltpu
from jax.sharding import PartitionSpec as P

LEAD_DEV = 2
HEAD_ROWS = 2
AHEAD = 2
FORWARD = 4
VMEM_ALL = 67043328
MESH = pl.DeviceIdType.MESH


def extended(x, sides, width, wrap):
    for axis, dim in sides:
        devices, length = (lax.axis_size(axis), x.shape[dim])
        up = [(i, (i + 1) % devices) for i in range(devices if wrap else devices - 1)]
        down = [(j, i) for i, j in up]
        last = lax.slice_in_dim(x, length - width, length, axis=dim)
        initial = lax.slice_in_dim(x, 0, width, axis=dim)
        before = lax.ppermute(last, axis, up)
        after = lax.ppermute(initial, axis, down)
        x = jnp.concatenate([before, x, after], axis=dim)
    return x


def conv_three(padded, weight):
    batched = padded if padded.ndim == 4 else padded[None]
    result = lax.conv_general_dilated(
        batched,
        weight,
        (1, 1),
        "VALID",
        dimension_numbers=("NHWC", "HWIO", "NHWC"),
        preferred_element_type=jnp.float32,
    )
    return result if padded.ndim == 4 else result[0]


def pool_pairs(field):
    summed = lax.reduce_window(
        field, jnp.array(0, field.dtype), lax.add, (2, 2, 1), (2, 2, 1), "VALID"
    )
    return summed * 0.25


def encoder_kernel(x_hbm, w_in, proj_ref, out_ref, xpad, pair_ref, w_ref, local_sem, send_sem, recv_sem):
    lat = lax.axis_index("lat")
    lon = lax.axis_index("lon")
    lats = lax.axis_size("lat")
    lons = lax.axis_size("lon")
    has_up = lat > 0
    has_down = lat < lats - 1
    up, down = lat - 1, lat + 1
    left, right = lax.rem(lon + lons - 1, lons), lax.rem(lon + 1, lons)
    rows, tile_cols, width = x_hbm.shape
    cols = xpad.shape[2]
    pooled_rows, pooled_cols = rows // 2, tile_cols // 2

    barrier = pltpu.get_barrier_semaphore()

    @pl.when(has_up)
    def _():
        pl.semaphore_signal(barrier, inc=1, device_id=(up, lon), device_id_type=MESH)

    @pl.when(has_down)
    def _():
        pl.semaphore_signal(barrier, inc=1, device_id=(down, lon), device_id_type=MESH)

    for peer in (left, right):
        pl.semaphore_signal(barrier, inc=1, device_id=(lat, peer), device_id_type=MESH)
    pl.semaphore_wait(barrier, 2 + has_up.astype(jnp.int32) + has_down.astype(jnp.int32))

    def remote(kind, src, dst, target):
        return pltpu.make_async_remote_copy(
            src_ref=src, dst_ref=dst, send_sem=send_sem.at[kind], recv_sem=recv_sem.at[kind],
            device_id=target, device_id_type=MESH,
        )

    halves = xpad.shape[1]
    lanes = xpad.shape[3]
    inner = pl.ds(0, tile_cols)
    right_halo = pl.ds(tile_cols, 2)
    left_halo = pl.ds(cols - 2, 2)
    halo = pl.ds(tile_cols, cols - tile_cols)

    @pl.when(lat == 0)
    def _():
        xpad[0] = jnp.zeros(xpad.shape[1:], xpad.dtype)

    @pl.when(lat == lats - 1)
    def _():
        xpad[rows + 1] = jnp.zeros(xpad.shape[1:], xpad.dtype)

    to_up, to_down, to_left, to_right, corner_up, corner_down = [], [], [], [], [], []
    body = pl.ds(1, rows)
    for h in range(halves):
        part = pl.ds(h * lanes, lanes)
        to_up.append(remote(h, x_hbm.at[0, :, part], xpad.at[rows + 1, h, inner], (up, lon)))
        to_down.append(remote(2 + h, x_hbm.at[rows - 1, :, part], xpad.at[0, h, inner], (down, lon)))
        to_left.append(
            remote(4 + h, x_hbm.at[:, pl.ds(0, 2), part], xpad.at[body, h, right_halo], (lat, left))
        )
        to_right.append(
            remote(6 + h, x_hbm.at[:, pl.ds(tile_cols - 2, 2), part], xpad.at[body, h, left_halo], (lat, right))
        )
        corner_up.append(remote(8 + h, xpad.at[1, h, halo], xpad.at[rows + 1, h, halo], (up, lon)))
        corner_down.append(remote(10 + h, xpad.at[rows, h, halo], xpad.at[0, h, halo], (down, lon)))
    for h in range(halves):
        to_left[h].start()
        to_right[h].start()
        pl.when(has_up)(to_up[h].start)
        pl.when(has_down)(to_down[h].start)
    for h in range(halves):
        xpad[body, h, inner] = x_hbm[:, :, h * lanes : (h + 1) * lanes]
    taps_n = w_in.shape[0]
    for di in range(taps_n):
        for dj in range(taps_n):
            w_ref[di * width : (di + 1) * width, dj * width : (dj + 1) * width] = w_in[di, dj]
    for h in range(halves):
        to_left[h].wait_recv()
        to_right[h].wait_recv()
    for h in range(halves):
        pl.when(has_up)(corner_up[h].start)
        pl.when(has_down)(corner_down[h].start)

    def encoded(row):
        stacked = jnp.concatenate(
            [xpad[row + k, h] for k in range(3) for h in range(halves)], axis=-1
        )
        taps = jnp.dot(stacked, w_ref[...], preferred_element_type=jnp.float32)
        conv = (
            pltpu.roll(taps[:, :width], 1, 0)
            + taps[:, width : 2 * width]
            + pltpu.roll(taps[:, 2 * width :], cols - 1, 0)
        )
        return jax.nn.gelu(conv)

    def pooled_row(p):
        pair = encoded(2 * p) + encoded(2 * p + 1)
        lanes = pair_ref.shape[2]
        chunks = []
        for c in range(width // lanes):
            pair_ref[c, pl.ds(0, cols)] = pair[:, c * lanes : (c + 1) * lanes]
            pair_ref[c, pl.ds(cols, 8)] = jnp.zeros((8, lanes), jnp.float32)
            half = pair_ref.shape[1] // 2
            chunks.append(
                pair_ref[c, pl.ds(0, half, stride=2)] + pair_ref[c, pl.ds(1, half, stride=2)]
            )
        summed = jnp.concatenate(chunks, axis=-1)
        pooled = (summed * 0.25).astype(jnp.bfloat16)
        projected = jnp.dot(pooled, proj_ref[...], preferred_element_type=jnp.float32)
        out_ref[p + 1] = projected[:pooled_cols].astype(out_ref.dtype)

    def one_row(p, carry):
        pooled_row(p)
        return carry

    lax.fori_loop(1, pooled_rows - 1, one_row, 0)
    for h in range(halves):
        pl.when(has_down)(to_up[h].wait_recv)
        pl.when(has_up)(to_down[h].wait_recv)
        pl.when(has_down)(corner_up[h].wait_recv)
        pl.when(has_up)(corner_down[h].wait_recv)
    pooled_row(0)
    edge_up = remote(12, out_ref.at[1], out_ref.at[pooled_rows + 1], (up, lon))
    pl.when(has_up)(edge_up.start)
    pooled_row(pooled_rows - 1)
    edge_down = remote(13, out_ref.at[pooled_rows], out_ref.at[0], (down, lon))
    pl.when(has_down)(edge_down.start)
    pl.when(has_down)(edge_up.wait_recv)
    pl.when(has_up)(edge_down.wait_recv)

    @pl.when(lat == 0)
    def _():
        out_ref[0] = jnp.zeros(out_ref.shape[1:], out_ref.dtype)

    @pl.when(lat == lats - 1)
    def _():
        out_ref[pooled_rows + 1] = jnp.zeros(out_ref.shape[1:], out_ref.dtype)

    for h in range(halves):
        pl.when(has_up)(to_up[h].wait_send)
        pl.when(has_down)(to_down[h].wait_send)
        to_left[h].wait_send()
        to_right[h].wait_send()
        pl.when(has_up)(corner_up[h].wait_send)
        pl.when(has_down)(corner_down[h].wait_send)
    pl.when(has_up)(edge_up.wait_send)
    pl.when(has_down)(edge_down.wait_send)


def encoder(tile, w_enc, w_proj):
    rows, tile_cols, width = tile.shape
    cols = tile_cols + 4
    vmem = pl.BlockSpec(memory_space=pltpu.VMEM)
    return pl.pallas_call(
        encoder_kernel,
        out_shape=jax.ShapeDtypeStruct((rows // 2 + 2, tile_cols // 2, w_proj.shape[1]), jnp.bfloat16),
        in_specs=[vmem, vmem, vmem],
        out_specs=vmem,
        scratch_shapes=[
            pltpu.VMEM((rows + 2, width // 128, cols, 128), jnp.bfloat16),
            pltpu.VMEM((width // 128, cols + 8, 128), jnp.float32),
            pltpu.VMEM((3 * width, 3 * width), jnp.bfloat16),
            pltpu.SemaphoreType.DMA((width // 128,)),
            pltpu.SemaphoreType.DMA((14,)),
            pltpu.SemaphoreType.DMA((14,)),
        ],
        compiler_params=pltpu.CompilerParams(
            collective_id=1, has_side_effects=True, vmem_limit_bytes=48 * 1024 * 1024
        ),
    )(tile, w_enc, w_proj)


def head_kernel(ids_ref, tile_ref, scale_ref, shift_ref, w_in, mix_ref, out_ref, band_ref, mod_ref,
                hidden_ref, w_ref, send_sem, recv_sem, local_sem):
    me = lax.axis_index("lon")
    n = lax.axis_size("lon")
    lat = lax.axis_index("lat")
    last_lat = lax.axis_size("lat") - 1
    halo_rows, tile_cols, width = tile_ref.shape
    cols = band_ref.shape[1]
    leads = out_ref.shape[0]
    step = HEAD_ROWS
    pieces = halo_rows // step

    chips = n // 2
    chip = me // 2
    core = me % 2
    sense = 1 - 2 * core
    kinds = 7

    def device(at_chip, at_core):
        return 2 * lax.rem(at_chip + 2 * chips, chips) + at_core

    sibling = device(chip, 1 - core)
    east = device(chip + 1, core)
    west = device(chip - 1, core)
    far = device(chip + 2, core)
    behind = device(chip - sense, core)
    ahead = device(chip + sense, core)

    barrier = pltpu.get_barrier_semaphore()
    for peer in (sibling, east, west):
        pl.semaphore_signal(barrier, inc=1, device_id=(lat, peer), device_id_type=MESH)
    pl.semaphore_wait(barrier, 3)

    def slot(piece, source):
        start = pl.multiple_of(piece * step, step)
        return band_ref.at[pl.ds(start, step), pl.ds(source * tile_cols, tile_cols)]

    def source_rows(piece):
        return tile_ref.at[pl.ds(pl.multiple_of(piece * step, step), step)]

    def local_copy(piece):
        return pltpu.make_async_copy(source_rows(piece), slot(piece, me), local_sem.at[piece])

    def transfer(piece, kind, origin, target, own=False):
        return pltpu.make_async_remote_copy(
            src_ref=source_rows(piece) if own else slot(piece, origin),
            dst_ref=slot(piece, origin),
            send_sem=send_sem.at[piece * kinds + kind],
            recv_sem=recv_sem.at[piece * kinds + kind],
            device_id=(lat, target),
            device_id_type=MESH,
        )

    def sends(piece):
        return [
            transfer(piece, 0, me, sibling, own=True),
            transfer(piece, 1, me, east, own=True),
            transfer(piece, 2, me, west, own=True),
            transfer(piece, 3, behind, ahead),
            transfer(piece, 4, west, sibling),
            transfer(piece, 5, east, sibling),
            transfer(piece, 6, far, sibling),
        ]

    def receive(piece, kind, origin):
        transfer(piece, kind, origin, me).wait_recv()

    def direct(piece):
        local_copy(piece).start()
        for copy in sends(piece)[:3]:
            copy.start()

    def forward_x(piece):
        receive(piece, 1 + core, behind)
        sends(piece)[3].start()

    def forward_sibling(piece):
        receive(piece, 2 - core, ahead)
        receive(piece, 3, far)
        for copy in sends(piece)[4:]:
            copy.start()

    def arrived(piece):
        local_copy(piece).wait()
        receive(piece, 0, sibling)
        receive(piece, 4, device(chip - 1, 1 - core))
        receive(piece, 5, device(chip + 1, 1 - core))
        receive(piece, 6, device(chip + 2, 1 - core))

    direct(0)
    taps_n = w_in.shape[0]
    for di in range(taps_n):
        for dj in range(taps_n):
            w_ref[di * width : (di + 1) * width, dj * width : (dj + 1) * width] = w_in[di, dj]
    gains, shifts = [], []
    for l in range(leads):
        row = ids_ref[leads * me + l]
        gains.append(1.0 + scale_ref[pl.ds(row, 1), :])
        shifts.append(shift_ref[pl.ds(row, 1), :])
    issued = 1
    for piece in range(min(FORWARD, pieces)):
        while issued < min(piece + 2, pieces):
            direct(issued)
            issued += 1
        forward_x(piece)
        if 1 <= piece <= 2:
            forward_sibling(piece - 1)
    while issued < min(AHEAD + FORWARD, pieces):
        direct(issued)
        issued += 1
    arrived(0)

    def modulate(piece):
        for j in range(step):
            row = piece * step + j
            keep = ((row > 0) | (lat > 0)) & ((row < halo_rows - 1) | (lat < last_lat))
            source = band_ref[row].astype(jnp.float32)
            for l in range(leads):
                value = jnp.where(keep, source * gains[l] + shifts[l], 0.0)
                mod_ref[l, row] = value.astype(jnp.bfloat16)

    modulate(0)

    def one_chunk(k, carry):
        @pl.when(k + AHEAD + FORWARD < pieces)
        def _():
            direct(k + AHEAD + FORWARD)

        @pl.when(k + FORWARD < pieces)
        def _():
            forward_x(k + FORWARD)

        @pl.when(k + 2 < pieces)
        def _():
            forward_sibling(k + 2)

        arrived(k + 1)
        modulate(k + 1)
        base = k * step
        for l in range(leads):
            for j in range(step):
                stacked = jnp.concatenate([mod_ref[l, base + j + t] for t in range(3)], axis=-1)
                taps = jnp.dot(stacked, w_ref[...], preferred_element_type=jnp.float32)
                conv = (
                    pltpu.roll(taps[:, :width], 1, 0)
                    + taps[:, width : 2 * width]
                    + pltpu.roll(taps[:, 2 * width :], cols - 1, 0)
                )
                at = (l * step + j) * width
                hidden_ref[:, at : at + width] = jax.nn.gelu(conv).astype(jnp.bfloat16)
        mixed = jnp.dot(mix_ref[...], hidden_ref[...], preferred_element_type=jnp.float32)
        for l in range(leads):
            for j in range(step):
                at = (l * step + j) * width
                own = mod_ref[l, base + j + 1].astype(jnp.float32)
                out_ref[l, base + j] = (own + mixed[:, at : at + width]).astype(out_ref.dtype)
        return carry

    lax.fori_loop(0, pieces - 1, one_chunk, 0)

    for piece in range(pieces):
        for copy in sends(piece):
            copy.wait_send()


def head(lead_ids, tile, film_scale, film_shift, w_head, zonal_mix, lon_devices):
    halo_rows, tile_cols, width = tile.shape
    rows = halo_rows - 2
    cols = tile_cols * lon_devices
    leads = LEAD_DEV
    pieces = halo_rows // HEAD_ROWS
    vmem = pl.BlockSpec(memory_space=pltpu.VMEM)
    return pl.pallas_call(
        head_kernel,
        out_shape=jax.ShapeDtypeStruct((leads, rows, cols, width), jnp.bfloat16),
        in_specs=[pl.BlockSpec(memory_space=pltpu.SMEM), pl.BlockSpec(memory_space=pl.ANY), vmem, vmem, vmem, vmem],
        out_specs=vmem,
        scratch_shapes=[
            pltpu.VMEM((halo_rows, cols, width), jnp.bfloat16),
            pltpu.VMEM((leads, halo_rows, cols, width), jnp.bfloat16),
            pltpu.VMEM((cols, leads * HEAD_ROWS * width), jnp.bfloat16),
            pltpu.VMEM((3 * width, 3 * width), jnp.bfloat16),
            pltpu.SemaphoreType.DMA((pieces * 7,)),
            pltpu.SemaphoreType.DMA((pieces * 7,)),
            pltpu.SemaphoreType.DMA((pieces,)),
        ],
        compiler_params=pltpu.CompilerParams(
            collective_id=0, has_side_effects=True, vmem_limit_bytes=VMEM_ALL
        ),
    )(lead_ids, tile, film_scale, film_shift, w_head, zonal_mix)


def shards(inputs, w_enc, w_proj, film_scale, film_shift, lead_ids, w_head, zonal_mix):
    lat_rows, lon_cols, channels = inputs.shape
    tile = encoder(inputs, w_enc, w_proj)
    return head(lead_ids, tile, film_scale, film_shift, w_head, zonal_mix, lax.axis_size("lon"))

def solution(mesh):
    in_specs = (P("lat", "lon", None), P(), P(), P(), P(), P(), P(), P())
    out_specs = P("lon", "lat", None, None)
    return jax.shard_map(shards, mesh=mesh, in_specs=in_specs, out_specs=out_specs, check_vma=False)
```

```python
import functools

import jax
import jax.numpy as jnp
from jax import lax
from jax.experimental import pallas as pl
from jax.experimental.pallas import tpu as pltpu
from jax.sharding import PartitionSpec as P

LEAD_DEV = 2
HEAD_ROWS = 2
AHEAD = 2
FORWARD = 5
VMEM_ALL = 67043328
MESH = pl.DeviceIdType.MESH


def extended(x, sides, width, wrap):
    for axis, dim in sides:
        devices, length = (lax.axis_size(axis), x.shape[dim])
        up = [(i, (i + 1) % devices) for i in range(devices if wrap else devices - 1)]
        down = [(j, i) for i, j in up]
        last = lax.slice_in_dim(x, length - width, length, axis=dim)
        initial = lax.slice_in_dim(x, 0, width, axis=dim)
        before = lax.ppermute(last, axis, up)
        after = lax.ppermute(initial, axis, down)
        x = jnp.concatenate([before, x, after], axis=dim)
    return x


def conv_three(padded, weight):
    batched = padded if padded.ndim == 4 else padded[None]
    result = lax.conv_general_dilated(
        batched,
        weight,
        (1, 1),
        "VALID",
        dimension_numbers=("NHWC", "HWIO", "NHWC"),
        preferred_element_type=jnp.float32,
    )
    return result if padded.ndim == 4 else result[0]


def pool_pairs(field):
    summed = lax.reduce_window(
        field, jnp.array(0, field.dtype), lax.add, (2, 2, 1), (2, 2, 1), "VALID"
    )
    return summed * 0.25


def encoder_kernel(x_hbm, w_in, proj_ref, out_ref, xpad, pair_ref, w_ref, local_sem, send_sem, recv_sem):
    lat = lax.axis_index("lat")
    lon = lax.axis_index("lon")
    lats = lax.axis_size("lat")
    lons = lax.axis_size("lon")
    has_up = lat > 0
    has_down = lat < lats - 1
    up, down = lat - 1, lat + 1
    left, right = lax.rem(lon + lons - 1, lons), lax.rem(lon + 1, lons)
    rows, tile_cols, width = x_hbm.shape
    cols = xpad.shape[2]
    pooled_rows, pooled_cols = rows // 2, tile_cols // 2

    barrier = pltpu.get_barrier_semaphore()

    @pl.when(has_up)
    def _():
        pl.semaphore_signal(barrier, inc=1, device_id=(up, lon), device_id_type=MESH)

    @pl.when(has_down)
    def _():
        pl.semaphore_signal(barrier, inc=1, device_id=(down, lon), device_id_type=MESH)

    for peer in (left, right):
        pl.semaphore_signal(barrier, inc=1, device_id=(lat, peer), device_id_type=MESH)
    pl.semaphore_wait(barrier, 2 + has_up.astype(jnp.int32) + has_down.astype(jnp.int32))

    def remote(kind, src, dst, target):
        return pltpu.make_async_remote_copy(
            src_ref=src, dst_ref=dst, send_sem=send_sem.at[kind], recv_sem=recv_sem.at[kind],
            device_id=target, device_id_type=MESH,
        )

    halves = xpad.shape[1]
    lanes = xpad.shape[3]
    inner = pl.ds(0, tile_cols)
    right_halo = pl.ds(tile_cols, 2)
    left_halo = pl.ds(cols - 2, 2)
    halo = pl.ds(tile_cols, cols - tile_cols)

    @pl.when(lat == 0)
    def _():
        xpad[0] = jnp.zeros(xpad.shape[1:], xpad.dtype)

    @pl.when(lat == lats - 1)
    def _():
        xpad[rows + 1] = jnp.zeros(xpad.shape[1:], xpad.dtype)

    to_up, to_down, to_left, to_right, corner_up, corner_down = [], [], [], [], [], []
    body = pl.ds(1, rows)
    for h in range(halves):
        part = pl.ds(h * lanes, lanes)
        to_up.append(remote(h, x_hbm.at[0, :, part], xpad.at[rows + 1, h, inner], (up, lon)))
        to_down.append(remote(2 + h, x_hbm.at[rows - 1, :, part], xpad.at[0, h, inner], (down, lon)))
        to_left.append(
            remote(4 + h, x_hbm.at[:, pl.ds(0, 2), part], xpad.at[body, h, right_halo], (lat, left))
        )
        to_right.append(
            remote(6 + h, x_hbm.at[:, pl.ds(tile_cols - 2, 2), part], xpad.at[body, h, left_halo], (lat, right))
        )
        corner_up.append(remote(8 + h, xpad.at[1, h, halo], xpad.at[rows + 1, h, halo], (up, lon)))
        corner_down.append(remote(10 + h, xpad.at[rows, h, halo], xpad.at[0, h, halo], (down, lon)))
    for h in range(halves):
        to_left[h].start()
        to_right[h].start()
        pl.when(has_up)(to_up[h].start)
        pl.when(has_down)(to_down[h].start)
    for h in range(halves):
        xpad[body, h, inner] = x_hbm[:, :, h * lanes : (h + 1) * lanes]
    taps_n = w_in.shape[0]
    for di in range(taps_n):
        for dj in range(taps_n):
            w_ref[di * width : (di + 1) * width, dj * width : (dj + 1) * width] = w_in[di, dj]
    for h in range(halves):
        to_left[h].wait_recv()
        to_right[h].wait_recv()
    for h in range(halves):
        pl.when(has_up)(corner_up[h].start)
        pl.when(has_down)(corner_down[h].start)

    def encoded(row):
        stacked = jnp.concatenate(
            [xpad[row + k, h] for k in range(3) for h in range(halves)], axis=-1
        )
        taps = jnp.dot(stacked, w_ref[...], preferred_element_type=jnp.float32)
        conv = (
            pltpu.roll(taps[:, :width], 1, 0)
            + taps[:, width : 2 * width]
            + pltpu.roll(taps[:, 2 * width :], cols - 1, 0)
        )
        return jax.nn.gelu(conv)

    def pooled_row(p):
        pair = encoded(2 * p) + encoded(2 * p + 1)
        lanes = pair_ref.shape[2]
        chunks = []
        for c in range(width // lanes):
            pair_ref[c, pl.ds(0, cols)] = pair[:, c * lanes : (c + 1) * lanes]
            pair_ref[c, pl.ds(cols, 8)] = jnp.zeros((8, lanes), jnp.float32)
            half = pair_ref.shape[1] // 2
            chunks.append(
                pair_ref[c, pl.ds(0, half, stride=2)] + pair_ref[c, pl.ds(1, half, stride=2)]
            )
        summed = jnp.concatenate(chunks, axis=-1)
        pooled = (summed * 0.25).astype(jnp.bfloat16)
        projected = jnp.dot(pooled, proj_ref[...], preferred_element_type=jnp.float32)
        out_ref[p + 1] = projected[:pooled_cols].astype(out_ref.dtype)

    def one_row(p, carry):
        pooled_row(p)
        return carry

    lax.fori_loop(1, pooled_rows - 1, one_row, 0)
    for h in range(halves):
        pl.when(has_down)(to_up[h].wait_recv)
        pl.when(has_up)(to_down[h].wait_recv)
        pl.when(has_down)(corner_up[h].wait_recv)
        pl.when(has_up)(corner_down[h].wait_recv)
    pooled_row(0)
    edge_up = remote(12, out_ref.at[1], out_ref.at[pooled_rows + 1], (up, lon))
    pl.when(has_up)(edge_up.start)
    pooled_row(pooled_rows - 1)
    edge_down = remote(13, out_ref.at[pooled_rows], out_ref.at[0], (down, lon))
    pl.when(has_down)(edge_down.start)
    pl.when(has_down)(edge_up.wait_recv)
    pl.when(has_up)(edge_down.wait_recv)

    @pl.when(lat == 0)
    def _():
        out_ref[0] = jnp.zeros(out_ref.shape[1:], out_ref.dtype)

    @pl.when(lat == lats - 1)
    def _():
        out_ref[pooled_rows + 1] = jnp.zeros(out_ref.shape[1:], out_ref.dtype)

    for h in range(halves):
        pl.when(has_up)(to_up[h].wait_send)
        pl.when(has_down)(to_down[h].wait_send)
        to_left[h].wait_send()
        to_right[h].wait_send()
        pl.when(has_up)(corner_up[h].wait_send)
        pl.when(has_down)(corner_down[h].wait_send)
    pl.when(has_up)(edge_up.wait_send)
    pl.when(has_down)(edge_down.wait_send)


def encoder(tile, w_enc, w_proj):
    rows, tile_cols, width = tile.shape
    cols = tile_cols + 4
    vmem = pl.BlockSpec(memory_space=pltpu.VMEM)
    return pl.pallas_call(
        encoder_kernel,
        out_shape=jax.ShapeDtypeStruct((rows // 2 + 2, tile_cols // 2, w_proj.shape[1]), jnp.bfloat16),
        in_specs=[vmem, vmem, vmem],
        out_specs=vmem,
        scratch_shapes=[
            pltpu.VMEM((rows + 2, width // 128, cols, 128), jnp.bfloat16),
            pltpu.VMEM((width // 128, cols + 8, 128), jnp.float32),
            pltpu.VMEM((3 * width, 3 * width), jnp.bfloat16),
            pltpu.SemaphoreType.DMA((width // 128,)),
            pltpu.SemaphoreType.DMA((14,)),
            pltpu.SemaphoreType.DMA((14,)),
        ],
        compiler_params=pltpu.CompilerParams(
            collective_id=1, has_side_effects=True, vmem_limit_bytes=48 * 1024 * 1024
        ),
    )(tile, w_enc, w_proj)


def head_kernel(ids_ref, tile_ref, scale_ref, shift_ref, w_in, mix_ref, out_ref, band_ref, mod_ref,
                hidden_ref, w_ref, send_sem, recv_sem, local_sem):
    me = lax.axis_index("lon")
    n = lax.axis_size("lon")
    lat = lax.axis_index("lat")
    last_lat = lax.axis_size("lat") - 1
    halo_rows, tile_cols, width = tile_ref.shape
    cols = band_ref.shape[1]
    leads = out_ref.shape[0]
    step = HEAD_ROWS
    pieces = halo_rows // step

    chips = n // 2
    chip = me // 2
    core = me % 2
    sense = 1 - 2 * core
    kinds = 7

    def device(at_chip, at_core):
        return 2 * lax.rem(at_chip + 2 * chips, chips) + at_core

    sibling = device(chip, 1 - core)
    east = device(chip + 1, core)
    west = device(chip - 1, core)
    far = device(chip + 2, core)
    behind = device(chip - sense, core)
    ahead = device(chip + sense, core)

    barrier = pltpu.get_barrier_semaphore()
    for peer in (sibling, east, west):
        pl.semaphore_signal(barrier, inc=1, device_id=(lat, peer), device_id_type=MESH)
    pl.semaphore_wait(barrier, 3)

    def slot(piece, source):
        start = pl.multiple_of(piece * step, step)
        return band_ref.at[pl.ds(start, step), pl.ds(source * tile_cols, tile_cols)]

    def source_rows(piece):
        return tile_ref.at[pl.ds(pl.multiple_of(piece * step, step), step)]

    def local_copy(piece):
        return pltpu.make_async_copy(source_rows(piece), slot(piece, me), local_sem.at[piece])

    def transfer(piece, kind, origin, target, own=False):
        return pltpu.make_async_remote_copy(
            src_ref=source_rows(piece) if own else slot(piece, origin),
            dst_ref=slot(piece, origin),
            send_sem=send_sem.at[piece * kinds + kind],
            recv_sem=recv_sem.at[piece * kinds + kind],
            device_id=(lat, target),
            device_id_type=MESH,
        )

    def sends(piece):
        return [
            transfer(piece, 0, me, sibling, own=True),
            transfer(piece, 1, me, east, own=True),
            transfer(piece, 2, me, west, own=True),
            transfer(piece, 3, behind, ahead),
            transfer(piece, 4, west, sibling),
            transfer(piece, 5, east, sibling),
            transfer(piece, 6, far, sibling),
        ]

    def receive(piece, kind, origin):
        transfer(piece, kind, origin, me).wait_recv()

    def direct(piece):
        local_copy(piece).start()
        for copy in sends(piece)[:3]:
            copy.start()

    def forward_x(piece):
        receive(piece, 1 + core, behind)
        sends(piece)[3].start()

    def forward_sibling(piece):
        receive(piece, 2 - core, ahead)
        receive(piece, 3, far)
        for copy in sends(piece)[4:]:
            copy.start()

    def arrived(piece):
        local_copy(piece).wait()
        receive(piece, 0, sibling)
        receive(piece, 4, device(chip - 1, 1 - core))
        receive(piece, 5, device(chip + 1, 1 - core))
        receive(piece, 6, device(chip + 2, 1 - core))

    for piece in range(min(AHEAD + FORWARD, pieces)):
        direct(piece)
    taps_n = w_in.shape[0]
    for di in range(taps_n):
        for dj in range(taps_n):
            w_ref[di * width : (di + 1) * width, dj * width : (dj + 1) * width] = w_in[di, dj]
    gains, shifts = [], []
    for l in range(leads):
        row = ids_ref[leads * me + l]
        gains.append(1.0 + scale_ref[pl.ds(row, 1), :])
        shifts.append(shift_ref[pl.ds(row, 1), :])
    for piece in range(min(FORWARD, pieces)):
        forward_x(piece)
    for piece in range(min(2, pieces)):
        forward_sibling(piece)
    arrived(0)

    def modulate(piece):
        for j in range(step):
            row = piece * step + j
            keep = ((row > 0) | (lat > 0)) & ((row < halo_rows - 1) | (lat < last_lat))
            source = band_ref[row].astype(jnp.float32)
            for l in range(leads):
                value = jnp.where(keep, source * gains[l] + shifts[l], 0.0)
                mod_ref[l, row] = value.astype(jnp.bfloat16)

    modulate(0)

    def one_chunk(k, carry):
        @pl.when(k + AHEAD + FORWARD < pieces)
        def _():
            direct(k + AHEAD + FORWARD)

        @pl.when(k + FORWARD < pieces)
        def _():
            forward_x(k + FORWARD)

        @pl.when(k + 2 < pieces)
        def _():
            forward_sibling(k + 2)

        arrived(k + 1)
        modulate(k + 1)
        base = k * step
        for l in range(leads):
            for j in range(step):
                stacked = jnp.concatenate([mod_ref[l, base + j + t] for t in range(3)], axis=-1)
                taps = jnp.dot(stacked, w_ref[...], preferred_element_type=jnp.float32)
                conv = (
                    pltpu.roll(taps[:, :width], 1, 0)
                    + taps[:, width : 2 * width]
                    + pltpu.roll(taps[:, 2 * width :], cols - 1, 0)
                )
                at = (l * step + j) * width
                hidden_ref[:, at : at + width] = jax.nn.gelu(conv).astype(jnp.bfloat16)
        mixed = jnp.dot(mix_ref[...], hidden_ref[...], preferred_element_type=jnp.float32)
        for l in range(leads):
            for j in range(step):
                at = (l * step + j) * width
                own = mod_ref[l, base + j + 1].astype(jnp.float32)
                out_ref[l, base + j] = (own + mixed[:, at : at + width]).astype(out_ref.dtype)
        return carry

    lax.fori_loop(0, pieces - 1, one_chunk, 0)

    for piece in range(pieces):
        for copy in sends(piece):
            copy.wait_send()


def head(lead_ids, tile, film_scale, film_shift, w_head, zonal_mix, lon_devices):
    halo_rows, tile_cols, width = tile.shape
    rows = halo_rows - 2
    cols = tile_cols * lon_devices
    leads = LEAD_DEV
    pieces = halo_rows // HEAD_ROWS
    vmem = pl.BlockSpec(memory_space=pltpu.VMEM)
    return pl.pallas_call(
        head_kernel,
        out_shape=jax.ShapeDtypeStruct((leads, rows, cols, width), jnp.bfloat16),
        in_specs=[pl.BlockSpec(memory_space=pltpu.SMEM), pl.BlockSpec(memory_space=pl.ANY), vmem, vmem, vmem, vmem],
        out_specs=vmem,
        scratch_shapes=[
            pltpu.VMEM((halo_rows, cols, width), jnp.bfloat16),
            pltpu.VMEM((leads, halo_rows, cols, width), jnp.bfloat16),
            pltpu.VMEM((cols, leads * HEAD_ROWS * width), jnp.bfloat16),
            pltpu.VMEM((3 * width, 3 * width), jnp.bfloat16),
            pltpu.SemaphoreType.DMA((pieces * 7,)),
            pltpu.SemaphoreType.DMA((pieces * 7,)),
            pltpu.SemaphoreType.DMA((pieces,)),
        ],
        compiler_params=pltpu.CompilerParams(
            collective_id=0, has_side_effects=True, vmem_limit_bytes=VMEM_ALL
        ),
    )(lead_ids, tile, film_scale, film_shift, w_head, zonal_mix)


def shards(inputs, w_enc, w_proj, film_scale, film_shift, lead_ids, w_head, zonal_mix):
    lat_rows, lon_cols, channels = inputs.shape
    tile = encoder(inputs, w_enc, w_proj)
    return head(lead_ids, tile, film_scale, film_shift, w_head, zonal_mix, lax.axis_size("lon"))

def solution(mesh):
    in_specs = (P("lat", "lon", None), P(), P(), P(), P(), P(), P(), P())
    out_specs = P("lon", "lat", None, None)
    return jax.shard_map(shards, mesh=mesh, in_specs=in_specs, out_specs=out_specs, check_vma=False)
```

```python
import functools

import jax
import jax.numpy as jnp
from jax import lax
from jax.experimental import pallas as pl
from jax.experimental.pallas import tpu as pltpu
from jax.sharding import PartitionSpec as P

LEAD_DEV = 2
HEAD_ROWS = 2
AHEAD = 2
FORWARD = 4
VMEM_ALL = 67043328
MESH = pl.DeviceIdType.MESH


def extended(x, sides, width, wrap):
    for axis, dim in sides:
        devices, length = (lax.axis_size(axis), x.shape[dim])
        up = [(i, (i + 1) % devices) for i in range(devices if wrap else devices - 1)]
        down = [(j, i) for i, j in up]
        last = lax.slice_in_dim(x, length - width, length, axis=dim)
        initial = lax.slice_in_dim(x, 0, width, axis=dim)
        before = lax.ppermute(last, axis, up)
        after = lax.ppermute(initial, axis, down)
        x = jnp.concatenate([before, x, after], axis=dim)
    return x


def conv_three(padded, weight):
    batched = padded if padded.ndim == 4 else padded[None]
    result = lax.conv_general_dilated(
        batched,
        weight,
        (1, 1),
        "VALID",
        dimension_numbers=("NHWC", "HWIO", "NHWC"),
        preferred_element_type=jnp.float32,
    )
    return result if padded.ndim == 4 else result[0]


def pool_pairs(field):
    summed = lax.reduce_window(
        field, jnp.array(0, field.dtype), lax.add, (2, 2, 1), (2, 2, 1), "VALID"
    )
    return summed * 0.25


def encoder_kernel(x_hbm, w_in, proj_ref, out_ref, xpad, pair_ref, w_ref, local_sem, send_sem, recv_sem):
    lat = lax.axis_index("lat")
    lon = lax.axis_index("lon")
    lats = lax.axis_size("lat")
    lons = lax.axis_size("lon")
    has_up = lat > 0
    has_down = lat < lats - 1
    up, down = lat - 1, lat + 1
    left, right = lax.rem(lon + lons - 1, lons), lax.rem(lon + 1, lons)
    rows, tile_cols, width = x_hbm.shape
    cols = xpad.shape[2]
    pooled_rows, pooled_cols = rows // 2, tile_cols // 2

    barrier = pltpu.get_barrier_semaphore()

    @pl.when(has_up)
    def _():
        pl.semaphore_signal(barrier, inc=1, device_id=(up, lon), device_id_type=MESH)

    @pl.when(has_down)
    def _():
        pl.semaphore_signal(barrier, inc=1, device_id=(down, lon), device_id_type=MESH)

    for peer in (left, right):
        pl.semaphore_signal(barrier, inc=1, device_id=(lat, peer), device_id_type=MESH)
    pl.semaphore_wait(barrier, 2 + has_up.astype(jnp.int32) + has_down.astype(jnp.int32))

    def remote(kind, src, dst, target):
        return pltpu.make_async_remote_copy(
            src_ref=src, dst_ref=dst, send_sem=send_sem.at[kind], recv_sem=recv_sem.at[kind],
            device_id=target, device_id_type=MESH,
        )

    halves = xpad.shape[1]
    lanes = xpad.shape[3]
    inner = pl.ds(0, tile_cols)
    right_halo = pl.ds(tile_cols, 2)
    left_halo = pl.ds(cols - 2, 2)
    halo = pl.ds(tile_cols, cols - tile_cols)

    @pl.when(lat == 0)
    def _():
        xpad[0] = jnp.zeros(xpad.shape[1:], xpad.dtype)

    @pl.when(lat == lats - 1)
    def _():
        xpad[rows + 1] = jnp.zeros(xpad.shape[1:], xpad.dtype)

    to_up, to_down, to_left, to_right, corner_up, corner_down = [], [], [], [], [], []
    body = pl.ds(1, rows)
    for h in range(halves):
        part = pl.ds(h * lanes, lanes)
        to_up.append(remote(h, x_hbm.at[0, :, part], xpad.at[rows + 1, h, inner], (up, lon)))
        to_down.append(remote(2 + h, x_hbm.at[rows - 1, :, part], xpad.at[0, h, inner], (down, lon)))
        to_left.append(
            remote(4 + h, x_hbm.at[:, pl.ds(0, 2), part], xpad.at[body, h, right_halo], (lat, left))
        )
        to_right.append(
            remote(6 + h, x_hbm.at[:, pl.ds(tile_cols - 2, 2), part], xpad.at[body, h, left_halo], (lat, right))
        )
        corner_up.append(remote(8 + h, xpad.at[1, h, halo], xpad.at[rows + 1, h, halo], (up, lon)))
        corner_down.append(remote(10 + h, xpad.at[rows, h, halo], xpad.at[0, h, halo], (down, lon)))
    for h in range(halves):
        to_left[h].start()
        to_right[h].start()
        pl.when(has_up)(to_up[h].start)
        pl.when(has_down)(to_down[h].start)
    for h in range(halves):
        xpad[body, h, inner] = x_hbm[:, :, h * lanes : (h + 1) * lanes]
    taps_n = w_in.shape[0]
    for di in range(taps_n):
        for dj in range(taps_n):
            w_ref[di * width : (di + 1) * width, dj * width : (dj + 1) * width] = w_in[di, dj]
    for h in range(halves):
        to_left[h].wait_recv()
        to_right[h].wait_recv()
    gap = cols - tile_cols - 4
    xpad[body, :, pl.ds(tile_cols + 2, gap)] = jnp.zeros((rows, halves, gap, lanes), xpad.dtype)
    for h in range(halves):
        pl.when(has_up)(corner_up[h].start)
        pl.when(has_down)(corner_down[h].start)

    def stacked(row):
        return jnp.concatenate([xpad[row + k, h] for k in range(3) for h in range(halves)], axis=-1)

    def pooled_row(p):
        both = jnp.concatenate([stacked(2 * p), stacked(2 * p + 1)], axis=0)
        taps = jnp.dot(both, w_ref[...], preferred_element_type=jnp.float32)
        pair = None
        for half_at in (0, cols):
            part = taps[half_at : half_at + cols]
            conv = (
                pltpu.roll(part[:, :width], 1, 0)
                + part[:, width : 2 * width]
                + pltpu.roll(part[:, 2 * width :], cols - 1, 0)
            )
            value = jax.nn.gelu(conv)
            pair = value if pair is None else pair + value
        lanes = pair_ref.shape[2]
        chunks = []
        for c in range(width // lanes):
            pair_ref[c] = pair[:, c * lanes : (c + 1) * lanes]
            half = pair_ref.shape[1] // 2
            chunks.append(
                pair_ref[c, pl.ds(0, half, stride=2)] + pair_ref[c, pl.ds(1, half, stride=2)]
            )
        summed = jnp.concatenate(chunks, axis=-1)
        pooled = (summed * 0.25).astype(jnp.bfloat16)
        projected = jnp.dot(pooled, proj_ref[...], preferred_element_type=jnp.float32)
        out_ref[p + 1] = projected[:pooled_cols].astype(out_ref.dtype)

    def one_row(p, carry):
        pooled_row(p)
        return carry

    lax.fori_loop(1, pooled_rows - 1, one_row, 0)
    for h in range(halves):
        pl.when(has_down)(to_up[h].wait_recv)
        pl.when(has_up)(to_down[h].wait_recv)
        pl.when(has_down)(corner_up[h].wait_recv)
        pl.when(has_up)(corner_down[h].wait_recv)
    pooled_row(0)
    edge_up = remote(12, out_ref.at[1], out_ref.at[pooled_rows + 1], (up, lon))
    pl.when(has_up)(edge_up.start)
    pooled_row(pooled_rows - 1)
    edge_down = remote(13, out_ref.at[pooled_rows], out_ref.at[0], (down, lon))
    pl.when(has_down)(edge_down.start)
    pl.when(has_down)(edge_up.wait_recv)
    pl.when(has_up)(edge_down.wait_recv)

    @pl.when(lat == 0)
    def _():
        out_ref[0] = jnp.zeros(out_ref.shape[1:], out_ref.dtype)

    @pl.when(lat == lats - 1)
    def _():
        out_ref[pooled_rows + 1] = jnp.zeros(out_ref.shape[1:], out_ref.dtype)

    for h in range(halves):
        pl.when(has_up)(to_up[h].wait_send)
        pl.when(has_down)(to_down[h].wait_send)
        to_left[h].wait_send()
        to_right[h].wait_send()
        pl.when(has_up)(corner_up[h].wait_send)
        pl.when(has_down)(corner_down[h].wait_send)
    pl.when(has_up)(edge_up.wait_send)
    pl.when(has_down)(edge_down.wait_send)


def encoder(tile, w_enc, w_proj):
    rows, tile_cols, width = tile.shape
    cols = tile_cols + 12
    vmem = pl.BlockSpec(memory_space=pltpu.VMEM)
    return pl.pallas_call(
        encoder_kernel,
        out_shape=jax.ShapeDtypeStruct((rows // 2 + 2, tile_cols // 2, w_proj.shape[1]), jnp.bfloat16),
        in_specs=[vmem, vmem, vmem],
        out_specs=vmem,
        scratch_shapes=[
            pltpu.VMEM((rows + 2, width // 128, cols, 128), jnp.bfloat16),
            pltpu.VMEM((width // 128, cols, 128), jnp.float32),
            pltpu.VMEM((3 * width, 3 * width), jnp.bfloat16),
            pltpu.SemaphoreType.DMA((width // 128,)),
            pltpu.SemaphoreType.DMA((14,)),
            pltpu.SemaphoreType.DMA((14,)),
        ],
        compiler_params=pltpu.CompilerParams(
            collective_id=1, has_side_effects=True, vmem_limit_bytes=48 * 1024 * 1024
        ),
    )(tile, w_enc, w_proj)


def head_kernel(ids_ref, tile_ref, scale_ref, shift_ref, w_in, mix_ref, out_ref, band_ref, mod_ref,
                hidden_ref, w_ref, send_sem, recv_sem, local_sem):
    me = lax.axis_index("lon")
    n = lax.axis_size("lon")
    lat = lax.axis_index("lat")
    last_lat = lax.axis_size("lat") - 1
    halo_rows, tile_cols, width = tile_ref.shape
    cols = band_ref.shape[1]
    leads = out_ref.shape[0]
    step = HEAD_ROWS
    pieces = halo_rows // step

    chips = n // 2
    chip = me // 2
    core = me % 2
    sense = 1 - 2 * core
    kinds = 7

    def device(at_chip, at_core):
        return 2 * lax.rem(at_chip + 2 * chips, chips) + at_core

    sibling = device(chip, 1 - core)
    east = device(chip + 1, core)
    west = device(chip - 1, core)
    far = device(chip + 2, core)
    behind = device(chip - sense, core)
    ahead = device(chip + sense, core)

    barrier = pltpu.get_barrier_semaphore()
    for peer in (sibling, east, west):
        pl.semaphore_signal(barrier, inc=1, device_id=(lat, peer), device_id_type=MESH)
    pl.semaphore_wait(barrier, 3)

    def slot(piece, source):
        start = pl.multiple_of(piece * step, step)
        return band_ref.at[pl.ds(start, step), pl.ds(source * tile_cols, tile_cols)]

    def source_rows(piece):
        return tile_ref.at[pl.ds(pl.multiple_of(piece * step, step), step)]

    def local_copy(piece):
        return pltpu.make_async_copy(source_rows(piece), slot(piece, me), local_sem.at[piece])

    def transfer(piece, kind, origin, target, own=False):
        return pltpu.make_async_remote_copy(
            src_ref=source_rows(piece) if own else slot(piece, origin),
            dst_ref=slot(piece, origin),
            send_sem=send_sem.at[piece * kinds + kind],
            recv_sem=recv_sem.at[piece * kinds + kind],
            device_id=(lat, target),
            device_id_type=MESH,
        )

    def sends(piece):
        return [
            transfer(piece, 0, me, sibling, own=True),
            transfer(piece, 1, me, east, own=True),
            transfer(piece, 2, me, west, own=True),
            transfer(piece, 3, behind, ahead),
            transfer(piece, 4, west, sibling),
            transfer(piece, 5, east, sibling),
            transfer(piece, 6, far, sibling),
        ]

    def receive(piece, kind, origin):
        transfer(piece, kind, origin, me).wait_recv()

    def direct(piece):
        local_copy(piece).start()
        for copy in sends(piece)[:3]:
            copy.start()

    def forward_x(piece):
        receive(piece, 1 + core, behind)
        sends(piece)[3].start()

    def forward_sibling(piece):
        receive(piece, 2 - core, ahead)
        receive(piece, 3, far)
        for copy in sends(piece)[4:]:
            copy.start()

    def arrived(piece):
        local_copy(piece).wait()
        receive(piece, 0, sibling)
        receive(piece, 4, device(chip - 1, 1 - core))
        receive(piece, 5, device(chip + 1, 1 - core))
        receive(piece, 6, device(chip + 2, 1 - core))

    for piece in range(min(AHEAD + FORWARD, pieces)):
        direct(piece)
    taps_n = w_in.shape[0]
    for di in range(taps_n):
        for dj in range(taps_n):
            w_ref[di * width : (di + 1) * width, dj * width : (dj + 1) * width] = w_in[di, dj]
    gains, shifts = [], []
    for l in range(leads):
        row = ids_ref[leads * me + l]
        gains.append(1.0 + scale_ref[pl.ds(row, 1), :])
        shifts.append(shift_ref[pl.ds(row, 1), :])
    for piece in range(min(FORWARD, pieces)):
        forward_x(piece)
    for piece in range(min(2, pieces)):
        forward_sibling(piece)
    arrived(0)

    def modulate(piece):
        for j in range(step):
            row = piece * step + j
            keep = ((row > 0) | (lat > 0)) & ((row < halo_rows - 1) | (lat < last_lat))
            source = band_ref[row].astype(jnp.float32)
            for l in range(leads):
                value = jnp.where(keep, source * gains[l] + shifts[l], 0.0)
                mod_ref[l, row] = value.astype(jnp.bfloat16)

    modulate(0)

    def one_chunk(k, carry):
        @pl.when(k + AHEAD + FORWARD < pieces)
        def _():
            direct(k + AHEAD + FORWARD)

        @pl.when(k + FORWARD < pieces)
        def _():
            forward_x(k + FORWARD)

        @pl.when(k + 2 < pieces)
        def _():
            forward_sibling(k + 2)

        arrived(k + 1)
        modulate(k + 1)
        base = k * step
        for l in range(leads):
            for j in range(step):
                stacked = jnp.concatenate([mod_ref[l, base + j + t] for t in range(3)], axis=-1)
                taps = jnp.dot(stacked, w_ref[...], preferred_element_type=jnp.float32)
                conv = (
                    pltpu.roll(taps[:, :width], 1, 0)
                    + taps[:, width : 2 * width]
                    + pltpu.roll(taps[:, 2 * width :], cols - 1, 0)
                )
                at = (l * step + j) * width
                hidden_ref[:, at : at + width] = jax.nn.gelu(conv).astype(jnp.bfloat16)
        mixed = jnp.dot(mix_ref[...], hidden_ref[...], preferred_element_type=jnp.float32)
        for l in range(leads):
            for j in range(step):
                at = (l * step + j) * width
                own = mod_ref[l, base + j + 1].astype(jnp.float32)
                out_ref[l, base + j] = (own + mixed[:, at : at + width]).astype(out_ref.dtype)
        return carry

    lax.fori_loop(0, pieces - 1, one_chunk, 0)

    for piece in range(pieces):
        for copy in sends(piece):
            copy.wait_send()


def head(lead_ids, tile, film_scale, film_shift, w_head, zonal_mix, lon_devices):
    halo_rows, tile_cols, width = tile.shape
    rows = halo_rows - 2
    cols = tile_cols * lon_devices
    leads = LEAD_DEV
    pieces = halo_rows // HEAD_ROWS
    vmem = pl.BlockSpec(memory_space=pltpu.VMEM)
    return pl.pallas_call(
        head_kernel,
        out_shape=jax.ShapeDtypeStruct((leads, rows, cols, width), jnp.bfloat16),
        in_specs=[pl.BlockSpec(memory_space=pltpu.SMEM), pl.BlockSpec(memory_space=pl.ANY), vmem, vmem, vmem, vmem],
        out_specs=vmem,
        scratch_shapes=[
            pltpu.VMEM((halo_rows, cols, width), jnp.bfloat16),
            pltpu.VMEM((leads, halo_rows, cols, width), jnp.bfloat16),
            pltpu.VMEM((cols, leads * HEAD_ROWS * width), jnp.bfloat16),
            pltpu.VMEM((3 * width, 3 * width), jnp.bfloat16),
            pltpu.SemaphoreType.DMA((pieces * 7,)),
            pltpu.SemaphoreType.DMA((pieces * 7,)),
            pltpu.SemaphoreType.DMA((pieces,)),
        ],
        compiler_params=pltpu.CompilerParams(
            collective_id=0, has_side_effects=True, vmem_limit_bytes=VMEM_ALL
        ),
    )(lead_ids, tile, film_scale, film_shift, w_head, zonal_mix)


def shards(inputs, w_enc, w_proj, film_scale, film_shift, lead_ids, w_head, zonal_mix):
    lat_rows, lon_cols, channels = inputs.shape
    tile = encoder(inputs, w_enc, w_proj)
    return head(lead_ids, tile, film_scale, film_shift, w_head, zonal_mix, lax.axis_size("lon"))

def solution(mesh):
    in_specs = (P("lat", "lon", None), P(), P(), P(), P(), P(), P(), P())
    out_specs = P("lon", "lat", None, None)
    return jax.shard_map(shards, mesh=mesh, in_specs=in_specs, out_specs=out_specs, check_vma=False)
```

```python
import functools

import jax
import jax.numpy as jnp
from jax import lax
from jax.experimental import pallas as pl
from jax.experimental.pallas import tpu as pltpu
from jax.sharding import PartitionSpec as P

LEAD_DEV = 2
HEAD_ROWS = 2
AHEAD = 3
FORWARD = 4
VMEM_ALL = 67043328
MESH = pl.DeviceIdType.MESH


def extended(x, sides, width, wrap):
    for axis, dim in sides:
        devices, length = (lax.axis_size(axis), x.shape[dim])
        up = [(i, (i + 1) % devices) for i in range(devices if wrap else devices - 1)]
        down = [(j, i) for i, j in up]
        last = lax.slice_in_dim(x, length - width, length, axis=dim)
        initial = lax.slice_in_dim(x, 0, width, axis=dim)
        before = lax.ppermute(last, axis, up)
        after = lax.ppermute(initial, axis, down)
        x = jnp.concatenate([before, x, after], axis=dim)
    return x


def conv_three(padded, weight):
    batched = padded if padded.ndim == 4 else padded[None]
    result = lax.conv_general_dilated(
        batched,
        weight,
        (1, 1),
        "VALID",
        dimension_numbers=("NHWC", "HWIO", "NHWC"),
        preferred_element_type=jnp.float32,
    )
    return result if padded.ndim == 4 else result[0]


def pool_pairs(field):
    summed = lax.reduce_window(
        field, jnp.array(0, field.dtype), lax.add, (2, 2, 1), (2, 2, 1), "VALID"
    )
    return summed * 0.25


def encoder_kernel(x_hbm, w_in, proj_ref, out_ref, xpad, pair_ref, w_ref, local_sem, send_sem, recv_sem):
    lat = lax.axis_index("lat")
    lon = lax.axis_index("lon")
    lats = lax.axis_size("lat")
    lons = lax.axis_size("lon")
    has_up = lat > 0
    has_down = lat < lats - 1
    up, down = lat - 1, lat + 1
    left, right = lax.rem(lon + lons - 1, lons), lax.rem(lon + 1, lons)
    rows, tile_cols, width = x_hbm.shape
    cols = xpad.shape[2]
    pooled_rows, pooled_cols = rows // 2, tile_cols // 2

    barrier = pltpu.get_barrier_semaphore()

    @pl.when(has_up)
    def _():
        pl.semaphore_signal(barrier, inc=1, device_id=(up, lon), device_id_type=MESH)

    @pl.when(has_down)
    def _():
        pl.semaphore_signal(barrier, inc=1, device_id=(down, lon), device_id_type=MESH)

    for peer in (left, right):
        pl.semaphore_signal(barrier, inc=1, device_id=(lat, peer), device_id_type=MESH)
    pl.semaphore_wait(barrier, 2 + has_up.astype(jnp.int32) + has_down.astype(jnp.int32))

    def remote(kind, src, dst, target):
        return pltpu.make_async_remote_copy(
            src_ref=src, dst_ref=dst, send_sem=send_sem.at[kind], recv_sem=recv_sem.at[kind],
            device_id=target, device_id_type=MESH,
        )

    halves = xpad.shape[1]
    lanes = xpad.shape[3]
    inner = pl.ds(0, tile_cols)
    right_halo = pl.ds(tile_cols, 2)
    left_halo = pl.ds(cols - 2, 2)
    halo = pl.ds(tile_cols, cols - tile_cols)

    @pl.when(lat == 0)
    def _():
        xpad[0] = jnp.zeros(xpad.shape[1:], xpad.dtype)

    @pl.when(lat == lats - 1)
    def _():
        xpad[rows + 1] = jnp.zeros(xpad.shape[1:], xpad.dtype)

    to_up, to_down, to_left, to_right, corner_up, corner_down = [], [], [], [], [], []
    body = pl.ds(1, rows)
    for h in range(halves):
        part = pl.ds(h * lanes, lanes)
        to_up.append(remote(h, x_hbm.at[0, :, part], xpad.at[rows + 1, h, inner], (up, lon)))
        to_down.append(remote(2 + h, x_hbm.at[rows - 1, :, part], xpad.at[0, h, inner], (down, lon)))
        to_left.append(
            remote(4 + h, x_hbm.at[:, pl.ds(0, 2), part], xpad.at[body, h, right_halo], (lat, left))
        )
        to_right.append(
            remote(6 + h, x_hbm.at[:, pl.ds(tile_cols - 2, 2), part], xpad.at[body, h, left_halo], (lat, right))
        )
        corner_up.append(remote(8 + h, xpad.at[1, h, halo], xpad.at[rows + 1, h, halo], (up, lon)))
        corner_down.append(remote(10 + h, xpad.at[rows, h, halo], xpad.at[0, h, halo], (down, lon)))
    for h in range(halves):
        to_left[h].start()
        to_right[h].start()
        pl.when(has_up)(to_up[h].start)
        pl.when(has_down)(to_down[h].start)
    for h in range(halves):
        xpad[body, h, inner] = x_hbm[:, :, h * lanes : (h + 1) * lanes]
    taps_n = w_in.shape[0]
    for di in range(taps_n):
        for dj in range(taps_n):
            w_ref[di * width : (di + 1) * width, dj * width : (dj + 1) * width] = w_in[di, dj]
    for h in range(halves):
        to_left[h].wait_recv()
        to_right[h].wait_recv()
    for h in range(halves):
        pl.when(has_up)(corner_up[h].start)
        pl.when(has_down)(corner_down[h].start)

    def encoded(row):
        stacked = jnp.concatenate(
            [xpad[row + k, h] for k in range(3) for h in range(halves)], axis=-1
        )
        taps = jnp.dot(stacked, w_ref[...], preferred_element_type=jnp.float32)
        conv = (
            pltpu.roll(taps[:, :width], 1, 0)
            + taps[:, width : 2 * width]
            + pltpu.roll(taps[:, 2 * width :], cols - 1, 0)
        )
        return jax.nn.gelu(conv)

    def pooled_row(p):
        pair = encoded(2 * p) + encoded(2 * p + 1)
        lanes = pair_ref.shape[2]
        chunks = []
        for c in range(width // lanes):
            pair_ref[c, pl.ds(0, cols)] = pair[:, c * lanes : (c + 1) * lanes]
            pair_ref[c, pl.ds(cols, 8)] = jnp.zeros((8, lanes), jnp.float32)
            half = pair_ref.shape[1] // 2
            chunks.append(
                pair_ref[c, pl.ds(0, half, stride=2)] + pair_ref[c, pl.ds(1, half, stride=2)]
            )
        summed = jnp.concatenate(chunks, axis=-1)
        pooled = (summed * 0.25).astype(jnp.bfloat16)
        projected = jnp.dot(pooled, proj_ref[...], preferred_element_type=jnp.float32)
        out_ref[p + 1] = projected[:pooled_cols].astype(out_ref.dtype)

    def one_row(p, carry):
        pooled_row(p)
        return carry

    lax.fori_loop(1, pooled_rows - 1, one_row, 0)
    for h in range(halves):
        pl.when(has_down)(to_up[h].wait_recv)
        pl.when(has_up)(to_down[h].wait_recv)
        pl.when(has_down)(corner_up[h].wait_recv)
        pl.when(has_up)(corner_down[h].wait_recv)
    pooled_row(0)
    edge_up = remote(12, out_ref.at[1], out_ref.at[pooled_rows + 1], (up, lon))
    pl.when(has_up)(edge_up.start)
    pooled_row(pooled_rows - 1)
    edge_down = remote(13, out_ref.at[pooled_rows], out_ref.at[0], (down, lon))
    pl.when(has_down)(edge_down.start)
    pl.when(has_down)(edge_up.wait_recv)
    pl.when(has_up)(edge_down.wait_recv)

    @pl.when(lat == 0)
    def _():
        out_ref[0] = jnp.zeros(out_ref.shape[1:], out_ref.dtype)

    @pl.when(lat == lats - 1)
    def _():
        out_ref[pooled_rows + 1] = jnp.zeros(out_ref.shape[1:], out_ref.dtype)

    for h in range(halves):
        pl.when(has_up)(to_up[h].wait_send)
        pl.when(has_down)(to_down[h].wait_send)
        to_left[h].wait_send()
        to_right[h].wait_send()
        pl.when(has_up)(corner_up[h].wait_send)
        pl.when(has_down)(corner_down[h].wait_send)
    pl.when(has_up)(edge_up.wait_send)
    pl.when(has_down)(edge_down.wait_send)


def encoder(tile, w_enc, w_proj):
    rows, tile_cols, width = tile.shape
    cols = tile_cols + 4
    vmem = pl.BlockSpec(memory_space=pltpu.VMEM)
    return pl.pallas_call(
        encoder_kernel,
        out_shape=jax.ShapeDtypeStruct((rows // 2 + 2, tile_cols // 2, w_proj.shape[1]), jnp.bfloat16),
        in_specs=[vmem, vmem, vmem],
        out_specs=vmem,
        scratch_shapes=[
            pltpu.VMEM((rows + 2, width // 128, cols, 128), jnp.bfloat16),
            pltpu.VMEM((width // 128, cols + 8, 128), jnp.float32),
            pltpu.VMEM((3 * width, 3 * width), jnp.bfloat16),
            pltpu.SemaphoreType.DMA((width // 128,)),
            pltpu.SemaphoreType.DMA((14,)),
            pltpu.SemaphoreType.DMA((14,)),
        ],
        compiler_params=pltpu.CompilerParams(
            collective_id=1, has_side_effects=True, vmem_limit_bytes=48 * 1024 * 1024
        ),
    )(tile, w_enc, w_proj)


def head_kernel(ids_ref, tile_ref, scale_ref, shift_ref, w_in, mix_ref, out_ref, band_ref, mod_ref,
                hidden_ref, w_ref, send_sem, recv_sem, local_sem):
    me = lax.axis_index("lon")
    n = lax.axis_size("lon")
    lat = lax.axis_index("lat")
    last_lat = lax.axis_size("lat") - 1
    halo_rows, tile_cols, width = tile_ref.shape
    cols = band_ref.shape[1]
    leads = out_ref.shape[0]
    step = HEAD_ROWS
    pieces = halo_rows // step

    chips = n // 2
    chip = me // 2
    core = me % 2
    sense = 1 - 2 * core
    kinds = 7

    def device(at_chip, at_core):
        return 2 * lax.rem(at_chip + 2 * chips, chips) + at_core

    sibling = device(chip, 1 - core)
    east = device(chip + 1, core)
    west = device(chip - 1, core)
    far = device(chip + 2, core)
    behind = device(chip - sense, core)
    ahead = device(chip + sense, core)

    barrier = pltpu.get_barrier_semaphore()
    for peer in (sibling, east, west):
        pl.semaphore_signal(barrier, inc=1, device_id=(lat, peer), device_id_type=MESH)
    pl.semaphore_wait(barrier, 3)

    def slot(piece, source):
        start = pl.multiple_of(piece * step, step)
        return band_ref.at[pl.ds(start, step), pl.ds(source * tile_cols, tile_cols)]

    def source_rows(piece):
        return tile_ref.at[pl.ds(pl.multiple_of(piece * step, step), step)]

    def local_copy(piece):
        return pltpu.make_async_copy(source_rows(piece), slot(piece, me), local_sem.at[piece])

    def transfer(piece, kind, origin, target, own=False):
        return pltpu.make_async_remote_copy(
            src_ref=source_rows(piece) if own else slot(piece, origin),
            dst_ref=slot(piece, origin),
            send_sem=send_sem.at[piece * kinds + kind],
            recv_sem=recv_sem.at[piece * kinds + kind],
            device_id=(lat, target),
            device_id_type=MESH,
        )

    def sends(piece):
        return [
            transfer(piece, 0, me, sibling, own=True),
            transfer(piece, 1, me, east, own=True),
            transfer(piece, 2, me, west, own=True),
            transfer(piece, 3, behind, ahead),
            transfer(piece, 4, west, sibling),
            transfer(piece, 5, east, sibling),
            transfer(piece, 6, far, sibling),
        ]

    def receive(piece, kind, origin):
        transfer(piece, kind, origin, me).wait_recv()

    def direct(piece):
        local_copy(piece).start()
        for copy in sends(piece)[:3]:
            copy.start()

    def forward_x(piece):
        receive(piece, 1 + core, behind)
        sends(piece)[3].start()

    def forward_sibling(piece):
        receive(piece, 2 - core, ahead)
        receive(piece, 3, far)
        for copy in sends(piece)[4:]:
            copy.start()

    def arrived(piece):
        local_copy(piece).wait()
        receive(piece, 0, sibling)
        receive(piece, 4, device(chip - 1, 1 - core))
        receive(piece, 5, device(chip + 1, 1 - core))
        receive(piece, 6, device(chip + 2, 1 - core))

    for piece in range(min(AHEAD + FORWARD, pieces)):
        direct(piece)
    taps_n = w_in.shape[0]
    for di in range(taps_n):
        for dj in range(taps_n):
            w_ref[di * width : (di + 1) * width, dj * width : (dj + 1) * width] = w_in[di, dj]
    gains, shifts = [], []
    for l in range(leads):
        row = ids_ref[leads * me + l]
        gains.append(1.0 + scale_ref[pl.ds(row, 1), :])
        shifts.append(shift_ref[pl.ds(row, 1), :])
    for piece in range(min(FORWARD, pieces)):
        forward_x(piece)
    for piece in range(min(2, pieces)):
        forward_sibling(piece)
    arrived(0)

    def modulate(piece):
        for j in range(step):
            row = piece * step + j
            keep = ((row > 0) | (lat > 0)) & ((row < halo_rows - 1) | (lat < last_lat))
            source = band_ref[row].astype(jnp.float32)
            for l in range(leads):
                value = jnp.where(keep, source * gains[l] + shifts[l], 0.0)
                mod_ref[l, row] = value.astype(jnp.bfloat16)

    modulate(0)

    def one_chunk(k, carry):
        @pl.when(k + AHEAD + FORWARD < pieces)
        def _():
            direct(k + AHEAD + FORWARD)

        @pl.when(k + FORWARD < pieces)
        def _():
            forward_x(k + FORWARD)

        @pl.when(k + 2 < pieces)
        def _():
            forward_sibling(k + 2)

        arrived(k + 1)
        modulate(k + 1)
        base = k * step
        for l in range(leads):
            for j in range(step):
                stacked = jnp.concatenate([mod_ref[l, base + j + t] for t in range(3)], axis=-1)
                taps = jnp.dot(stacked, w_ref[...], preferred_element_type=jnp.float32)
                conv = (
                    pltpu.roll(taps[:, :width], 1, 0)
                    + taps[:, width : 2 * width]
                    + pltpu.roll(taps[:, 2 * width :], cols - 1, 0)
                )
                at = (l * step + j) * width
                hidden_ref[:, at : at + width] = jax.nn.gelu(conv).astype(jnp.bfloat16)
        mixed = jnp.dot(mix_ref[...], hidden_ref[...], preferred_element_type=jnp.float32)
        for l in range(leads):
            for j in range(step):
                at = (l * step + j) * width
                own = mod_ref[l, base + j + 1].astype(jnp.float32)
                out_ref[l, base + j] = (own + mixed[:, at : at + width]).astype(out_ref.dtype)
        return carry

    lax.fori_loop(0, pieces - 1, one_chunk, 0)

    for piece in range(pieces):
        for copy in sends(piece):
            copy.wait_send()


def head(lead_ids, tile, film_scale, film_shift, w_head, zonal_mix, lon_devices):
    halo_rows, tile_cols, width = tile.shape
    rows = halo_rows - 2
    cols = tile_cols * lon_devices
    leads = LEAD_DEV
    pieces = halo_rows // HEAD_ROWS
    vmem = pl.BlockSpec(memory_space=pltpu.VMEM)
    return pl.pallas_call(
        head_kernel,
        out_shape=jax.ShapeDtypeStruct((leads, rows, cols, width), jnp.bfloat16),
        in_specs=[pl.BlockSpec(memory_space=pltpu.SMEM), pl.BlockSpec(memory_space=pl.ANY), vmem, vmem, vmem, vmem],
        out_specs=vmem,
        scratch_shapes=[
            pltpu.VMEM((halo_rows, cols, width), jnp.bfloat16),
            pltpu.VMEM((leads, halo_rows, cols, width), jnp.bfloat16),
            pltpu.VMEM((cols, leads * HEAD_ROWS * width), jnp.bfloat16),
            pltpu.VMEM((3 * width, 3 * width), jnp.bfloat16),
            pltpu.SemaphoreType.DMA((pieces * 7,)),
            pltpu.SemaphoreType.DMA((pieces * 7,)),
            pltpu.SemaphoreType.DMA((pieces,)),
        ],
        compiler_params=pltpu.CompilerParams(
            collective_id=0, has_side_effects=True, vmem_limit_bytes=VMEM_ALL
        ),
    )(lead_ids, tile, film_scale, film_shift, w_head, zonal_mix)


def shards(inputs, w_enc, w_proj, film_scale, film_shift, lead_ids, w_head, zonal_mix):
    lat_rows, lon_cols, channels = inputs.shape
    tile = encoder(inputs, w_enc, w_proj)
    return head(lead_ids, tile, film_scale, film_shift, w_head, zonal_mix, lax.axis_size("lon"))

def solution(mesh):
    in_specs = (P("lat", "lon", None), P(), P(), P(), P(), P(), P(), P())
    out_specs = P("lon", "lat", None, None)
    return jax.shard_map(shards, mesh=mesh, in_specs=in_specs, out_specs=out_specs, check_vma=False)
```

```python
import functools

import jax
import jax.numpy as jnp
from jax import lax
from jax.experimental import pallas as pl
from jax.experimental.pallas import tpu as pltpu
from jax.sharding import PartitionSpec as P

LEAD_DEV = 2
HEAD_ROWS = 2
AHEAD = 2
FORWARD = 4
VMEM_ALL = 67043328
MESH = pl.DeviceIdType.MESH


def extended(x, sides, width, wrap):
    for axis, dim in sides:
        devices, length = (lax.axis_size(axis), x.shape[dim])
        up = [(i, (i + 1) % devices) for i in range(devices if wrap else devices - 1)]
        down = [(j, i) for i, j in up]
        last = lax.slice_in_dim(x, length - width, length, axis=dim)
        initial = lax.slice_in_dim(x, 0, width, axis=dim)
        before = lax.ppermute(last, axis, up)
        after = lax.ppermute(initial, axis, down)
        x = jnp.concatenate([before, x, after], axis=dim)
    return x


def conv_three(padded, weight):
    batched = padded if padded.ndim == 4 else padded[None]
    result = lax.conv_general_dilated(
        batched,
        weight,
        (1, 1),
        "VALID",
        dimension_numbers=("NHWC", "HWIO", "NHWC"),
        preferred_element_type=jnp.float32,
    )
    return result if padded.ndim == 4 else result[0]


def pool_pairs(field):
    summed = lax.reduce_window(
        field, jnp.array(0, field.dtype), lax.add, (2, 2, 1), (2, 2, 1), "VALID"
    )
    return summed * 0.25


def encoder_kernel(x_hbm, w_in, proj_ref, out_ref, xpad, pair_ref, w_ref, local_sem, send_sem, recv_sem):
    lat = lax.axis_index("lat")
    lon = lax.axis_index("lon")
    lats = lax.axis_size("lat")
    lons = lax.axis_size("lon")
    has_up = lat > 0
    has_down = lat < lats - 1
    up, down = lat - 1, lat + 1
    left, right = lax.rem(lon + lons - 1, lons), lax.rem(lon + 1, lons)
    rows, tile_cols, width = x_hbm.shape
    cols = xpad.shape[2]
    pooled_rows, pooled_cols = rows // 2, tile_cols // 2

    barrier = pltpu.get_barrier_semaphore()

    @pl.when(has_up)
    def _():
        pl.semaphore_signal(barrier, inc=1, device_id=(up, lon), device_id_type=MESH)

    @pl.when(has_down)
    def _():
        pl.semaphore_signal(barrier, inc=1, device_id=(down, lon), device_id_type=MESH)

    for peer in (left, right):
        pl.semaphore_signal(barrier, inc=1, device_id=(lat, peer), device_id_type=MESH)
    pl.semaphore_wait(barrier, 2 + has_up.astype(jnp.int32) + has_down.astype(jnp.int32))

    def remote(kind, src, dst, target):
        return pltpu.make_async_remote_copy(
            src_ref=src, dst_ref=dst, send_sem=send_sem.at[kind], recv_sem=recv_sem.at[kind],
            device_id=target, device_id_type=MESH,
        )

    halves = xpad.shape[1]
    lanes = xpad.shape[3]
    inner = pl.ds(0, tile_cols)
    right_halo = pl.ds(tile_cols, 2)
    left_halo = pl.ds(cols - 2, 2)
    halo = pl.ds(tile_cols, cols - tile_cols)

    @pl.when(lat == 0)
    def _():
        xpad[0] = jnp.zeros(xpad.shape[1:], xpad.dtype)

    @pl.when(lat == lats - 1)
    def _():
        xpad[rows + 1] = jnp.zeros(xpad.shape[1:], xpad.dtype)

    to_up, to_down, to_left, to_right, corner_up, corner_down = [], [], [], [], [], []
    body = pl.ds(1, rows)
    for h in range(halves):
        part = pl.ds(h * lanes, lanes)
        to_up.append(remote(h, x_hbm.at[0, :, part], xpad.at[rows + 1, h, inner], (up, lon)))
        to_down.append(remote(2 + h, x_hbm.at[rows - 1, :, part], xpad.at[0, h, inner], (down, lon)))
        to_left.append(
            remote(4 + h, x_hbm.at[:, pl.ds(0, 2), part], xpad.at[body, h, right_halo], (lat, left))
        )
        to_right.append(
            remote(6 + h, x_hbm.at[:, pl.ds(tile_cols - 2, 2), part], xpad.at[body, h, left_halo], (lat, right))
        )
        corner_up.append(remote(8 + h, xpad.at[1, h, halo], xpad.at[rows + 1, h, halo], (up, lon)))
        corner_down.append(remote(10 + h, xpad.at[rows, h, halo], xpad.at[0, h, halo], (down, lon)))
    for h in range(halves):
        to_left[h].start()
        to_right[h].start()
        pl.when(has_up)(to_up[h].start)
        pl.when(has_down)(to_down[h].start)
    for h in range(halves):
        xpad[body, h, inner] = x_hbm[:, :, h * lanes : (h + 1) * lanes]
    taps_n = w_in.shape[0]
    for di in range(taps_n):
        for dj in range(taps_n):
            w_ref[di * width : (di + 1) * width, dj * width : (dj + 1) * width] = w_in[di, dj]
    for h in range(halves):
        to_left[h].wait_recv()
        to_right[h].wait_recv()
    for h in range(halves):
        pl.when(has_up)(corner_up[h].start)
        pl.when(has_down)(corner_down[h].start)

    def encoded(row):
        stacked = jnp.concatenate(
            [xpad[row + k, h] for k in range(3) for h in range(halves)], axis=-1
        )
        taps = jnp.dot(stacked, w_ref[...], preferred_element_type=jnp.float32)
        conv = (
            pltpu.roll(taps[:, :width], 1, 0)
            + taps[:, width : 2 * width]
            + pltpu.roll(taps[:, 2 * width :], cols - 1, 0)
        )
        return jax.nn.gelu(conv)

    def pooled_row(p):
        pair = encoded(2 * p) + encoded(2 * p + 1)
        lanes = pair_ref.shape[2]
        chunks = []
        for c in range(width // lanes):
            pair_ref[c, pl.ds(0, cols)] = pair[:, c * lanes : (c + 1) * lanes]
            pair_ref[c, pl.ds(cols, 8)] = jnp.zeros((8, lanes), jnp.float32)
            half = pair_ref.shape[1] // 2
            chunks.append(
                pair_ref[c, pl.ds(0, half, stride=2)] + pair_ref[c, pl.ds(1, half, stride=2)]
            )
        summed = jnp.concatenate(chunks, axis=-1)
        pooled = (summed * 0.25).astype(jnp.bfloat16)
        projected = jnp.dot(pooled, proj_ref[...], preferred_element_type=jnp.float32)
        out_ref[p + 1] = projected[:pooled_cols].astype(out_ref.dtype)

    def one_row(p, carry):
        pooled_row(p)
        return carry

    middle = pooled_rows // 4
    lax.fori_loop(1, middle, one_row, 0)
    for h in range(halves):
        pl.when(has_down)(to_up[h].wait_recv)
        pl.when(has_up)(to_down[h].wait_recv)
        pl.when(has_down)(corner_up[h].wait_recv)
        pl.when(has_up)(corner_down[h].wait_recv)
    pooled_row(0)
    edge_up = remote(12, out_ref.at[1], out_ref.at[pooled_rows + 1], (up, lon))
    pl.when(has_up)(edge_up.start)
    pooled_row(pooled_rows - 1)
    edge_down = remote(13, out_ref.at[pooled_rows], out_ref.at[0], (down, lon))
    pl.when(has_down)(edge_down.start)
    lax.fori_loop(middle, pooled_rows - 1, one_row, 0)
    pl.when(has_down)(edge_up.wait_recv)
    pl.when(has_up)(edge_down.wait_recv)

    @pl.when(lat == 0)
    def _():
        out_ref[0] = jnp.zeros(out_ref.shape[1:], out_ref.dtype)

    @pl.when(lat == lats - 1)
    def _():
        out_ref[pooled_rows + 1] = jnp.zeros(out_ref.shape[1:], out_ref.dtype)

    for h in range(halves):
        pl.when(has_up)(to_up[h].wait_send)
        pl.when(has_down)(to_down[h].wait_send)
        to_left[h].wait_send()
        to_right[h].wait_send()
        pl.when(has_up)(corner_up[h].wait_send)
        pl.when(has_down)(corner_down[h].wait_send)
    pl.when(has_up)(edge_up.wait_send)
    pl.when(has_down)(edge_down.wait_send)


def encoder(tile, w_enc, w_proj):
    rows, tile_cols, width = tile.shape
    cols = tile_cols + 4
    vmem = pl.BlockSpec(memory_space=pltpu.VMEM)
    return pl.pallas_call(
        encoder_kernel,
        out_shape=jax.ShapeDtypeStruct((rows // 2 + 2, tile_cols // 2, w_proj.shape[1]), jnp.bfloat16),
        in_specs=[vmem, vmem, vmem],
        out_specs=vmem,
        scratch_shapes=[
            pltpu.VMEM((rows + 2, width // 128, cols, 128), jnp.bfloat16),
            pltpu.VMEM((width // 128, cols + 8, 128), jnp.float32),
            pltpu.VMEM((3 * width, 3 * width), jnp.bfloat16),
            pltpu.SemaphoreType.DMA((width // 128,)),
            pltpu.SemaphoreType.DMA((14,)),
            pltpu.SemaphoreType.DMA((14,)),
        ],
        compiler_params=pltpu.CompilerParams(
            collective_id=1, has_side_effects=True, vmem_limit_bytes=48 * 1024 * 1024
        ),
    )(tile, w_enc, w_proj)


def head_kernel(ids_ref, tile_ref, scale_ref, shift_ref, w_in, mix_ref, out_ref, band_ref, mod_ref,
                hidden_ref, w_ref, send_sem, recv_sem, local_sem, out_buf, out_sem):
    me = lax.axis_index("lon")
    n = lax.axis_size("lon")
    lat = lax.axis_index("lat")
    last_lat = lax.axis_size("lat") - 1
    halo_rows, tile_cols, width = tile_ref.shape
    cols = band_ref.shape[1]
    leads = out_ref.shape[0]
    step = HEAD_ROWS
    pieces = halo_rows // step

    chips = n // 2
    chip = me // 2
    core = me % 2
    sense = 1 - 2 * core
    kinds = 7

    def device(at_chip, at_core):
        return 2 * lax.rem(at_chip + 2 * chips, chips) + at_core

    sibling = device(chip, 1 - core)
    east = device(chip + 1, core)
    west = device(chip - 1, core)
    far = device(chip + 2, core)
    behind = device(chip - sense, core)
    ahead = device(chip + sense, core)

    barrier = pltpu.get_barrier_semaphore()
    for peer in (sibling, east, west):
        pl.semaphore_signal(barrier, inc=1, device_id=(lat, peer), device_id_type=MESH)
    pl.semaphore_wait(barrier, 3)

    def slot(piece, source):
        start = pl.multiple_of(piece * step, step)
        return band_ref.at[pl.ds(start, step), pl.ds(source * tile_cols, tile_cols)]

    def source_rows(piece):
        return tile_ref.at[pl.ds(pl.multiple_of(piece * step, step), step)]

    def local_copy(piece):
        return pltpu.make_async_copy(source_rows(piece), slot(piece, me), local_sem.at[piece])

    def transfer(piece, kind, origin, target, own=False):
        return pltpu.make_async_remote_copy(
            src_ref=source_rows(piece) if own else slot(piece, origin),
            dst_ref=slot(piece, origin),
            send_sem=send_sem.at[piece * kinds + kind],
            recv_sem=recv_sem.at[piece * kinds + kind],
            device_id=(lat, target),
            device_id_type=MESH,
        )

    def sends(piece):
        return [
            transfer(piece, 0, me, sibling, own=True),
            transfer(piece, 1, me, east, own=True),
            transfer(piece, 2, me, west, own=True),
            transfer(piece, 3, behind, ahead),
            transfer(piece, 4, west, sibling),
            transfer(piece, 5, east, sibling),
            transfer(piece, 6, far, sibling),
        ]

    def receive(piece, kind, origin):
        transfer(piece, kind, origin, me).wait_recv()

    def direct(piece):
        local_copy(piece).start()
        for copy in sends(piece)[:3]:
            copy.start()

    def forward_x(piece):
        receive(piece, 1 + core, behind)
        sends(piece)[3].start()

    def forward_sibling(piece):
        receive(piece, 2 - core, ahead)
        receive(piece, 3, far)
        for copy in sends(piece)[4:]:
            copy.start()

    def arrived(piece):
        local_copy(piece).wait()
        receive(piece, 0, sibling)
        receive(piece, 4, device(chip - 1, 1 - core))
        receive(piece, 5, device(chip + 1, 1 - core))
        receive(piece, 6, device(chip + 2, 1 - core))

    for piece in range(min(AHEAD + FORWARD, pieces)):
        direct(piece)
    taps_n = w_in.shape[0]
    for di in range(taps_n):
        for dj in range(taps_n):
            w_ref[di * width : (di + 1) * width, dj * width : (dj + 1) * width] = w_in[di, dj]
    gains, shifts = [], []
    for l in range(leads):
        row = ids_ref[leads * me + l]
        gains.append(1.0 + scale_ref[pl.ds(row, 1), :])
        shifts.append(shift_ref[pl.ds(row, 1), :])
    for piece in range(min(FORWARD, pieces)):
        forward_x(piece)
    for piece in range(min(2, pieces)):
        forward_sibling(piece)
    arrived(0)

    def modulate(piece):
        for j in range(step):
            row = piece * step + j
            keep = ((row > 0) | (lat > 0)) & ((row < halo_rows - 1) | (lat < last_lat))
            source = band_ref[row].astype(jnp.float32)
            for l in range(leads):
                value = jnp.where(keep, source * gains[l] + shifts[l], 0.0)
                mod_ref[l, row] = value.astype(jnp.bfloat16)

    modulate(0)

    def one_chunk(k, carry):
        @pl.when(k + AHEAD + FORWARD < pieces)
        def _():
            direct(k + AHEAD + FORWARD)

        @pl.when(k + 2 < pieces)
        def _():
            forward_sibling(k + 2)

        @pl.when(k + FORWARD < pieces)
        def _():
            forward_x(k + FORWARD)

        arrived(k + 1)
        modulate(k + 1)
        base = k * step
        for l in range(leads):
            for j in range(step):
                stacked = jnp.concatenate([mod_ref[l, base + j + t] for t in range(3)], axis=-1)
                taps = jnp.dot(stacked, w_ref[...], preferred_element_type=jnp.float32)
                conv = (
                    pltpu.roll(taps[:, :width], 1, 0)
                    + taps[:, width : 2 * width]
                    + pltpu.roll(taps[:, 2 * width :], cols - 1, 0)
                )
                at = (l * step + j) * width
                hidden_ref[:, at : at + width] = jax.nn.gelu(conv).astype(jnp.bfloat16)
        mixed = jnp.dot(mix_ref[...], hidden_ref[...], preferred_element_type=jnp.float32)
        for l in range(leads):
            for j in range(step):
                at = (l * step + j) * width
                own = mod_ref[l, base + j + 1].astype(jnp.float32)
                out_buf[l, base + j] = (own + mixed[:, at : at + width]).astype(out_buf.dtype)
        write_out(k).start()
        return carry

    def write_out(k):
        rows_at = pl.ds(pl.multiple_of(k * step, step), step)
        return pltpu.make_async_copy(out_buf.at[:, rows_at], out_ref.at[:, rows_at], out_sem.at[k])

    lax.fori_loop(0, pieces - 1, one_chunk, 0)
    for k in range(pieces - 1):
        write_out(k).wait()

    for piece in range(pieces):
        for copy in sends(piece):
            copy.wait_send()


def head(lead_ids, tile, film_scale, film_shift, w_head, zonal_mix, lon_devices):
    halo_rows, tile_cols, width = tile.shape
    rows = halo_rows - 2
    cols = tile_cols * lon_devices
    leads = LEAD_DEV
    pieces = halo_rows // HEAD_ROWS
    vmem = pl.BlockSpec(memory_space=pltpu.VMEM)
    return pl.pallas_call(
        head_kernel,
        out_shape=jax.ShapeDtypeStruct((leads, rows, cols, width), jnp.bfloat16),
        in_specs=[pl.BlockSpec(memory_space=pltpu.SMEM), pl.BlockSpec(memory_space=pl.ANY), vmem, vmem, vmem, vmem],
        out_specs=pl.BlockSpec(memory_space=pl.ANY),
        scratch_shapes=[
            pltpu.VMEM((halo_rows, cols, width), jnp.bfloat16),
            pltpu.VMEM((leads, halo_rows, cols, width), jnp.bfloat16),
            pltpu.VMEM((cols, leads * HEAD_ROWS * width), jnp.bfloat16),
            pltpu.VMEM((3 * width, 3 * width), jnp.bfloat16),
            pltpu.SemaphoreType.DMA((pieces * 7,)),
            pltpu.SemaphoreType.DMA((pieces * 7,)),
            pltpu.SemaphoreType.DMA((pieces,)),
            pltpu.VMEM((leads, rows, cols, width), jnp.bfloat16),
            pltpu.SemaphoreType.DMA((pieces - 1,)),
        ],
        compiler_params=pltpu.CompilerParams(
            collective_id=0, has_side_effects=True, vmem_limit_bytes=VMEM_ALL
        ),
    )(lead_ids, tile, film_scale, film_shift, w_head, zonal_mix)


def shards(inputs, w_enc, w_proj, film_scale, film_shift, lead_ids, w_head, zonal_mix):
    lat_rows, lon_cols, channels = inputs.shape
    tile = encoder(inputs, w_enc, w_proj)
    return head(lead_ids, tile, film_scale, film_shift, w_head, zonal_mix, lax.axis_size("lon"))

def solution(mesh):
    in_specs = (P("lat", "lon", None), P(), P(), P(), P(), P(), P(), P())
    out_specs = P("lon", "lat", None, None)
    return jax.shard_map(shards, mesh=mesh, in_specs=in_specs, out_specs=out_specs, check_vma=False)
```

```python
import functools

import jax
import jax.numpy as jnp
from jax import lax
from jax.experimental import pallas as pl
from jax.experimental.pallas import tpu as pltpu
from jax.sharding import PartitionSpec as P

LEAD_DEV = 2
HEAD_ROWS = 2
AHEAD = 3
FORWARD = 4
VMEM_ALL = 67043328
MESH = pl.DeviceIdType.MESH


def extended(x, sides, width, wrap):
    for axis, dim in sides:
        devices, length = (lax.axis_size(axis), x.shape[dim])
        up = [(i, (i + 1) % devices) for i in range(devices if wrap else devices - 1)]
        down = [(j, i) for i, j in up]
        last = lax.slice_in_dim(x, length - width, length, axis=dim)
        initial = lax.slice_in_dim(x, 0, width, axis=dim)
        before = lax.ppermute(last, axis, up)
        after = lax.ppermute(initial, axis, down)
        x = jnp.concatenate([before, x, after], axis=dim)
    return x


def conv_three(padded, weight):
    batched = padded if padded.ndim == 4 else padded[None]
    result = lax.conv_general_dilated(
        batched,
        weight,
        (1, 1),
        "VALID",
        dimension_numbers=("NHWC", "HWIO", "NHWC"),
        preferred_element_type=jnp.float32,
    )
    return result if padded.ndim == 4 else result[0]


def pool_pairs(field):
    summed = lax.reduce_window(
        field, jnp.array(0, field.dtype), lax.add, (2, 2, 1), (2, 2, 1), "VALID"
    )
    return summed * 0.25


def encoder_kernel(x_hbm, w_in, proj_ref, out_ref, xpad, pair_ref, w_ref, local_sem, send_sem, recv_sem):
    lat = lax.axis_index("lat")
    lon = lax.axis_index("lon")
    lats = lax.axis_size("lat")
    lons = lax.axis_size("lon")
    has_up = lat > 0
    has_down = lat < lats - 1
    up, down = lat - 1, lat + 1
    left, right = lax.rem(lon + lons - 1, lons), lax.rem(lon + 1, lons)
    rows, tile_cols, width = x_hbm.shape
    cols = xpad.shape[2]
    pooled_rows, pooled_cols = rows // 2, tile_cols // 2

    barrier = pltpu.get_barrier_semaphore()

    @pl.when(has_up)
    def _():
        pl.semaphore_signal(barrier, inc=1, device_id=(up, lon), device_id_type=MESH)

    @pl.when(has_down)
    def _():
        pl.semaphore_signal(barrier, inc=1, device_id=(down, lon), device_id_type=MESH)

    for peer in (left, right):
        pl.semaphore_signal(barrier, inc=1, device_id=(lat, peer), device_id_type=MESH)
    pl.semaphore_wait(barrier, 2 + has_up.astype(jnp.int32) + has_down.astype(jnp.int32))

    def remote(kind, src, dst, target):
        return pltpu.make_async_remote_copy(
            src_ref=src, dst_ref=dst, send_sem=send_sem.at[kind], recv_sem=recv_sem.at[kind],
            device_id=target, device_id_type=MESH,
        )

    halves = xpad.shape[1]
    lanes = xpad.shape[3]
    inner = pl.ds(0, tile_cols)
    right_halo = pl.ds(tile_cols, 2)
    left_halo = pl.ds(cols - 2, 2)
    halo = pl.ds(tile_cols, cols - tile_cols)

    @pl.when(lat == 0)
    def _():
        xpad[0] = jnp.zeros(xpad.shape[1:], xpad.dtype)

    @pl.when(lat == lats - 1)
    def _():
        xpad[rows + 1] = jnp.zeros(xpad.shape[1:], xpad.dtype)

    to_up, to_down, to_left, to_right, corner_up, corner_down = [], [], [], [], [], []
    body = pl.ds(1, rows)
    for h in range(halves):
        part = pl.ds(h * lanes, lanes)
        to_up.append(remote(h, x_hbm.at[0, :, part], xpad.at[rows + 1, h, inner], (up, lon)))
        to_down.append(remote(2 + h, x_hbm.at[rows - 1, :, part], xpad.at[0, h, inner], (down, lon)))
        to_left.append(
            remote(4 + h, x_hbm.at[:, pl.ds(0, 2), part], xpad.at[body, h, right_halo], (lat, left))
        )
        to_right.append(
            remote(6 + h, x_hbm.at[:, pl.ds(tile_cols - 2, 2), part], xpad.at[body, h, left_halo], (lat, right))
        )
        corner_up.append(remote(8 + h, xpad.at[1, h, halo], xpad.at[rows + 1, h, halo], (up, lon)))
        corner_down.append(remote(10 + h, xpad.at[rows, h, halo], xpad.at[0, h, halo], (down, lon)))
    for h in range(halves):
        to_left[h].start()
        to_right[h].start()
        pl.when(has_up)(to_up[h].start)
        pl.when(has_down)(to_down[h].start)
    for h in range(halves):
        xpad[body, h, inner] = x_hbm[:, :, h * lanes : (h + 1) * lanes]
    taps_n = w_in.shape[0]
    for di in range(taps_n):
        for dj in range(taps_n):
            w_ref[di * width : (di + 1) * width, dj * width : (dj + 1) * width] = w_in[di, dj]
    for h in range(halves):
        to_left[h].wait_recv()
        to_right[h].wait_recv()
    for h in range(halves):
        pl.when(has_up)(corner_up[h].start)
        pl.when(has_down)(corner_down[h].start)

    def encoded(row):
        stacked = jnp.concatenate(
            [xpad[row + k, h] for k in range(3) for h in range(halves)], axis=-1
        )
        taps = jnp.dot(stacked, w_ref[...], preferred_element_type=jnp.float32)
        conv = (
            pltpu.roll(taps[:, :width], 1, 0)
            + taps[:, width : 2 * width]
            + pltpu.roll(taps[:, 2 * width :], cols - 1, 0)
        )
        return jax.nn.gelu(conv)

    def pooled_row(p):
        pair = encoded(2 * p) + encoded(2 * p + 1)
        lanes = pair_ref.shape[2]
        chunks = []
        for c in range(width // lanes):
            pair_ref[c, pl.ds(0, cols)] = pair[:, c * lanes : (c + 1) * lanes]
            pair_ref[c, pl.ds(cols, 8)] = jnp.zeros((8, lanes), jnp.float32)
            half = pair_ref.shape[1] // 2
            chunks.append(
                pair_ref[c, pl.ds(0, half, stride=2)] + pair_ref[c, pl.ds(1, half, stride=2)]
            )
        summed = jnp.concatenate(chunks, axis=-1)
        pooled = (summed * 0.25).astype(jnp.bfloat16)
        projected = jnp.dot(pooled, proj_ref[...], preferred_element_type=jnp.float32)
        out_ref[p + 1] = projected[:pooled_cols].astype(out_ref.dtype)

    def one_row(p, carry):
        pooled_row(p)
        return carry

    middle = pooled_rows // 4
    lax.fori_loop(1, middle, one_row, 0)
    for h in range(halves):
        pl.when(has_down)(to_up[h].wait_recv)
        pl.when(has_up)(to_down[h].wait_recv)
        pl.when(has_down)(corner_up[h].wait_recv)
        pl.when(has_up)(corner_down[h].wait_recv)
    pooled_row(0)
    edge_up = remote(12, out_ref.at[1], out_ref.at[pooled_rows + 1], (up, lon))
    pl.when(has_up)(edge_up.start)
    pooled_row(pooled_rows - 1)
    edge_down = remote(13, out_ref.at[pooled_rows], out_ref.at[0], (down, lon))
    pl.when(has_down)(edge_down.start)
    lax.fori_loop(middle, pooled_rows - 1, one_row, 0)
    pl.when(has_down)(edge_up.wait_recv)
    pl.when(has_up)(edge_down.wait_recv)

    @pl.when(lat == 0)
    def _():
        out_ref[0] = jnp.zeros(out_ref.shape[1:], out_ref.dtype)

    @pl.when(lat == lats - 1)
    def _():
        out_ref[pooled_rows + 1] = jnp.zeros(out_ref.shape[1:], out_ref.dtype)

    for h in range(halves):
        pl.when(has_up)(to_up[h].wait_send)
        pl.when(has_down)(to_down[h].wait_send)
        to_left[h].wait_send()
        to_right[h].wait_send()
        pl.when(has_up)(corner_up[h].wait_send)
        pl.when(has_down)(corner_down[h].wait_send)
    pl.when(has_up)(edge_up.wait_send)
    pl.when(has_down)(edge_down.wait_send)


def encoder(tile, w_enc, w_proj):
    rows, tile_cols, width = tile.shape
    cols = tile_cols + 4
    vmem = pl.BlockSpec(memory_space=pltpu.VMEM)
    return pl.pallas_call(
        encoder_kernel,
        out_shape=jax.ShapeDtypeStruct((rows // 2 + 2, tile_cols // 2, w_proj.shape[1]), jnp.bfloat16),
        in_specs=[vmem, vmem, vmem],
        out_specs=vmem,
        scratch_shapes=[
            pltpu.VMEM((rows + 2, width // 128, cols, 128), jnp.bfloat16),
            pltpu.VMEM((width // 128, cols + 8, 128), jnp.float32),
            pltpu.VMEM((3 * width, 3 * width), jnp.bfloat16),
            pltpu.SemaphoreType.DMA((width // 128,)),
            pltpu.SemaphoreType.DMA((14,)),
            pltpu.SemaphoreType.DMA((14,)),
        ],
        compiler_params=pltpu.CompilerParams(
            collective_id=1, has_side_effects=True, vmem_limit_bytes=48 * 1024 * 1024
        ),
    )(tile, w_enc, w_proj)


def head_kernel(ids_ref, tile_ref, scale_ref, shift_ref, w_in, mix_ref, out_ref, band_ref, mod_ref,
                hidden_ref, w_ref, send_sem, recv_sem, local_sem, out_buf, out_sem):
    me = lax.axis_index("lon")
    n = lax.axis_size("lon")
    lat = lax.axis_index("lat")
    last_lat = lax.axis_size("lat") - 1
    halo_rows, tile_cols, width = tile_ref.shape
    cols = band_ref.shape[1]
    leads = out_ref.shape[0]
    step = HEAD_ROWS
    pieces = halo_rows // step

    chips = n // 2
    chip = me // 2
    core = me % 2
    sense = 1 - 2 * core
    kinds = 7

    def device(at_chip, at_core):
        return 2 * lax.rem(at_chip + 2 * chips, chips) + at_core

    sibling = device(chip, 1 - core)
    east = device(chip + 1, core)
    west = device(chip - 1, core)
    far = device(chip + 2, core)
    behind = device(chip - sense, core)
    ahead = device(chip + sense, core)

    barrier = pltpu.get_barrier_semaphore()
    for peer in (sibling, east, west):
        pl.semaphore_signal(barrier, inc=1, device_id=(lat, peer), device_id_type=MESH)
    pl.semaphore_wait(barrier, 3)

    def slot(piece, source):
        start = pl.multiple_of(piece * step, step)
        return band_ref.at[pl.ds(start, step), pl.ds(source * tile_cols, tile_cols)]

    def source_rows(piece):
        return tile_ref.at[pl.ds(pl.multiple_of(piece * step, step), step)]

    def local_copy(piece):
        return pltpu.make_async_copy(source_rows(piece), slot(piece, me), local_sem.at[piece])

    def transfer(piece, kind, origin, target, own=False):
        return pltpu.make_async_remote_copy(
            src_ref=source_rows(piece) if own else slot(piece, origin),
            dst_ref=slot(piece, origin),
            send_sem=send_sem.at[piece * kinds + kind],
            recv_sem=recv_sem.at[piece * kinds + kind],
            device_id=(lat, target),
            device_id_type=MESH,
        )

    def sends(piece):
        return [
            transfer(piece, 0, me, sibling, own=True),
            transfer(piece, 1, me, east, own=True),
            transfer(piece, 2, me, west, own=True),
            transfer(piece, 3, behind, ahead),
            transfer(piece, 4, west, sibling),
            transfer(piece, 5, east, sibling),
            transfer(piece, 6, far, sibling),
        ]

    def receive(piece, kind, origin):
        transfer(piece, kind, origin, me).wait_recv()

    def direct(piece):
        local_copy(piece).start()
        for copy in sends(piece)[:3]:
            copy.start()

    def forward_x(piece):
        receive(piece, 1 + core, behind)
        sends(piece)[3].start()

    def forward_sibling(piece):
        receive(piece, 2 - core, ahead)
        receive(piece, 3, far)
        for copy in sends(piece)[4:]:
            copy.start()

    def arrived(piece):
        local_copy(piece).wait()
        receive(piece, 0, sibling)
        receive(piece, 4, device(chip - 1, 1 - core))
        receive(piece, 5, device(chip + 1, 1 - core))
        receive(piece, 6, device(chip + 2, 1 - core))

    for piece in range(min(AHEAD + FORWARD, pieces)):
        direct(piece)
    taps_n = w_in.shape[0]
    for di in range(taps_n):
        for dj in range(taps_n):
            w_ref[di * width : (di + 1) * width, dj * width : (dj + 1) * width] = w_in[di, dj]
    gains, shifts = [], []
    for l in range(leads):
        row = ids_ref[leads * me + l]
        gains.append(1.0 + scale_ref[pl.ds(row, 1), :])
        shifts.append(shift_ref[pl.ds(row, 1), :])
    for piece in range(min(FORWARD, pieces)):
        forward_x(piece)
    for piece in range(min(2, pieces)):
        forward_sibling(piece)
    arrived(0)

    def modulate(piece):
        for j in range(step):
            row = piece * step + j
            keep = ((row > 0) | (lat > 0)) & ((row < halo_rows - 1) | (lat < last_lat))
            source = band_ref[row].astype(jnp.float32)
            for l in range(leads):
                value = jnp.where(keep, source * gains[l] + shifts[l], 0.0)
                mod_ref[l, row] = value.astype(jnp.bfloat16)

    modulate(0)

    def one_chunk(k, carry):
        @pl.when(k + AHEAD + FORWARD < pieces)
        def _():
            direct(k + AHEAD + FORWARD)

        @pl.when(k + FORWARD < pieces)
        def _():
            forward_x(k + FORWARD)

        @pl.when(k + 2 < pieces)
        def _():
            forward_sibling(k + 2)

        arrived(k + 1)
        modulate(k + 1)
        base = k * step
        for l in range(leads):
            for j in range(step):
                stacked = jnp.concatenate([mod_ref[l, base + j + t] for t in range(3)], axis=-1)
                taps = jnp.dot(stacked, w_ref[...], preferred_element_type=jnp.float32)
                conv = (
                    pltpu.roll(taps[:, :width], 1, 0)
                    + taps[:, width : 2 * width]
                    + pltpu.roll(taps[:, 2 * width :], cols - 1, 0)
                )
                at = (l * step + j) * width
                hidden_ref[:, at : at + width] = jax.nn.gelu(conv).astype(jnp.bfloat16)
        mixed = jnp.dot(mix_ref[...], hidden_ref[...], preferred_element_type=jnp.float32)
        for l in range(leads):
            for j in range(step):
                at = (l * step + j) * width
                own = mod_ref[l, base + j + 1].astype(jnp.float32)
                out_buf[l, base + j] = (own + mixed[:, at : at + width]).astype(out_buf.dtype)
        write_out(k).start()
        return carry

    def write_out(k):
        rows_at = pl.ds(pl.multiple_of(k * step, step), step)
        return pltpu.make_async_copy(out_buf.at[:, rows_at], out_ref.at[:, rows_at], out_sem.at[k])

    lax.fori_loop(0, pieces - 1, one_chunk, 0)
    for k in range(pieces - 1):
        write_out(k).wait()

    for piece in range(pieces):
        for copy in sends(piece):
            copy.wait_send()


def head(lead_ids, tile, film_scale, film_shift, w_head, zonal_mix, lon_devices):
    halo_rows, tile_cols, width = tile.shape
    rows = halo_rows - 2
    cols = tile_cols * lon_devices
    leads = LEAD_DEV
    pieces = halo_rows // HEAD_ROWS
    vmem = pl.BlockSpec(memory_space=pltpu.VMEM)
    return pl.pallas_call(
        head_kernel,
        out_shape=jax.ShapeDtypeStruct((leads, rows, cols, width), jnp.bfloat16),
        in_specs=[pl.BlockSpec(memory_space=pltpu.SMEM), pl.BlockSpec(memory_space=pl.ANY), vmem, vmem, vmem, vmem],
        out_specs=pl.BlockSpec(memory_space=pl.ANY),
        scratch_shapes=[
            pltpu.VMEM((halo_rows, cols, width), jnp.bfloat16),
            pltpu.VMEM((leads, halo_rows, cols, width), jnp.bfloat16),
            pltpu.VMEM((cols, leads * HEAD_ROWS * width), jnp.bfloat16),
            pltpu.VMEM((3 * width, 3 * width), jnp.bfloat16),
            pltpu.SemaphoreType.DMA((pieces * 7,)),
            pltpu.SemaphoreType.DMA((pieces * 7,)),
            pltpu.SemaphoreType.DMA((pieces,)),
            pltpu.VMEM((leads, rows, cols, width), jnp.bfloat16),
            pltpu.SemaphoreType.DMA((pieces - 1,)),
        ],
        compiler_params=pltpu.CompilerParams(
            collective_id=0, has_side_effects=True, vmem_limit_bytes=VMEM_ALL
        ),
    )(lead_ids, tile, film_scale, film_shift, w_head, zonal_mix)


def shards(inputs, w_enc, w_proj, film_scale, film_shift, lead_ids, w_head, zonal_mix):
    lat_rows, lon_cols, channels = inputs.shape
    tile = encoder(inputs, w_enc, w_proj)
    return head(lead_ids, tile, film_scale, film_shift, w_head, zonal_mix, lax.axis_size("lon"))

def solution(mesh):
    in_specs = (P("lat", "lon", None), P(), P(), P(), P(), P(), P(), P())
    out_specs = P("lon", "lat", None, None)
    return jax.shard_map(shards, mesh=mesh, in_specs=in_specs, out_specs=out_specs, check_vma=False)
```
